128 devices in a mesh: rows: 16 (over z, x_hi, core), cols: 8 (over y, x_lo).
Axes of the slice: x: 4 (x_hi: 2, x_lo: 2; x = x_hi * 2 + x_lo), y: 4, z: 4, core: 2. Of those that a mesh axis runs over, the one named last changes fastest.
Arguments:
- wave_coarse: float32 [192, 192, 192], P('rows', 'cols'), may hold values from -6 to 6
- potential_coarse: float32 [192, 192, 192], P('rows', 'cols'), may hold values from 0 to 5
- potential_fine: float32 [384, 384, 384], P('cols', 'rows'), may hold values from 0 to 5
Outputs:
- fine_wave: float32 [384, 384, 384], P('cols', 'rows')
The draws below stay inside these ranges and needn't reach their ends.
All inputs are finite; a program needn't handle non-finite values.
Results may differ from the reference program's by a relative error of at most 0.0003.
Values sent between devices are 32-bit elements; how exact they have to be, the bound alone decides.
No kernel may reach another device: no remote copies, remote signals or barrier semaphores. Data moves between devices by JAX's collectives and lax.ppermute only.
A program may use at most 128 MiB of HBM per device.

```python
import math
import jax
import jax.numpy as jnp
from jax import lax

NC = 192
NF = 384
COARSE_STEPS = 1
FINE_STEPS = 1


def incline_potential(key, length, steepness, rough_low, rough_high):
    positions = jnp.arange(length, dtype=jnp.float32) / length
    incline = steepness * (positions[:, None, None] + positions[None, :, None] + positions[None, None, :])
    roughness = jax.random.uniform(key, (length, length, length), jnp.float32, rough_low, rough_high)
    return incline + roughness


def draw_potential_coarse(key, part):
    return incline_potential(jax.random.fold_in(key, 11), NC, 1.1, 0.0, 1.5)


def draw_potential_fine(key, part):
    return incline_potential(jax.random.fold_in(key, 23), NF, 1.1, 0.0, 1.5)


def steps_of(rng, extent, shards, least, top_value):
    loudness = 1.0
    for position, blocks in shards:
        draws = jax.random.uniform(jax.random.fold_in(jax.random.fold_in(rng, 6), position), (blocks,), jnp.float32, least / len(shards), top_value / len(shards))
        loudness = loudness * jnp.repeat(jnp.exp(draws), extent[position] // blocks).reshape((-1,) + (1,) * (len(extent) - 1 - position))
    return loudness


def scatter_about(key, dims, scale, reach, shards=(), kind=jnp.bfloat16):
    gain = steps_of(key, dims, shards, -0.22, 0.18) if shards else 1.0
    drawn = jax.random.normal(key, dims, jnp.float32) * scale * gain
    return jnp.minimum(jnp.maximum(drawn, -reach), reach).astype(kind)


def setup_inputs(seed: int = 0) -> dict:
    seeds = jax.random.split(jax.random.key(seed), 4)
    return {
        "wave_coarse": scatter_about(seeds[0], (NC, NC, NC), 1.0, 6.0, ((0, 16), (1, 8)), jnp.float32),
        "potential_coarse": draw_potential_coarse(jax.random.fold_in(seeds[3], 71), 0),
        "potential_fine": draw_potential_fine(jax.random.fold_in(seeds[3], 71), 0),
    }


TIME_STEP = 0.5
CONTACT = 0.4
DIPOLE_STRENGTH = 0.3
EPSILON = 1e-06

def hartley(values, dimension):
    spectrum = jnp.fft.fft(values, axis=dimension)
    return (spectrum.real - spectrum.imag).astype(values.dtype)

def hartley_cube(values):
    for dimension in range(3):
        values = hartley(values, dimension)
    return values

def wavenumbers(length, spacing):
    positions = jnp.arange(length, dtype=jnp.int32)
    signed = jnp.where(positions < length // 2, positions, positions - length)
    return 2.0 * math.pi / (length * spacing) * signed.astype(jnp.float32)

def multipliers(along_x, along_y, along_z, length):
    squares = along_x + along_y + along_z
    volume = float(length) ** 3
    kinetic = jnp.exp(-0.5 * TIME_STEP * squares) / volume
    nonzero = jnp.where(squares > 0, squares, 1.0)
    dipolar = jnp.where(squares > 0, DIPOLE_STRENGTH * (3.0 * along_z - squares) / nonzero, 0.0) / volume
    return (kinetic, dipolar)

def advance(amplitude, potential, kinetic, dipolar, length):
    evolved = hartley_cube(kinetic * hartley_cube(amplitude))
    density = evolved * evolved
    field_dd = hartley_cube(dipolar * hartley_cube(density))
    damped = jnp.exp(-TIME_STEP * (potential + CONTACT * density + field_dd)) * evolved
    squares = jnp.sum(damped * damped)
    return damped * lax.rsqrt(squares / float(length) ** 3 + EPSILON)

def refine(values, dimension):
    spectrum = hartley(values, dimension)
    lower_half, upper_half = jnp.split(spectrum, 2, axis=dimension)
    empty_band = jnp.zeros_like(lower_half)
    padded = jnp.concatenate([lower_half, empty_band, empty_band, upper_half], axis=dimension)
    return hartley(padded, dimension) / NC

def grid_kernels(length, spacing):
    waves = wavenumbers(length, spacing)
    squared = waves * waves
    return multipliers(squared[:, None, None], squared[None, :, None], squared[None, None, :], length)

def reference(wave_coarse, potential_coarse, potential_fine):
    kinetic, dipolar = grid_kernels(NC, 2.0)
    amplitude = wave_coarse
    for repeat in range(COARSE_STEPS):
        amplitude = advance(amplitude, potential_coarse, kinetic, dipolar, NC)
    for dimension in range(3):
        amplitude = refine(amplitude, dimension)
    potential = jnp.transpose(potential_fine, (2, 1, 0))
    kinetic, dipolar = grid_kernels(NF, 1.0)
    for repeat in range(FINE_STEPS):
        amplitude = advance(amplitude, potential, kinetic, dipolar, NF)
    return jnp.transpose(amplitude, (2, 1, 0))
```

```python
import math

import jax
import jax.numpy as jnp
import numpy as np
from jax import lax
from jax.sharding import Mesh
from jax.sharding import PartitionSpec as P

NC = 192
NF = 384
ROWS = ("rows_0", "rows_1", "rows_2")
COLS = ("cols_0", "cols_1")
ALL = ROWS + COLS
CHIPS = ("rows_0", "rows_1", "cols_0", "cols_1")
CORE = "rows_2"

TIME_STEP = 0.5
CONTACT = 0.4
DIPOLE_STRENGTH = 0.3
EPSILON = 1e-06
PREC = lax.Precision.HIGH


def cas_table(rows, columns, length):
    phases = 2.0 * math.pi / length * ((np.outer(rows, columns)) % length)
    return np.cos(phases) + np.sin(phases)


def signed(length):
    k = np.arange(length)
    return np.where(k < length // 2, k, k - length)


def tables():
    k = np.arange(NC)
    wave = 2.0 * math.pi / NF * signed(NC)
    decay = np.exp(-0.5 * TIME_STEP * wave**2)
    hc = cas_table(k, k, NC)
    hf = cas_table(np.arange(NF), np.arange(NF), NF)
    evolve = hc @ (decay[:, None] * hc) / NC
    lifted = np.where(k < NC // 2, k, k + NC)
    lift = hf[:, lifted] @ (decay[:, None] * hc) / NC
    return [t.astype(np.float32) for t in (hc, hf, evolve, lift)]


HC, HF, EVOLVE, LIFT = tables()


def squares(index, length, spacing):
    s = jnp.where(index < length // 2, index, index - length).astype(jnp.float32)
    w = 2.0 * math.pi / (length * spacing) * s
    return w * w


def dipolar(wx, wy, wz, length):
    q = wx + wy + wz
    safe = jnp.where(q > 0, q, 1.0)
    return jnp.where(q > 0, DIPOLE_STRENGTH * (3.0 * wz - q) / safe, 0.0) / float(length) ** 3


def es(spec, *args):
    return jnp.einsum(spec, *args, precision=PREC)


def exchange(buffer, axes, count):
    flat = buffer.reshape(count, 1, -1)
    return lax.all_to_all(flat, axes, split_axis=0, concat_axis=0, tiled=False)


def move_potential(potential, core):
    other = lax.ppermute(potential, CORE, [(0, 1), (1, 0)])
    low = jnp.where(core == 0, potential, other)
    high = jnp.where(core == 0, other, potential)
    both = jnp.concatenate([low, high], axis=0)
    moved = exchange(both, COLS, 8).reshape(8, 3, 24, NC)
    return moved.transpose(1, 0, 2, 3).reshape(3, NC, NC)


def per_device(wave_coarse, potential_coarse, potential_fine):
    core = lax.axis_index(CORE)
    chip = lax.axis_index(CHIPS)
    device = lax.axis_index(ALL)
    v_slab = move_potential(potential_coarse, core)

    turned = es("Zz,xyz->Zxy", EVOLVE, wave_coarse).reshape(3, 8, 8, 288)
    turned = turned.transpose(1, 2, 0, 3)[:, None]
    turned = jnp.broadcast_to(turned, (8, 2, 8, 3, 288))
    got = exchange(turned, ALL, 128).reshape(16, 8, 3, 12, 24)

    plane = got.transpose(2, 1, 4, 0, 3).reshape(3, NC, NC)
    evolved = es("Yy,kyx,xX->kYX", EVOLVE, plane, EVOLVE)
    spectrum = es("Yy,kyx->kYx", HC, evolved * evolved)
    pair = jnp.stack([spectrum, evolved], axis=2)
    pair = pair.reshape(3, 3, 64, 2, NC).transpose(2, 0, 1, 3, 4)
    got = exchange(pair, CHIPS, 64).reshape(64, 3, 3, 2, NC)

    both = got.transpose(3, 2, 4, 1, 0).reshape(2, 3, NC, NC)
    wz = squares(jnp.arange(NC), NC, 2.0)[None, None, :]
    wx = squares(jnp.arange(NC), NC, 2.0)[None, :, None]
    wy = squares(64 * jnp.arange(3) + chip, NC, 2.0)[:, None, None]
    mid = es("Xx,kxz,zZ->kXZ", HC, both[0], HC) * dipolar(wx, wy, wz, NC)
    mid = es("Xx,kxz,zZ->kXZ", HC, mid, HC)
    pair = jnp.stack([mid, both[1]], axis=2).reshape(3, 64, 3, 2, NC)
    got = exchange(pair.transpose(1, 2, 0, 3, 4), CHIPS, 64).reshape(64, 3, 3, 2, NC)

    both = got.transpose(3, 1, 2, 0, 4).reshape(2, 3, NC, NC)
    field = es("Yy,kyz->kYz", HC, both[0])
    evolved = both[1]
    damped = jnp.exp(-TIME_STEP * (v_slab + CONTACT * evolved * evolved + field)) * evolved
    part = jnp.sum(damped * damped)
    lift_y = jnp.asarray(LIFT).reshape(8, 2, 24, NC)
    lift_y = lax.dynamic_index_in_dim(lift_y, core, 1, keepdims=False).reshape(NC, NC)
    lifted = es("Zz,kyz,Yy->kZY", LIFT, damped, lift_y)
    lifted = lifted.reshape(3, 8, 48, 8, 24).transpose(3, 1, 0, 2, 4).reshape(64, 3456)
    lifted = jnp.concatenate([lifted, jnp.broadcast_to(part, (64, 128))], axis=1)
    got = exchange(lifted, CHIPS, 64).reshape(64, 3584)

    total = jnp.sum(got[:, 3456])
    scale = lax.rsqrt(total / float(NC) ** 3 + EPSILON)
    got = got[:, :3456].reshape(NC, 1152)
    evolved = es("Xx,xm->Xm", LIFT, got) * scale
    density = evolved * evolved
    spectrum = es("Xx,xm->Xm", HF, density)
    spectrum = spectrum.reshape(3, 128, 1152).transpose(1, 0, 2)
    got = exchange(spectrum, ALL, 128).reshape(16, 8, 3, 48, 24)

    plane = got.transpose(2, 1, 3, 0, 4).reshape(3, NF, NF)
    wz = squares(jnp.arange(NF), NF, 1.0)[None, :, None]
    wy = squares(jnp.arange(NF), NF, 1.0)[None, None, :]
    wx = squares(128 * jnp.arange(3) + device, NF, 1.0)[:, None, None]
    mid = es("Zz,kzy,yY->kZY", HF, plane, HF) * dipolar(wx, wy, wz, NF)
    mid = es("Zz,kzy,yY->kZY", HF, mid, HF)
    mid = mid.reshape(3, 8, 48, 16, 24).transpose(3, 1, 0, 2, 4)
    got = exchange(mid, ALL, 128).reshape(128, 3, 1152)

    spectrum = got.transpose(1, 0, 2).reshape(NF, 1152)
    field = es("Xx,xm->Xm", HF, spectrum)
    v_turned = potential_fine.reshape(1152, NF).T
    damped = jnp.exp(-TIME_STEP * (v_turned + CONTACT * density + field)) * evolved
    part = jnp.sum(damped * damped)
    parts = exchange(jnp.broadcast_to(part, (128, 128)), ALL, 128).reshape(128, 128)
    total = jnp.sum(parts[:, 0])
    return (damped.T * lax.rsqrt(total / float(NF) ** 3 + EPSILON)).reshape(48, 24, NF)


def solution(mesh):
    torus = Mesh(
        mesh.devices.reshape(4, 2, 2, 4, 2), ("rows_0", "rows_1", "rows_2", "cols_0", "cols_1")
    )
    return jax.shard_map(
        per_device,
        mesh=torus,
        in_specs=(P(ROWS, COLS, None), P(ROWS, COLS, None), P(COLS, ROWS, None)),
        out_specs=P(COLS, ROWS, None),
        check_vma=False,
    )
```

```python
import math

import jax
import jax.numpy as jnp
import numpy as np
from jax import lax
from jax.experimental import pallas as pl
from jax.experimental.pallas import tpu as pltpu
from jax.sharding import Mesh
from jax.sharding import PartitionSpec as P

NC = 192
NF = 384
ROWS = ("rows_0", "rows_1", "rows_2")
COLS = ("cols_0", "cols_1")
ALL = ROWS + COLS
CHIPS = ("rows_0", "rows_1", "cols_0", "cols_1")
CORE = "rows_2"

TIME_STEP = 0.5
CONTACT = 0.4
DIPOLE_STRENGTH = 0.3
EPSILON = 1e-06


def cas_table(rows, columns, length):
    phases = 2.0 * math.pi / length * ((np.outer(rows, columns)) % length)
    return np.cos(phases) + np.sin(phases)


def signed(length):
    k = np.arange(length)
    return np.where(k < length // 2, k, k - length)


def tables():
    k = np.arange(NC)
    wave = 2.0 * math.pi / NF * signed(NC)
    decay = np.exp(-0.5 * TIME_STEP * wave**2)
    hc = cas_table(k, k, NC)
    hf = cas_table(np.arange(NF), np.arange(NF), NF)
    evolve = hc @ (decay[:, None] * hc) / NC
    lifted = np.where(k < NC // 2, k, k + NC)
    lift = hf[:, lifted] @ (decay[:, None] * hc) / NC
    return [t.astype(np.float32) for t in (hc, hf, evolve, lift)]


HC, HF, EVOLVE, LIFT = tables()


def squares(index, length, spacing):
    s = jnp.where(index < length // 2, index, index - length).astype(jnp.float32)
    w = 2.0 * math.pi / (length * spacing) * s
    return w * w


def dipolar(wx, wy, wz, length):
    q = wx + wy + wz
    safe = jnp.where(q > 0, q, 1.0)
    return jnp.where(q > 0, DIPOLE_STRENGTH * (3.0 * wz - q) / safe, 0.0) / float(length) ** 3


F32 = jnp.float32
BF16 = jnp.bfloat16
VMEM = pl.BlockSpec(memory_space=pltpu.VMEM)
SMEM = pl.BlockSpec(memory_space=pltpu.SMEM)


def halves(table):
    high = table.astype(BF16)
    return np.stack([high, (table - high.astype(np.float32)).astype(BF16)])


HF2 = halves(HF)
BY_SLAB = np.arange(NF).reshape(8, 48).T.reshape(-1)
HF_OUT2 = halves(HF[:, BY_SLAB])
HF_BACK2 = halves(HF[BY_SLAB, :])
PLANE = np.arange(NC).reshape(16, 12).T.reshape(-1)
LIFT_X2 = halves(LIFT[:, np.arange(NC).reshape(64, 3).T.reshape(-1)])
HC2 = halves(HC)
HC_WIDE2 = halves(np.pad(HC, ((0, 64), (0, 64))))
EVOLVE2 = halves(EVOLVE)
EVOLVE_Y2 = halves(np.pad(EVOLVE, ((0, 0), (0, 64))))
EVOLVE_X2 = halves(np.concatenate([EVOLVE[PLANE, :]] * 2, axis=1))
LIFT_Z2 = halves(LIFT[BY_SLAB, :])
LIFT_Y2 = np.stack(
    [
        halves(np.pad(LIFT.reshape(8, 2, 24, NC)[:, core].reshape(NC, NC).T, ((0, 0), (0, 64))))
        for core in range(2)
    ]
)
TURNED = (((1,), (1,)), ((), ()))
PLAIN = (((1,), (0,)), ((), ()))


def split(x):
    high = x.astype(BF16)
    return high, (x - high.astype(F32)).astype(BF16)


def dot3(a, b, dims=PLAIN):
    (ah, al), (bh, bl) = a, b

    def dot(p, q):
        return lax.dot_general(p, q, dims, preferred_element_type=F32)

    return dot(ah, bh) + (dot(al, bh) + dot(ah, bl))


def pair(ref):
    return ref[0], ref[1]


def tiles_of(row):
    return [row[:, 128 * t : 128 * t + 128] for t in range(row.shape[1] // 128)]


def turn_blocks(rows, count, lead=0):
    lane = lax.broadcasted_iota(jnp.int32, rows[0][0].shape, 1)
    shifted = []
    for a, row in enumerate(rows):
        shift = (24 * a - lead) % NF
        whole = jnp.concatenate(row, axis=1)
        shifted.append(tiles_of(pltpu.roll(whole, shift, 1) if shift else whole))
    result = []
    for b in range(count):
        tiles = []
        for t in range(3):
            tile = None
            for p in range(128 * t // 24, (128 * t + 127) // 24 + 1):
                a = (p - b) % 16
                if a < len(rows):
                    piece = shifted[a][t]
                    tile = piece if tile is None else jnp.where(lane < 24 * p - 128 * t, tile, piece)
            tiles.append(shifted[0][t] if tile is None else tile)
        whole = jnp.concatenate(tiles, axis=1)
        result.append(pltpu.roll(whole, NF - 24 * b, 1) if b else whole)
    return result


def coarse_pencil_kernel(wave_ref, matrix_ref, out_ref):
    high, low = split(wave_ref[...])
    pieces = []
    for k in range(3):
        lead = 32 * k

        def padded(x):
            parts = [jnp.zeros((lead, NC), BF16)] * (k > 0) + [x]
            return jnp.concatenate(parts + [jnp.zeros((96 - lead, NC), BF16)], axis=0)

        rows = slice(64 * k, 64 * k + 64)
        matrix = (matrix_ref[0, rows, :], matrix_ref[1, rows, :])
        pieces.append(tiles_of(dot3(matrix, (padded(high), padded(low)), TURNED)))
    (a0, a1, a2), (b0, b1, b2), (c0, c1, c2) = pieces
    for t, tile in enumerate([a0, a1, a2 + b0, b1, b2 + c0, c1, c2]):
        for p in range(8):
            for core in range(2):
                out_ref[pl.ds(p * 112 + core * 56 + t, 8, stride=7), :] = tile[8 * p : 8 * p + 8, :]


def coarse_pencil(wave):
    return pl.pallas_call(
        coarse_pencil_kernel,
        out_shape=jax.ShapeDtypeStruct((896, 128), F32),
        in_specs=[VMEM] * 2,
        out_specs=VMEM,
    )(wave, jnp.asarray(EVOLVE2))


def coarse_z_kernel(got_ref, ey_ref, ex_ref, matrix_ref, out_ref, plane_ref):
    lane = lax.broadcasted_iota(jnp.int32, (64, 128), 1)
    for k in range(3):
        for g in range(2):
            rows = [
                [got_ref[pl.ds(g * 448 + c * 7 + 2 * k + t, 8, stride=56), :] for t in range(3)]
                for c in range(8)
            ]
            for i, row in enumerate(turn_blocks(rows, 12, 32 * k)):
                plane_ref[16 * i + 8 * g : 16 * i + 8 * g + 8, :] = row[:, :256]
        half = dot3(pair(ey_ref), split(plane_ref[...]), TURNED)
        evolved = dot3(split(half), pair(ex_ref))
        density = evolved[:, :256] * evolved[:, :256]
        turned = dot3(pair(matrix_ref), split(density))
        for j in range(3):
            f = tiles_of(turned[64 * j : 64 * j + 64, :])
            e = tiles_of(evolved[64 * j : 64 * j + 64, :])
            for t, tile in enumerate([f[0], jnp.where(lane < 64, f[1], e[1]), e[2]]):
                out_ref[pl.ds(k * 9 + j * 3 + t, 64, stride=27), :] = tile


def coarse_z(got):
    return pl.pallas_call(
        coarse_z_kernel,
        out_shape=jax.ShapeDtypeStruct((1728, 128), F32),
        in_specs=[VMEM] * 4,
        out_specs=VMEM,
        scratch_shapes=[pltpu.VMEM((NC, 256), F32)],
    )(got, jnp.asarray(EVOLVE_Y2), jnp.asarray(EVOLVE_X2), jnp.asarray(HC2))


def rows_of_plane(got_ref, base):
    rows = []
    for j in range(3):
        tiles = [got_ref[pl.ds(base + 9 * j + t, 64, stride=27), :] for t in range(3)]
        rows.append(jnp.concatenate(tiles, axis=1))
    return jnp.concatenate(rows, axis=0)


def coarse_y_kernel(chip_ref, got_ref, matrix_ref, wide_ref, out_ref):
    lane = lax.broadcasted_iota(jnp.int32, (NC, 128), 1)
    wx = squares(lax.broadcasted_iota(jnp.int32, (NC, 256), 0), NC, 2.0)
    wz = squares(lax.broadcasted_iota(jnp.int32, (NC, 256), 1), NC, 2.0)
    for k in range(3):
        both = rows_of_plane(got_ref, 3 * k)
        both = jnp.concatenate([both, jnp.zeros((64, 384), F32)], axis=0).T
        mid = dot3(pair(matrix_ref), split(both[:NC, :]))
        mid = dot3(split(mid), pair(wide_ref))
        wy = squares(jnp.full((1, 1), 64 * k + chip_ref[0], jnp.int32), NC, 2.0)
        mid = mid * dipolar(wx, wy, wz, NC)
        mid = dot3(split(mid), pair(wide_ref))
        q = tiles_of(dot3(pair(matrix_ref), split(mid)))
        e = [pltpu.roll(tile, 64, 1) for tile in tiles_of(both[NC:, :])]
        pieces = [q[0], jnp.where(lane < 64, q[1], e[0]), jnp.where(lane < 64, e[0], e[1])]
        for t, tile in enumerate(pieces):
            out_ref[pl.ds(3 * k + t, NC, stride=9), :] = tile


def coarse_y(chip, got):
    return pl.pallas_call(
        coarse_y_kernel,
        out_shape=jax.ShapeDtypeStruct((1728, 128), F32),
        in_specs=[SMEM] + [VMEM] * 3,
        out_specs=VMEM,
    )(chip, got, jnp.asarray(HC2), jnp.asarray(HC_WIDE2))


def coarse_x_kernel(core_ref, got_ref, potential_ref, matrix_ref, lz_ref, ly_ref, out_ref, lifted_ref):
    lane = lax.broadcasted_iota(jnp.int32, (NC, 128), 1)
    core = core_ref[0]
    lift_y = (ly_ref[core, 0], ly_ref[core, 1])
    part = jnp.zeros((1, 1), F32)
    blank = jnp.zeros((8, 128), F32)
    for k in range(3):
        rows = []
        for j in range(3):
            tiles = [got_ref[pl.ds(9 * k + 3 * j + t, 64, stride=27), :] for t in range(3)]
            rows.append(jnp.concatenate(tiles, axis=1))
        both = jnp.concatenate(rows, axis=0)
        field = dot3(pair(matrix_ref), split(both[:, :256]))
        e1, e2 = [pltpu.roll(tile, 64, 1) for tile in tiles_of(both)[1:]]
        evolved = [jnp.where(lane < 64, e1, e2), e2[:, :64]]
        pieces = []
        for t, e in enumerate(evolved):
            lanes = slice(128 * t, 128 * t + e.shape[1])
            v = jnp.concatenate([potential_ref[c, 24 * k : 24 * k + 24, lanes] for c in range(8)], axis=0)
            d = jnp.exp(-TIME_STEP * (v + CONTACT * e * e + field[:, lanes])) * e
            part = part + jnp.sum(d * d, keepdims=True)
            pieces.append(d)
        damped = split(jnp.concatenate(pieces, axis=1))
        lifted = dot3(pair(lz_ref), damped, TURNED)
        lifted_ref[...] = dot3(split(lifted), lift_y)
        for g in range(3):
            rows = []
            for i in range(16):
                row = lifted_ref[128 * g + 8 * i : 128 * g + 8 * i + 8, :]
                rows.append(tiles_of(row) + [blank])
            for p, row in enumerate(turn_blocks(rows, 8)):
                for t, tile in enumerate(tiles_of(row)):
                    out_ref[pl.ds(p * 224 + k * 9 + g * 3 + t, 8, stride=28), :] = tile
    out_ref[pl.ds(27, 64, stride=28), :] = jnp.broadcast_to(part, (64, 128))


def coarse_x(core, got, potential):
    return pl.pallas_call(
        coarse_x_kernel,
        out_shape=jax.ShapeDtypeStruct((1792, 128), F32),
        in_specs=[SMEM] + [VMEM] * 5,
        out_specs=VMEM,
        scratch_shapes=[pltpu.VMEM((NF, 256), F32)],
    )(core, got, potential, jnp.asarray(HC2), jnp.asarray(LIFT_Z2), jnp.asarray(LIFT_Y2))


def fine_in_kernel(got_ref, lift_ref, matrix_ref, evolved_ref, out_ref):
    parts = got_ref[pl.ds(27, 64, stride=28), :]
    total = jnp.sum(parts, axis=0, keepdims=True)
    scale = lax.rsqrt(total / float(NC) ** 3 + EPSILON)
    scale = jnp.concatenate([scale] * 3, axis=1)

    def body(n, carry):
        rows = []
        for k in range(3):
            tiles = [got_ref[pl.ds(k * 9 + 3 * n + t, 64, stride=28), :] for t in range(3)]
            rows.append(jnp.concatenate(tiles, axis=1))
        spectrum = split(jnp.concatenate(rows, axis=0))
        evolved = dot3(pair(lift_ref), spectrum) * scale
        evolved_ref[:, pl.ds(pl.multiple_of(n * 384, 128), 384)] = evolved
        turned = dot3(pair(matrix_ref), split(evolved * evolved))
        for k in range(3):
            for t in range(3):
                piece = turned[128 * k : 128 * k + 128, 128 * t : 128 * t + 128]
                out_ref[pl.ds(k * 9 + 3 * n + t, 128, stride=27), :] = piece
        return carry

    lax.fori_loop(0, 3, body, 0)


def fine_in(got):
    return pl.pallas_call(
        fine_in_kernel,
        out_shape=[
            jax.ShapeDtypeStruct((NF, 1152), F32),
            jax.ShapeDtypeStruct((3456, 128), F32),
        ],
        in_specs=[VMEM] * 3,
        out_specs=[VMEM] * 2,
    )(got, jnp.asarray(LIFT_X2), jnp.asarray(HF2))


def fine_slab_kernel(device_ref, got_ref, out_m_ref, back_m_ref, matrix_ref, out_ref, plane_ref):
    wz = squares(lax.broadcasted_iota(jnp.int32, (NF, NF), 0), NF, 1.0)
    wy = squares(lax.broadcasted_iota(jnp.int32, (NF, NF), 1), NF, 1.0)

    def body(k, carry):
        def unpack(g, carry):
            base = k * 9 + g * 3
            rows = [
                [got_ref[pl.ds(r * 216 + base + t, 8, stride=27), :] for t in range(3)]
                for r in range(16)
            ]
            for i, row in enumerate(turn_blocks(rows, 16)):
                plane_ref[pl.ds(pl.multiple_of(g * 128 + 8 * i, 8), 8), :] = row
            return carry

        lax.fori_loop(0, 3, unpack, 0)
        mid = dot3(pair(out_m_ref), split(plane_ref[...]))
        mid = dot3(split(mid), pair(matrix_ref))
        kx = 128 * k + device_ref[0]
        wx = squares(jnp.full((1, 1), kx, jnp.int32), NF, 1.0)
        mid = mid * dipolar(wx, wy, wz, NF)
        mid = dot3(split(mid), pair(matrix_ref))
        plane_ref[...] = dot3(pair(back_m_ref), split(mid))

        def pack(g, carry):
            base = k * 9 + g * 3
            rows = []
            for i in range(16):
                rows.append(tiles_of(plane_ref[pl.ds(pl.multiple_of(g * 128 + 8 * i, 8), 8), :]))
            for r, row in enumerate(turn_blocks(rows, 16)):
                for t, tile in enumerate(tiles_of(row)):
                    out_ref[pl.ds(r * 216 + base + t, 8, stride=27), :] = tile
            return carry

        lax.fori_loop(0, 3, pack, 0)
        return carry

    lax.fori_loop(0, 3, body, 0)


def fine_slab(device, got):
    return pl.pallas_call(
        fine_slab_kernel,
        out_shape=jax.ShapeDtypeStruct((3456, 128), F32),
        in_specs=[SMEM] + [VMEM] * 4,
        out_specs=VMEM,
        scratch_shapes=[pltpu.VMEM((NF, NF), F32)],
    )(device, got, jnp.asarray(HF_OUT2), jnp.asarray(HF_BACK2), jnp.asarray(HF2))


def fine_out_kernel(got_ref, evolved_ref, potential_ref, matrix_ref, damped_ref, part_ref):
    part_ref[...] = jnp.zeros_like(part_ref)

    def body(n, carry):
        rows = []
        for k in range(3):
            tiles = [got_ref[pl.ds(k * 9 + 3 * n + t, 128, stride=27), :] for t in range(3)]
            rows.append(jnp.concatenate(tiles, axis=1))
        field = dot3(pair(matrix_ref), split(jnp.concatenate(rows, axis=0)))
        columns = pl.ds(pl.multiple_of(n * 384, 128), 384)
        evolved = evolved_ref[:, columns]
        potential = potential_ref[columns, :].T
        exponent = -TIME_STEP * (potential + CONTACT * evolved * evolved + field)
        damped = jnp.exp(exponent) * evolved
        part_ref[...] += jnp.sum(damped * damped)
        damped_ref[columns, :] = damped.T
        return carry

    lax.fori_loop(0, 3, body, 0)


def fine_out(got, evolved, potential):
    return pl.pallas_call(
        fine_out_kernel,
        out_shape=[
            jax.ShapeDtypeStruct((1152, NF), F32),
            jax.ShapeDtypeStruct((8, 128), F32),
        ],
        in_specs=[VMEM] * 4,
        out_specs=[VMEM] * 2,
    )(got, evolved, potential, jnp.asarray(HF2))


def exchange(buffer, axes, count):
    flat = buffer.reshape(count, 1, -1)
    return lax.all_to_all(flat, axes, split_axis=0, concat_axis=0, tiled=False)


def move_potential(potential, core):
    other = lax.ppermute(potential, CORE, [(0, 1), (1, 0)])
    low = jnp.where(core == 0, potential, other)
    high = jnp.where(core == 0, other, potential)
    both = jnp.concatenate([low, high], axis=0).reshape(8, 72, NC)
    return lax.all_to_all(both, COLS, split_axis=0, concat_axis=0, tiled=False)


def per_device(wave_coarse, potential_coarse, potential_fine):
    core = lax.axis_index(CORE)
    chip = lax.axis_index(CHIPS)
    device = lax.axis_index(ALL)
    v_slab = move_potential(potential_coarse, core)

    turned = coarse_pencil(wave_coarse.reshape(288, NC))
    turned = coarse_z(exchange(turned, ALL, 128).reshape(896, 128))
    turned = coarse_y(chip.reshape(1), exchange(turned, CHIPS, 64).reshape(1728, 128))
    got = exchange(turned, CHIPS, 64).reshape(1728, 128)
    turned = coarse_x(core.reshape(1), got, v_slab)
    got = exchange(turned, CHIPS, 64).reshape(1792, 128)

    evolved, spectrum = fine_in(got)
    got = exchange(spectrum, ALL, 128).reshape(3456, 128)
    spectrum = fine_slab(device.reshape(1), got)
    got = exchange(spectrum, ALL, 128).reshape(3456, 128)
    damped, part = fine_out(got, evolved, potential_fine.reshape(1152, NF))
    parts = exchange(jnp.broadcast_to(part[:1], (128, 128)), ALL, 128).reshape(128, 128)
    total = jnp.sum(parts[:, 0])
    return (damped * lax.rsqrt(total / float(NF) ** 3 + EPSILON)).reshape(48, 24, NF)


def solution(mesh):
    torus = Mesh(
        mesh.devices.reshape(4, 2, 2, 4, 2), ("rows_0", "rows_1", "rows_2", "cols_0", "cols_1")
    )
    return jax.shard_map(
        per_device,
        mesh=torus,
        in_specs=(P(ROWS, COLS, None), P(ROWS, COLS, None), P(COLS, ROWS, None)),
        out_specs=P(COLS, ROWS, None),
        check_vma=False,
    )
```

```python
import math

import jax
import jax.numpy as jnp
import numpy as np
from jax import lax
from jax.experimental import pallas as pl
from jax.experimental.pallas import tpu as pltpu
from jax.sharding import Mesh
from jax.sharding import PartitionSpec as P

NC = 192
NF = 384
ROWS = ("rows_0", "rows_1", "rows_2")
COLS = ("cols_0", "cols_1")
ALL = ROWS + COLS
CHIPS = ("rows_0", "rows_1", "cols_0", "cols_1")
CORE = "rows_2"

TIME_STEP = 0.5
CONTACT = 0.4
DIPOLE_STRENGTH = 0.3
EPSILON = 1e-06


def cas_table(rows, columns, length):
    phases = 2.0 * math.pi / length * ((np.outer(rows, columns)) % length)
    return np.cos(phases) + np.sin(phases)


def signed(length):
    k = np.arange(length)
    return np.where(k < length // 2, k, k - length)


def tables():
    k = np.arange(NC)
    wave = 2.0 * math.pi / NF * signed(NC)
    decay = np.exp(-0.5 * TIME_STEP * wave**2)
    hc = cas_table(k, k, NC)
    hf = cas_table(np.arange(NF), np.arange(NF), NF)
    evolve = hc @ (decay[:, None] * hc) / NC
    lifted = np.where(k < NC // 2, k, k + NC)
    lift = hf[:, lifted] @ (decay[:, None] * hc) / NC
    return [t.astype(np.float32) for t in (hc, hf, evolve, lift)]


HC, HF, EVOLVE, LIFT = tables()


def squares(index, length, spacing):
    s = jnp.where(index < length // 2, index, index - length).astype(jnp.float32)
    w = 2.0 * math.pi / (length * spacing) * s
    return w * w


def dipolar(wx, wy, wz, length):
    q = wx + wy + wz
    safe = jnp.where(q > 0, q, 1.0)
    return jnp.where(q > 0, DIPOLE_STRENGTH * (3.0 * wz - q) / safe, 0.0) / float(length) ** 3


F32 = jnp.float32
BF16 = jnp.bfloat16
VMEM = pl.BlockSpec(memory_space=pltpu.VMEM)
SMEM = pl.BlockSpec(memory_space=pltpu.SMEM)
HBM = pl.BlockSpec(memory_space=pltpu.HBM)
LIMIT = pltpu.CompilerParams(vmem_limit_bytes=20 * 1024 * 1024)


def halves(table):
    high = table.astype(BF16)
    return np.stack([high, (table - high.astype(np.float32)).astype(BF16)])


HF2 = halves(HF)
BY_SLAB = np.arange(NF).reshape(8, 48).T.reshape(-1)
HF_OUT2 = halves(HF[:, BY_SLAB])
HF_BACK2 = halves(HF[BY_SLAB, :])
PLANE = np.arange(NC).reshape(16, 12).T.reshape(-1)
LIFT_X2 = halves(LIFT[:, np.arange(NC).reshape(64, 3).T.reshape(-1)])
HC2 = halves(HC)
HC_WIDE2 = halves(np.pad(HC, ((0, 64), (0, 64))))
EVOLVE2 = halves(EVOLVE)
EVOLVE_Y2 = halves(np.pad(EVOLVE, ((0, 0), (0, 64))))
EVOLVE_X2 = halves(np.concatenate([EVOLVE[PLANE, :]] * 2, axis=1))
LIFT_Z2 = halves(LIFT[BY_SLAB, :])
LIFT_Y2 = np.stack(
    [
        halves(np.pad(LIFT.reshape(8, 2, 24, NC)[:, core].reshape(NC, NC).T, ((0, 0), (0, 64))))
        for core in range(2)
    ]
)
TURNED = (((1,), (1,)), ((), ()))
PLAIN = (((1,), (0,)), ((), ()))


def split(x):
    high = x.astype(BF16)
    return high, (x - high.astype(F32)).astype(BF16)


def dot3(a, b, dims=PLAIN):
    (ah, al), (bh, bl) = a, b

    def dot(p, q):
        return lax.dot_general(p, q, dims, preferred_element_type=F32)

    return dot(ah, bh) + (dot(al, bh) + dot(ah, bl))


def dot(a, b):
    return jnp.dot(a, b, preferred_element_type=F32)


def left3(x):
    high, low = split(x)
    return jnp.concatenate([high, low, high], axis=1)


def right3(x):
    high, low = split(x)
    return jnp.concatenate([high, high, low], axis=0)


def fetch_left(table, wide, sems):
    size = table.shape[2]
    return [
        pltpu.make_async_copy(table.at[part], wide.at[:, pl.ds(i * size, size)], sems.at[i])
        for i, part in enumerate((0, 1, 0))
    ]


def fetch_right(table, tall, sems):
    size = table.shape[1]
    return [
        pltpu.make_async_copy(table.at[part], tall.at[pl.ds(i * size, size), :], sems.at[i])
        for i, part in enumerate((0, 0, 1))
    ]


def begin(copies):
    for copy in copies:
        copy.start()


def finish(copies):
    for copy in copies:
        copy.wait()


def pair(ref):
    return ref[0], ref[1]


def tiles_of(row):
    return [row[:, 128 * t : 128 * t + 128] for t in range(row.shape[1] // 128)]


def turn_blocks(rows, count, lead=0):
    lane = lax.broadcasted_iota(jnp.int32, rows[0][0].shape, 1)
    shifted = []
    for a, row in enumerate(rows):
        shift = (24 * a - lead) % NF
        whole = jnp.concatenate(row, axis=1)
        shifted.append(tiles_of(pltpu.roll(whole, shift, 1) if shift else whole))
    result = []
    for b in range(count):
        tiles = []
        for t in range(3):
            tile = None
            for p in range(128 * t // 24, (128 * t + 127) // 24 + 1):
                a = (p - b) % 16
                if a < len(rows):
                    piece = shifted[a][t]
                    tile = piece if tile is None else jnp.where(lane < 24 * p - 128 * t, tile, piece)
            tiles.append(shifted[0][t] if tile is None else tile)
        whole = jnp.concatenate(tiles, axis=1)
        result.append(pltpu.roll(whole, NF - 24 * b, 1) if b else whole)
    return result


def coarse_pencil_kernel(wave_hbm, matrix_hbm, out_ref, wave_ref, matrix_ref, sems):
    copies = [
        pltpu.make_async_copy(wave_hbm, wave_ref, sems.at[0]),
        pltpu.make_async_copy(matrix_hbm, matrix_ref, sems.at[1]),
    ]
    begin(copies)
    finish(copies)
    high, low = split(wave_ref[...])
    pieces = []
    for k in range(3):
        lead = 32 * k

        def padded(x):
            parts = [jnp.zeros((lead, NC), BF16)] * (k > 0) + [x]
            return jnp.concatenate(parts + [jnp.zeros((96 - lead, NC), BF16)], axis=0)

        rows = slice(64 * k, 64 * k + 64)
        matrix = (matrix_ref[0, rows, :], matrix_ref[1, rows, :])
        pieces.append(tiles_of(dot3(matrix, (padded(high), padded(low)), TURNED)))
    (a0, a1, a2), (b0, b1, b2), (c0, c1, c2) = pieces
    for t, tile in enumerate([a0, a1, a2 + b0, b1, b2 + c0, c1, c2]):
        for p in range(8):
            for core in range(2):
                out_ref[pl.ds(p * 112 + core * 56 + t, 8, stride=7), :] = tile[8 * p : 8 * p + 8, :]


def coarse_pencil(wave):
    return pl.pallas_call(
        coarse_pencil_kernel,
        out_shape=jax.ShapeDtypeStruct((896, 128), F32),
        compiler_params=LIMIT,
        in_specs=[HBM] * 2,
        out_specs=VMEM,
        scratch_shapes=[
            pltpu.VMEM((288, NC), F32),
            pltpu.VMEM((2, NC, NC), BF16),
            pltpu.SemaphoreType.DMA((2,)),
        ],
    )(wave, jnp.asarray(EVOLVE2))


def coarse_z_kernel(got_ref, ey_ref, ex_ref, matrix_ref, out_ref, plane_ref):
    lane = lax.broadcasted_iota(jnp.int32, (64, 128), 1)
    for k in range(3):
        for g in range(2):
            rows = [
                [got_ref[pl.ds(g * 448 + c * 7 + 2 * k + t, 8, stride=56), :] for t in range(3)]
                for c in range(8)
            ]
            for i, row in enumerate(turn_blocks(rows, 12, 32 * k)):
                plane_ref[16 * i + 8 * g : 16 * i + 8 * g + 8, :] = row[:, :256]
        half = dot3(pair(ey_ref), split(plane_ref[...]), TURNED)
        evolved = dot3(split(half), pair(ex_ref))
        density = evolved[:, :256] * evolved[:, :256]
        turned = dot3(pair(matrix_ref), split(density))
        for j in range(3):
            f = tiles_of(turned[64 * j : 64 * j + 64, :])
            e = tiles_of(evolved[64 * j : 64 * j + 64, :])
            for t, tile in enumerate([f[0], jnp.where(lane < 64, f[1], e[1]), e[2]]):
                out_ref[pl.ds(k * 9 + j * 3 + t, 64, stride=27), :] = tile


def coarse_z(got):
    return pl.pallas_call(
        coarse_z_kernel,
        out_shape=jax.ShapeDtypeStruct((1728, 128), F32),
        compiler_params=LIMIT,
        in_specs=[VMEM] * 4,
        out_specs=VMEM,
        scratch_shapes=[pltpu.VMEM((NC, 256), F32)],
    )(got, jnp.asarray(EVOLVE_Y2), jnp.asarray(EVOLVE_X2), jnp.asarray(HC2))


def rows_of_plane(got_ref, base):
    rows = []
    for j in range(3):
        tiles = [got_ref[pl.ds(base + 9 * j + t, 64, stride=27), :] for t in range(3)]
        rows.append(jnp.concatenate(tiles, axis=1))
    return jnp.concatenate(rows, axis=0)


def coarse_y_kernel(place_ref, got_ref, matrix_ref, wide_ref, out_ref):
    lane = lax.broadcasted_iota(jnp.int32, (NC, 128), 1)
    wx = squares(lax.broadcasted_iota(jnp.int32, (NC, 256), 0), NC, 2.0)
    wz = squares(lax.broadcasted_iota(jnp.int32, (NC, 256), 1), NC, 2.0)
    for k in range(3):
        both = rows_of_plane(got_ref, 3 * k)
        both = jnp.concatenate([both, jnp.zeros((64, 384), F32)], axis=0).T
        mid = dot3(pair(matrix_ref), split(both[:NC, :]))
        mid = dot3(split(mid), pair(wide_ref))
        wy = squares(jnp.full((1, 1), 64 * k + place_ref[3], jnp.int32), NC, 2.0)
        mid = mid * dipolar(wx, wy, wz, NC)
        mid = dot3(split(mid), pair(wide_ref))
        q = tiles_of(dot3(pair(matrix_ref), split(mid)))
        e = [pltpu.roll(tile, 64, 1) for tile in tiles_of(both[NC:, :])]
        pieces = [q[0], jnp.where(lane < 64, q[1], e[0]), jnp.where(lane < 64, e[0], e[1])]
        for t, tile in enumerate(pieces):
            out_ref[pl.ds(3 * k + t, NC, stride=9), :] = tile


def coarse_y(place, got):
    return pl.pallas_call(
        coarse_y_kernel,
        out_shape=jax.ShapeDtypeStruct((1728, 128), F32),
        compiler_params=LIMIT,
        in_specs=[SMEM] + [VMEM] * 3,
        out_specs=VMEM,
    )(place, got, jnp.asarray(HC2), jnp.asarray(HC_WIDE2))


def coarse_x_kernel(place_ref, got_ref, potential_ref, matrix_ref, lz_ref, ly_ref, out_ref, lifted_ref):
    lane = lax.broadcasted_iota(jnp.int32, (NC, 128), 1)
    core = place_ref[0]
    slots = []
    for c in range(8):
        slots.append(lax.rem(place_ref[1] - c // 2 + 4, 4) + 4 * (place_ref[2] ^ (c % 2)))
    lift_y = (ly_ref[core, 0], ly_ref[core, 1])
    part = jnp.zeros((1, 1), F32)
    blank = jnp.zeros((8, 128), F32)
    for k in range(3):
        rows = []
        for j in range(3):
            tiles = [got_ref[pl.ds(9 * k + 3 * j + t, 64, stride=27), :] for t in range(3)]
            rows.append(jnp.concatenate(tiles, axis=1))
        both = jnp.concatenate(rows, axis=0)
        field = dot3(pair(matrix_ref), split(both[:, :256]))
        e1, e2 = [pltpu.roll(tile, 64, 1) for tile in tiles_of(both)[1:]]
        evolved = [jnp.where(lane < 64, e1, e2), e2[:, :64]]
        pieces = []
        for t, e in enumerate(evolved):
            lanes = slice(128 * t, 128 * t + e.shape[1])
            v = jnp.concatenate([potential_ref[c, 24 * k : 24 * k + 24, lanes] for c in slots], axis=0)
            d = jnp.exp(-TIME_STEP * (v + CONTACT * e * e + field[:, lanes])) * e
            part = part + jnp.sum(d * d, keepdims=True)
            pieces.append(d)
        damped = split(jnp.concatenate(pieces, axis=1))
        lifted = dot3(pair(lz_ref), damped, TURNED)
        lifted_ref[...] = dot3(split(lifted), lift_y)
        for g in range(3):
            rows = []
            for i in range(16):
                row = lifted_ref[128 * g + 8 * i : 128 * g + 8 * i + 8, :]
                rows.append(tiles_of(row) + [blank])
            for p, row in enumerate(turn_blocks(rows, 8)):
                for t, tile in enumerate(tiles_of(row)):
                    out_ref[pl.ds(p * 224 + k * 9 + g * 3 + t, 8, stride=28), :] = tile
    out_ref[pl.ds(27, 64, stride=28), :] = jnp.broadcast_to(part, (64, 128))


def coarse_x(place, got, potential):
    return pl.pallas_call(
        coarse_x_kernel,
        out_shape=jax.ShapeDtypeStruct((1792, 128), F32),
        compiler_params=LIMIT,
        in_specs=[SMEM] + [VMEM] * 5,
        out_specs=VMEM,
        scratch_shapes=[pltpu.VMEM((NF, 256), F32)],
    )(place, got, potential, jnp.asarray(HC2), jnp.asarray(LIFT_Z2), jnp.asarray(LIFT_Y2))


def fine_in_kernel(
    got_ref, lift_ref, matrix_hbm, evolved_hbm, out_ref, evolved_ref, matrix_ref, sems, saved
):
    copies = fetch_left(matrix_hbm, matrix_ref, sems)
    begin(copies)
    parts = got_ref[pl.ds(27, 64, stride=28), :]
    total = jnp.sum(parts, axis=0, keepdims=True)
    scale = lax.rsqrt(total / float(NC) ** 3 + EPSILON)
    scale = jnp.concatenate([scale] * 3, axis=1)
    finish(copies)

    def save(n):
        columns = pl.ds(pl.multiple_of(n * 384, 128), 384)
        source, target = evolved_ref.at[:, columns], evolved_hbm.at[:, columns]
        return pltpu.make_async_copy(source, target, saved.at[n])

    def body(n, carry):
        rows = []
        for k in range(3):
            tiles = [got_ref[pl.ds(k * 9 + 3 * n + t, 64, stride=28), :] for t in range(3)]
            rows.append(jnp.concatenate(tiles, axis=1))
        spectrum = split(jnp.concatenate(rows, axis=0))
        evolved = dot3(pair(lift_ref), spectrum) * scale
        evolved_ref[:, pl.ds(pl.multiple_of(n * 384, 128), 384)] = evolved
        turned = dot(matrix_ref[...], right3(evolved * evolved))
        for k in range(3):
            for t in range(3):
                piece = turned[128 * k : 128 * k + 128, 128 * t : 128 * t + 128]
                out_ref[pl.ds(k * 9 + 3 * n + t, 128, stride=27), :] = piece
        save(n).start()
        return carry

    lax.fori_loop(0, 3, body, 0)
    for n in range(3):
        save(n).wait()


def fine_in(got):
    return pl.pallas_call(
        fine_in_kernel,
        out_shape=[
            pltpu.HBM((NF, 1152), F32),
            jax.ShapeDtypeStruct((3456, 128), F32),
        ],
        compiler_params=LIMIT,
        in_specs=[VMEM, VMEM, HBM],
        out_specs=[HBM, VMEM],
        scratch_shapes=[
            pltpu.VMEM((NF, 1152), F32),
            pltpu.VMEM((NF, 1152), BF16),
            pltpu.SemaphoreType.DMA((3,)),
            pltpu.SemaphoreType.DMA((3,)),
        ],
    )(got, jnp.asarray(LIFT_X2), jnp.asarray(HF2))


def fine_slab_kernel(
    place_ref, got_ref, out_hbm, back_hbm, matrix_hbm, out_ref, plane_ref, out_m, back_m, matrix, sems
):
    out_copies = fetch_left(out_hbm, out_m, sems.at[0])
    back_copies = fetch_left(back_hbm, back_m, sems.at[1])
    copies = fetch_right(matrix_hbm, matrix, sems.at[2])
    begin(out_copies + copies + back_copies)
    wz = squares(lax.broadcasted_iota(jnp.int32, (NF, NF), 0), NF, 1.0)
    wy = squares(lax.broadcasted_iota(jnp.int32, (NF, NF), 1), NF, 1.0)

    def body(k, carry):
        def unpack(g, carry):
            base = k * 9 + g * 3
            rows = [
                [got_ref[pl.ds(r * 216 + base + t, 8, stride=27), :] for t in range(3)]
                for r in range(16)
            ]
            for i, row in enumerate(turn_blocks(rows, 16)):
                plane_ref[pl.ds(pl.multiple_of(g * 128 + 8 * i, 8), 8), :] = row
            return carry

        lax.fori_loop(0, 3, unpack, 0)

        @pl.when(k == 0)
        def _():
            finish(out_copies + copies + back_copies)

        mid = dot(out_m[...], right3(plane_ref[...]))
        mid = dot(left3(mid), matrix[...])
        kx = 128 * k + place_ref[4]
        wx = squares(jnp.full((1, 1), kx, jnp.int32), NF, 1.0)
        mid = mid * dipolar(wx, wy, wz, NF)
        mid = dot(left3(mid), matrix[...])
        plane_ref[...] = dot(back_m[...], right3(mid))

        def pack(g, carry):
            base = k * 9 + g * 3
            rows = []
            for i in range(16):
                rows.append(tiles_of(plane_ref[pl.ds(pl.multiple_of(g * 128 + 8 * i, 8), 8), :]))
            for r, row in enumerate(turn_blocks(rows, 16)):
                for t, tile in enumerate(tiles_of(row)):
                    out_ref[pl.ds(r * 216 + base + t, 8, stride=27), :] = tile
            return carry

        lax.fori_loop(0, 3, pack, 0)
        return carry

    lax.fori_loop(0, 3, body, 0)


def fine_slab(place, got):
    return pl.pallas_call(
        fine_slab_kernel,
        out_shape=jax.ShapeDtypeStruct((3456, 128), F32),
        compiler_params=LIMIT,
        in_specs=[SMEM, VMEM] + [HBM] * 3,
        out_specs=VMEM,
        scratch_shapes=[
            pltpu.VMEM((NF, NF), F32),
            pltpu.VMEM((NF, 1152), BF16),
            pltpu.VMEM((NF, 1152), BF16),
            pltpu.VMEM((1152, NF), BF16),
            pltpu.SemaphoreType.DMA((3, 3)),
        ],
    )(place, got, jnp.asarray(HF_OUT2), jnp.asarray(HF_BACK2), jnp.asarray(HF2))


def fine_out_kernel(got_ref, evolved_ref, potential_ref, matrix_ref, damped_ref, part_ref):
    part_ref[...] = jnp.zeros_like(part_ref)

    def body(n, carry):
        rows = []
        for k in range(3):
            tiles = [got_ref[pl.ds(k * 9 + 3 * n + t, 128, stride=27), :] for t in range(3)]
            rows.append(jnp.concatenate(tiles, axis=1))
        field = dot3(pair(matrix_ref), split(jnp.concatenate(rows, axis=0)))
        columns = pl.ds(pl.multiple_of(n * 384, 128), 384)
        evolved = evolved_ref[:, columns]
        potential = potential_ref[columns, :].T
        exponent = -TIME_STEP * (potential + CONTACT * evolved * evolved + field)
        damped = jnp.exp(exponent) * evolved
        part_ref[...] += jnp.sum(damped * damped)
        damped_ref[columns, :] = damped.T
        return carry

    lax.fori_loop(0, 3, body, 0)


def fine_out(got, evolved, potential):
    return pl.pallas_call(
        fine_out_kernel,
        out_shape=[
            jax.ShapeDtypeStruct((1152, NF), F32),
            jax.ShapeDtypeStruct((128, 128), F32),
        ],
        compiler_params=LIMIT,
        in_specs=[VMEM] * 4,
        out_specs=[VMEM] * 2,
    )(got, evolved, potential, jnp.asarray(HF2))


def scale_kernel(parts_ref, damped_ref, out_hbm, scaled_ref, sems):
    total = jnp.sum(parts_ref[...], axis=0, keepdims=True)
    scale = lax.rsqrt(total / float(NF) ** 3 + EPSILON)
    scale = jnp.concatenate([scale] * 3, axis=1)
    copies = []
    for i in range(4):
        rows = pl.ds(288 * i, 288)
        copies.append(pltpu.make_async_copy(scaled_ref.at[rows], out_hbm.at[rows], sems.at[i]))
        scaled_ref[rows, :] = damped_ref[rows, :] * scale
        if i:
            copies[i - 1].start()
    copies[3].start()
    finish(copies)


def scaled(parts, damped):
    return pl.pallas_call(
        scale_kernel,
        out_shape=jax.ShapeDtypeStruct((1152, NF), F32),
        compiler_params=LIMIT,
        in_specs=[VMEM] * 2,
        out_specs=HBM,
        scratch_shapes=[pltpu.VMEM((1152, NF), F32), pltpu.SemaphoreType.DMA((4,))],
    )(parts, damped)


def exchange(buffer, axes, count):
    flat = buffer.reshape(count, 1, -1)
    return lax.all_to_all(flat, axes, split_axis=0, concat_axis=0, tiled=False)


def pair_planes(potential, core):
    other = lax.ppermute(potential, CORE, [(0, 1), (1, 0)])
    low = jnp.where(core == 0, potential, other)
    high = jnp.where(core == 0, other, potential)
    return jnp.concatenate([low, high], axis=0).reshape(4, 2, 72, NC)


def spread_planes(both):
    across = lax.axis_index("cols_0")
    slots = []
    for i in range(4):
        chunk = lax.dynamic_index_in_dim(both, (across + i) % 4, 0, keepdims=False)
        if i:
            chunk = lax.ppermute(chunk, "cols_0", [(s, (s + i) % 4) for s in range(4)])
        slots.append(chunk)
    return jnp.stack(slots, axis=1)


def join_planes(slots):
    near = lax.axis_index("cols_1")
    mine = lax.dynamic_index_in_dim(slots, near, 0, keepdims=False)
    theirs = lax.dynamic_index_in_dim(slots, 1 - near, 0, keepdims=False)
    return jnp.concatenate([mine, lax.ppermute(theirs, "cols_1", [(0, 1), (1, 0)])], axis=0)


def per_device(wave_coarse, potential_coarse, potential_fine):
    core = lax.axis_index(CORE)
    chip = lax.axis_index(CHIPS)
    device = lax.axis_index(ALL)
    across, near = lax.axis_index("cols_0"), lax.axis_index("cols_1")
    place = jnp.stack([core, across, near, chip, device])

    got = exchange(coarse_pencil(wave_coarse.reshape(288, NC)), ALL, 128).reshape(896, 128)
    got, planes = lax.optimization_barrier((got, pair_planes(potential_coarse, core)))
    got = exchange(coarse_z(got), CHIPS, 64).reshape(1728, 128)
    got, planes = lax.optimization_barrier((got, spread_planes(planes)))
    got = exchange(coarse_y(place, got), CHIPS, 64).reshape(1728, 128)
    turned = coarse_x(place, got, join_planes(planes))
    got = exchange(turned, CHIPS, 64).reshape(1792, 128)

    evolved, spectrum = fine_in(got)
    got = exchange(spectrum, ALL, 128).reshape(3456, 128)
    spectrum = fine_slab(place, got)
    got = exchange(spectrum, ALL, 128).reshape(3456, 128)
    damped, part = fine_out(got, evolved, potential_fine.reshape(1152, NF))
    parts = exchange(part, ALL, 128).reshape(128, 128)
    return scaled(parts, damped).reshape(48, 24, NF)


def solution(mesh):
    torus = Mesh(
        mesh.devices.reshape(4, 2, 2, 4, 2), ("rows_0", "rows_1", "rows_2", "cols_0", "cols_1")
    )
    return jax.shard_map(
        per_device,
        mesh=torus,
        in_specs=(P(ROWS, COLS, None), P(ROWS, COLS, None), P(COLS, ROWS, None)),
        out_specs=P(COLS, ROWS, None),
        check_vma=False,
    )
```

```python
import math

import jax
import jax.numpy as jnp
import numpy as np
from jax import lax
from jax.experimental import pallas as pl
from jax.experimental.pallas import tpu as pltpu
from jax.sharding import Mesh
from jax.sharding import PartitionSpec as P

NC = 192
NF = 384
ROWS = ("rows_0", "rows_1", "rows_2")
COLS = ("cols_0", "cols_1")
ALL = ROWS + COLS
CHIPS = ("rows_0", "rows_1", "cols_0", "cols_1")
CORE = "rows_2"

TIME_STEP = 0.5
CONTACT = 0.4
DIPOLE_STRENGTH = 0.3
EPSILON = 1e-06


def cas_table(rows, columns, length):
    phases = 2.0 * math.pi / length * ((np.outer(rows, columns)) % length)
    return np.cos(phases) + np.sin(phases)


def signed(length):
    k = np.arange(length)
    return np.where(k < length // 2, k, k - length)


def tables():
    k = np.arange(NC)
    wave = 2.0 * math.pi / NF * signed(NC)
    decay = np.exp(-0.5 * TIME_STEP * wave**2)
    hc = cas_table(k, k, NC)
    hf = cas_table(np.arange(NF), np.arange(NF), NF)
    evolve = hc @ (decay[:, None] * hc) / NC
    lifted = np.where(k < NC // 2, k, k + NC)
    lift = hf[:, lifted] @ (decay[:, None] * hc) / NC
    return [t.astype(np.float32) for t in (hc, hf, evolve, lift)]


HC, HF, EVOLVE, LIFT = tables()


def squares(index, length, spacing):
    s = jnp.where(index < length // 2, index, index - length).astype(jnp.float32)
    w = 2.0 * math.pi / (length * spacing) * s
    return w * w


def dipolar(wx, wy, wz, length):
    q = wx + wy + wz
    safe = jnp.where(q > 0, q, 1.0)
    return jnp.where(q > 0, DIPOLE_STRENGTH * (3.0 * wz - q) / safe, 0.0) / float(length) ** 3


F32 = jnp.float32
BF16 = jnp.bfloat16
VMEM = pl.BlockSpec(memory_space=pltpu.VMEM)
SMEM = pl.BlockSpec(memory_space=pltpu.SMEM)
HBM = pl.BlockSpec(memory_space=pltpu.HBM)
LIMIT = pltpu.CompilerParams(vmem_limit_bytes=20 * 1024 * 1024)


def halves(table):
    high = table.astype(BF16)
    return np.stack([high, (table - high.astype(np.float32)).astype(BF16)])


HF2 = halves(HF)
BY_SLAB = np.arange(NF).reshape(8, 48).T.reshape(-1)
HF_OUT2 = halves(HF[:, BY_SLAB])
HF_BACK2 = halves(HF[BY_SLAB, :])
PLANE = np.arange(NC).reshape(16, 12).T.reshape(-1)
LIFT_X2 = halves(LIFT[:, np.arange(NC).reshape(64, 3).T.reshape(-1)])
HC2 = halves(HC)
HC_WIDE2 = halves(np.pad(HC, ((0, 64), (0, 64))))
EVOLVE2 = halves(EVOLVE)
EVOLVE_Y2 = halves(np.pad(EVOLVE, ((0, 0), (0, 64))))
EVOLVE_X2 = halves(np.concatenate([EVOLVE[PLANE, :]] * 2, axis=1))
LIFT_Z2 = halves(LIFT[BY_SLAB, :])
LIFT_Y2 = np.stack(
    [
        halves(np.pad(LIFT.reshape(8, 2, 24, NC)[:, core].reshape(NC, NC).T, ((0, 0), (0, 64))))
        for core in range(2)
    ]
)
TURNED = (((1,), (1,)), ((), ()))
PLAIN = (((1,), (0,)), ((), ()))


def split(x):
    high = x.astype(BF16)
    return high, (x - high.astype(F32)).astype(BF16)


def dot3(a, b, dims=PLAIN):
    (ah, al), (bh, bl) = a, b

    def dot(p, q):
        return lax.dot_general(p, q, dims, preferred_element_type=F32)

    return dot(ah, bh) + (dot(al, bh) + dot(ah, bl))


def dot(a, b):
    return jnp.dot(a, b, preferred_element_type=F32)


def left3(x):
    high, low = split(x)
    return jnp.concatenate([high, low, high], axis=1)


def right3(x):
    high, low = split(x)
    return jnp.concatenate([high, high, low], axis=0)


def fetch_left(table, wide, sems):
    size = table.shape[2]
    return [
        pltpu.make_async_copy(table.at[part], wide.at[:, pl.ds(i * size, size)], sems.at[i])
        for i, part in enumerate((0, 1, 0))
    ]


def fetch_right(table, tall, sems):
    size = table.shape[1]
    return [
        pltpu.make_async_copy(table.at[part], tall.at[pl.ds(i * size, size), :], sems.at[i])
        for i, part in enumerate((0, 0, 1))
    ]


def begin(copies):
    for copy in copies:
        copy.start()


def finish(copies):
    for copy in copies:
        copy.wait()


def pair(ref):
    return ref[0], ref[1]


def tiles_of(row):
    return [row[:, 128 * t : 128 * t + 128] for t in range(row.shape[1] // 128)]


def turn_blocks(rows, count, lead=0):
    lane = lax.broadcasted_iota(jnp.int32, rows[0][0].shape, 1)
    shifted = []
    for a, row in enumerate(rows):
        shift = (24 * a - lead) % NF
        whole = jnp.concatenate(row, axis=1)
        shifted.append(tiles_of(pltpu.roll(whole, shift, 1) if shift else whole))
    result = []
    for b in range(count):
        tiles = []
        for t in range(3):
            tile = None
            for p in range(128 * t // 24, (128 * t + 127) // 24 + 1):
                a = (p - b) % 16
                if a < len(rows):
                    piece = shifted[a][t]
                    tile = piece if tile is None else jnp.where(lane < 24 * p - 128 * t, tile, piece)
            tiles.append(shifted[0][t] if tile is None else tile)
        whole = jnp.concatenate(tiles, axis=1)
        result.append(pltpu.roll(whole, NF - 24 * b, 1) if b else whole)
    return result


def in_hbm(x):
    return pltpu.with_memory_space_constraint(x, pltpu.HBM)


def coarse_pencil_kernel(wave_hbm, matrix_hbm, out_ref, wave_ref, matrix_ref, sems):
    copies = [
        pltpu.make_async_copy(wave_hbm, wave_ref, sems.at[0]),
        pltpu.make_async_copy(matrix_hbm, matrix_ref, sems.at[1]),
    ]
    begin(copies)
    finish(copies)
    high, low = split(wave_ref[...])
    pieces = []
    for k in range(3):
        lead = 32 * k

        def padded(x):
            parts = [jnp.zeros((lead, NC), BF16)] * (k > 0) + [x]
            return jnp.concatenate(parts + [jnp.zeros((96 - lead, NC), BF16)], axis=0)

        rows = slice(64 * k, 64 * k + 64)
        matrix = (matrix_ref[0, rows, :], matrix_ref[1, rows, :])
        pieces.append(tiles_of(dot3(matrix, (padded(high), padded(low)), TURNED)))
    (a0, a1, a2), (b0, b1, b2), (c0, c1, c2) = pieces
    for t, tile in enumerate([a0, a1, a2 + b0, b1, b2 + c0, c1, c2]):
        for p in range(8):
            for core in range(2):
                out_ref[pl.ds(p * 112 + core * 56 + t, 8, stride=7), :] = tile[8 * p : 8 * p + 8, :]


def coarse_pencil(wave):
    return pl.pallas_call(
        coarse_pencil_kernel,
        out_shape=jax.ShapeDtypeStruct((896, 128), F32),
        compiler_params=LIMIT,
        in_specs=[HBM] * 2,
        out_specs=VMEM,
        scratch_shapes=[
            pltpu.VMEM((288, NC), F32),
            pltpu.VMEM((2, NC, NC), BF16),
            pltpu.SemaphoreType.DMA((2,)),
        ],
    )(in_hbm(wave), in_hbm(jnp.asarray(EVOLVE2)))


def coarse_z_kernel(got_ref, ey_ref, ex_ref, matrix_ref, out_ref, plane_ref):
    lane = lax.broadcasted_iota(jnp.int32, (64, 128), 1)
    for k in range(3):
        for g in range(2):
            rows = [
                [got_ref[pl.ds(g * 448 + c * 7 + 2 * k + t, 8, stride=56), :] for t in range(3)]
                for c in range(8)
            ]
            for i, row in enumerate(turn_blocks(rows, 12, 32 * k)):
                plane_ref[16 * i + 8 * g : 16 * i + 8 * g + 8, :] = row[:, :256]
        half = dot3(pair(ey_ref), split(plane_ref[...]), TURNED)
        evolved = dot3(split(half), pair(ex_ref))
        density = evolved[:, :256] * evolved[:, :256]
        turned = dot3(pair(matrix_ref), split(density))
        for j in range(3):
            f = tiles_of(turned[64 * j : 64 * j + 64, :])
            e = tiles_of(evolved[64 * j : 64 * j + 64, :])
            for t, tile in enumerate([f[0], jnp.where(lane < 64, f[1], e[1]), e[2]]):
                out_ref[pl.ds(k * 9 + j * 3 + t, 64, stride=27), :] = tile


def coarse_z(got):
    return pl.pallas_call(
        coarse_z_kernel,
        out_shape=jax.ShapeDtypeStruct((1728, 128), F32),
        compiler_params=LIMIT,
        in_specs=[VMEM] * 4,
        out_specs=VMEM,
        scratch_shapes=[pltpu.VMEM((NC, 256), F32)],
    )(got, jnp.asarray(EVOLVE_Y2), jnp.asarray(EVOLVE_X2), jnp.asarray(HC2))


def rows_of_plane(got_ref, base):
    rows = []
    for j in range(3):
        tiles = [got_ref[pl.ds(base + 9 * j + t, 64, stride=27), :] for t in range(3)]
        rows.append(jnp.concatenate(tiles, axis=1))
    return jnp.concatenate(rows, axis=0)


def coarse_y_kernel(place_ref, got_ref, matrix_ref, wide_ref, out_ref):
    lane = lax.broadcasted_iota(jnp.int32, (NC, 128), 1)
    wx = squares(lax.broadcasted_iota(jnp.int32, (NC, 256), 0), NC, 2.0)
    wz = squares(lax.broadcasted_iota(jnp.int32, (NC, 256), 1), NC, 2.0)
    for k in range(3):
        both = rows_of_plane(got_ref, 3 * k)
        both = jnp.concatenate([both, jnp.zeros((64, 384), F32)], axis=0).T
        mid = dot3(pair(matrix_ref), split(both[:NC, :]))
        mid = dot3(split(mid), pair(wide_ref))
        wy = squares(jnp.full((1, 1), 64 * k + place_ref[3], jnp.int32), NC, 2.0)
        mid = mid * dipolar(wx, wy, wz, NC)
        mid = dot3(split(mid), pair(wide_ref))
        q = tiles_of(dot3(pair(matrix_ref), split(mid)))
        e = [pltpu.roll(tile, 64, 1) for tile in tiles_of(both[NC:, :])]
        pieces = [q[0], jnp.where(lane < 64, q[1], e[0]), jnp.where(lane < 64, e[0], e[1])]
        for t, tile in enumerate(pieces):
            out_ref[pl.ds(3 * k + t, NC, stride=9), :] = tile


def coarse_y(place, got):
    return pl.pallas_call(
        coarse_y_kernel,
        out_shape=jax.ShapeDtypeStruct((1728, 128), F32),
        compiler_params=LIMIT,
        in_specs=[SMEM] + [VMEM] * 3,
        out_specs=VMEM,
    )(place, got, jnp.asarray(HC2), jnp.asarray(HC_WIDE2))


def coarse_x_kernel(place_ref, got_ref, potential_ref, matrix_ref, lz_ref, ly_ref, out_ref, lifted_ref):
    lane = lax.broadcasted_iota(jnp.int32, (NC, 128), 1)
    core = place_ref[0]
    slots = []
    for c in range(8):
        slots.append(2 * lax.rem(place_ref[1] - c // 2 + 4, 4) + (place_ref[2] ^ (c % 2)))
    lift_y = (ly_ref[core, 0], ly_ref[core, 1])
    part = jnp.zeros((1, 1), F32)
    blank = jnp.zeros((8, 128), F32)
    for k in range(3):
        rows = []
        for j in range(3):
            tiles = [got_ref[pl.ds(9 * k + 3 * j + t, 64, stride=27), :] for t in range(3)]
            rows.append(jnp.concatenate(tiles, axis=1))
        both = jnp.concatenate(rows, axis=0)
        field = dot3(pair(matrix_ref), split(both[:, :256]))
        e1, e2 = [pltpu.roll(tile, 64, 1) for tile in tiles_of(both)[1:]]
        evolved = [jnp.where(lane < 64, e1, e2), e2[:, :64]]
        pieces = []
        for t, e in enumerate(evolved):
            lanes = slice(128 * t, 128 * t + e.shape[1])
            v = jnp.concatenate([potential_ref[c, 24 * k : 24 * k + 24, lanes] for c in slots], axis=0)
            d = jnp.exp(-TIME_STEP * (v + CONTACT * e * e + field[:, lanes])) * e
            part = part + jnp.sum(d * d, keepdims=True)
            pieces.append(d)
        damped = split(jnp.concatenate(pieces, axis=1))
        lifted = dot3(pair(lz_ref), damped, TURNED)
        lifted_ref[...] = dot3(split(lifted), lift_y)
        for g in range(3):
            rows = []
            for i in range(16):
                row = lifted_ref[128 * g + 8 * i : 128 * g + 8 * i + 8, :]
                rows.append(tiles_of(row) + [blank])
            for p, row in enumerate(turn_blocks(rows, 8)):
                for t, tile in enumerate(tiles_of(row)):
                    out_ref[pl.ds(p * 224 + k * 9 + g * 3 + t, 8, stride=28), :] = tile
    out_ref[pl.ds(27, 64, stride=28), :] = jnp.broadcast_to(part, (64, 128))


def coarse_x(place, got, potential):
    return pl.pallas_call(
        coarse_x_kernel,
        out_shape=jax.ShapeDtypeStruct((1792, 128), F32),
        compiler_params=LIMIT,
        in_specs=[SMEM] + [VMEM] * 5,
        out_specs=VMEM,
        scratch_shapes=[pltpu.VMEM((NF, 256), F32)],
    )(place, got, potential, jnp.asarray(HC2), jnp.asarray(LIFT_Z2), jnp.asarray(LIFT_Y2))


def fine_in_kernel(
    got_ref, lift_ref, matrix_hbm, evolved_hbm, out_ref, evolved_ref, matrix_ref, sems, saved
):
    copies = fetch_left(matrix_hbm, matrix_ref, sems)
    begin(copies)
    parts = got_ref[pl.ds(27, 64, stride=28), :]
    total = jnp.sum(parts, axis=0, keepdims=True)
    scale = lax.rsqrt(total / float(NC) ** 3 + EPSILON)
    scale = jnp.concatenate([scale] * 3, axis=1)
    finish(copies)

    def save(n):
        columns = pl.ds(pl.multiple_of(n * 384, 128), 384)
        source, target = evolved_ref.at[:, columns], evolved_hbm.at[:, columns]
        return pltpu.make_async_copy(source, target, saved.at[n])

    def body(n, carry):
        rows = []
        for k in range(3):
            tiles = [got_ref[pl.ds(k * 9 + 3 * n + t, 64, stride=28), :] for t in range(3)]
            rows.append(jnp.concatenate(tiles, axis=1))
        spectrum = split(jnp.concatenate(rows, axis=0))
        evolved = dot3(pair(lift_ref), spectrum) * scale
        evolved_ref[:, pl.ds(pl.multiple_of(n * 384, 128), 384)] = evolved
        turned = dot(matrix_ref[...], right3(evolved * evolved))
        for k in range(3):
            for t in range(3):
                piece = turned[128 * k : 128 * k + 128, 128 * t : 128 * t + 128]
                out_ref[pl.ds(k * 9 + 3 * n + t, 128, stride=27), :] = piece
        save(n).start()
        return carry

    lax.fori_loop(0, 3, body, 0)
    for n in range(3):
        save(n).wait()


def fine_in(got):
    return pl.pallas_call(
        fine_in_kernel,
        out_shape=[
            pltpu.HBM((NF, 1152), F32),
            jax.ShapeDtypeStruct((3456, 128), F32),
        ],
        compiler_params=LIMIT,
        in_specs=[VMEM, VMEM, HBM],
        out_specs=[HBM, VMEM],
        scratch_shapes=[
            pltpu.VMEM((NF, 1152), F32),
            pltpu.VMEM((NF, 1152), BF16),
            pltpu.SemaphoreType.DMA((3,)),
            pltpu.SemaphoreType.DMA((3,)),
        ],
    )(got, jnp.asarray(LIFT_X2), jnp.asarray(HF2))


def fine_slab_kernel(
    place_ref, got_ref, out_hbm, back_hbm, matrix_hbm, out_ref, plane_ref, out_m, back_m, matrix, sems
):
    out_copies = fetch_left(out_hbm, out_m, sems.at[0])
    back_copies = fetch_left(back_hbm, back_m, sems.at[1])
    copies = fetch_right(matrix_hbm, matrix, sems.at[2])
    begin(out_copies + copies + back_copies)
    wz = squares(lax.broadcasted_iota(jnp.int32, (NF, NF), 0), NF, 1.0)
    wy = squares(lax.broadcasted_iota(jnp.int32, (NF, NF), 1), NF, 1.0)

    def body(k, carry):
        def unpack(g, carry):
            base = k * 9 + g * 3
            rows = [
                [got_ref[pl.ds(r * 216 + base + t, 8, stride=27), :] for t in range(3)]
                for r in range(16)
            ]
            for i, row in enumerate(turn_blocks(rows, 16)):
                plane_ref[pl.ds(pl.multiple_of(g * 128 + 8 * i, 8), 8), :] = row
            return carry

        lax.fori_loop(0, 3, unpack, 0)

        @pl.when(k == 0)
        def _():
            finish(out_copies + copies + back_copies)

        mid = dot(out_m[...], right3(plane_ref[...]))
        mid = dot(left3(mid), matrix[...])
        kx = 128 * k + place_ref[4]
        wx = squares(jnp.full((1, 1), kx, jnp.int32), NF, 1.0)
        mid = mid * dipolar(wx, wy, wz, NF)
        mid = dot(left3(mid), matrix[...])
        plane_ref[...] = dot(back_m[...], right3(mid))

        def pack(g, carry):
            base = k * 9 + g * 3
            rows = []
            for i in range(16):
                rows.append(tiles_of(plane_ref[pl.ds(pl.multiple_of(g * 128 + 8 * i, 8), 8), :]))
            for r, row in enumerate(turn_blocks(rows, 16)):
                for t, tile in enumerate(tiles_of(row)):
                    out_ref[pl.ds(r * 216 + base + t, 8, stride=27), :] = tile
            return carry

        lax.fori_loop(0, 3, pack, 0)
        return carry

    lax.fori_loop(0, 3, body, 0)


def fine_slab(place, got):
    return pl.pallas_call(
        fine_slab_kernel,
        out_shape=jax.ShapeDtypeStruct((3456, 128), F32),
        compiler_params=LIMIT,
        in_specs=[SMEM, VMEM] + [HBM] * 3,
        out_specs=VMEM,
        scratch_shapes=[
            pltpu.VMEM((NF, NF), F32),
            pltpu.VMEM((NF, 1152), BF16),
            pltpu.VMEM((NF, 1152), BF16),
            pltpu.VMEM((1152, NF), BF16),
            pltpu.SemaphoreType.DMA((3, 3)),
        ],
    )(place, got, jnp.asarray(HF_OUT2), jnp.asarray(HF_BACK2), jnp.asarray(HF2))


def fine_out_kernel(got_ref, evolved_ref, potential_ref, matrix_ref, damped_ref, part_ref):
    part_ref[...] = jnp.zeros_like(part_ref)

    def body(n, carry):
        rows = []
        for k in range(3):
            tiles = [got_ref[pl.ds(k * 9 + 3 * n + t, 128, stride=27), :] for t in range(3)]
            rows.append(jnp.concatenate(tiles, axis=1))
        field = dot3(pair(matrix_ref), split(jnp.concatenate(rows, axis=0)))
        columns = pl.ds(pl.multiple_of(n * 384, 128), 384)
        evolved = evolved_ref[:, columns]
        potential = potential_ref[columns, :].T
        exponent = -TIME_STEP * (potential + CONTACT * evolved * evolved + field)
        damped = jnp.exp(exponent) * evolved
        part_ref[...] += jnp.sum(damped * damped)
        damped_ref[columns, :] = damped.T
        return carry

    lax.fori_loop(0, 3, body, 0)


def fine_out(got, evolved, potential):
    return pl.pallas_call(
        fine_out_kernel,
        out_shape=[
            jax.ShapeDtypeStruct((1152, NF), F32),
            jax.ShapeDtypeStruct((128, 128), F32),
        ],
        compiler_params=LIMIT,
        in_specs=[VMEM] * 4,
        out_specs=[VMEM] * 2,
    )(got, evolved, potential, jnp.asarray(HF2))


def scale_kernel(parts_ref, damped_ref, out_hbm, scaled_ref, sems):
    total = jnp.sum(parts_ref[...], axis=0, keepdims=True)
    scale = lax.rsqrt(total / float(NF) ** 3 + EPSILON)
    scale = jnp.concatenate([scale] * 3, axis=1)
    copies = []
    for i in range(4):
        rows = pl.ds(288 * i, 288)
        copies.append(pltpu.make_async_copy(scaled_ref.at[rows], out_hbm.at[rows], sems.at[i]))
        scaled_ref[rows, :] = damped_ref[rows, :] * scale
        if i:
            copies[i - 1].start()
    copies[3].start()
    finish(copies)


def scaled(parts, damped):
    return pl.pallas_call(
        scale_kernel,
        out_shape=jax.ShapeDtypeStruct((1152, NF), F32),
        compiler_params=LIMIT,
        in_specs=[VMEM] * 2,
        out_specs=HBM,
        scratch_shapes=[pltpu.VMEM((1152, NF), F32), pltpu.SemaphoreType.DMA((4,))],
    )(parts, damped)


def exchange(buffer, axes, count):
    flat = buffer.reshape(count, 1, -1)
    return lax.all_to_all(flat, axes, split_axis=0, concat_axis=0, tiled=False)


def swap_planes(potential, near):
    planes = potential.reshape(2, 2, 72, NC)
    mine = lax.dynamic_index_in_dim(planes, near, 1, keepdims=False)
    theirs = lax.dynamic_index_in_dim(planes, 1 - near, 1, keepdims=False)
    return jnp.stack([mine, lax.ppermute(theirs, "cols_1", [(0, 1), (1, 0)])], axis=1)


def spread_planes(planes, across):
    slots = []
    for i in range(4):
        chunk = lax.dynamic_index_in_dim(planes, (across + i) % 2, 0, keepdims=False)
        if i:
            moves = [(c * 4 + (y - i) % 4, c * 4 + y) for c in range(2) for y in (2 * c, 2 * c + 1)]
            chunk = lax.ppermute(chunk, (CORE, "cols_0"), moves)
        slots.append(chunk)
    return jnp.stack(slots)


def share_planes(slots, core, across):
    moves = [(y // 2 * 4 + y, (1 - y // 2) * 4 + y) for y in range(4)]
    other = lax.ppermute(slots, (CORE, "cols_0"), moves)
    return jnp.where(core == across // 2, slots, other).reshape(8, 72, NC)


def per_device(wave_coarse, potential_coarse, potential_fine):
    core = lax.axis_index(CORE)
    chip = lax.axis_index(CHIPS)
    device = lax.axis_index(ALL)
    across, near = lax.axis_index("cols_0"), lax.axis_index("cols_1")
    place = jnp.stack([core, across, near, chip, device])

    got = exchange(coarse_pencil(wave_coarse.reshape(288, NC)), ALL, 128).reshape(896, 128)
    got, planes = lax.optimization_barrier((got, swap_planes(potential_coarse, near)))
    got = exchange(coarse_z(got), CHIPS, 64).reshape(1728, 128)
    got, planes = lax.optimization_barrier((got, spread_planes(planes, across)))
    got = exchange(coarse_y(place, got), CHIPS, 64).reshape(1728, 128)
    turned = coarse_x(place, got, share_planes(planes, core, across))
    got = exchange(turned, CHIPS, 64).reshape(1792, 128)

    evolved, spectrum = fine_in(got)
    got = exchange(spectrum, ALL, 128).reshape(3456, 128)
    spectrum = fine_slab(place, got)
    got = exchange(spectrum, ALL, 128).reshape(3456, 128)
    damped, part = fine_out(got, evolved, potential_fine.reshape(1152, NF))
    parts = exchange(part, ALL, 128).reshape(128, 128)
    return scaled(parts, damped).reshape(48, 24, NF)


def solution(mesh):
    torus = Mesh(
        mesh.devices.reshape(4, 2, 2, 4, 2), ("rows_0", "rows_1", "rows_2", "cols_0", "cols_1")
    )
    return jax.shard_map(
        per_device,
        mesh=torus,
        in_specs=(P(ROWS, COLS, None), P(ROWS, COLS, None), P(COLS, ROWS, None)),
        out_specs=P(COLS, ROWS, None),
        check_vma=False,
    )
```

```python
import math

import jax
import jax.numpy as jnp
import numpy as np
from jax import lax
from jax.experimental import pallas as pl
from jax.experimental.pallas import tpu as pltpu
from jax.sharding import Mesh
from jax.sharding import PartitionSpec as P

NC = 192
NF = 384
ROWS = ("rows_0", "rows_1", "rows_2")
COLS = ("cols_0", "cols_1")
ALL = ROWS + COLS
CHIPS = ("rows_0", "rows_1", "cols_0", "cols_1")
CORE = "rows_2"

TIME_STEP = 0.5
CONTACT = 0.4
DIPOLE_STRENGTH = 0.3
EPSILON = 1e-06


def cas_table(rows, columns, length):
    phases = 2.0 * math.pi / length * ((np.outer(rows, columns)) % length)
    return np.cos(phases) + np.sin(phases)


def signed(length):
    k = np.arange(length)
    return np.where(k < length // 2, k, k - length)


def tables():
    k = np.arange(NC)
    wave = 2.0 * math.pi / NF * signed(NC)
    decay = np.exp(-0.5 * TIME_STEP * wave**2)
    hc = cas_table(k, k, NC)
    hf = cas_table(np.arange(NF), np.arange(NF), NF)
    evolve = hc @ (decay[:, None] * hc) / NC
    lifted = np.where(k < NC // 2, k, k + NC)
    lift = hf[:, lifted] @ (decay[:, None] * hc) / NC
    return [t.astype(np.float32) for t in (hc, hf, evolve, lift)]


HC, HF, EVOLVE, LIFT = tables()


def squares(index, length, spacing):
    s = jnp.where(index < length // 2, index, index - length).astype(jnp.float32)
    w = 2.0 * math.pi / (length * spacing) * s
    return w * w


def dipolar(wx, wy, wz, length):
    q = wx + wy + wz
    safe = jnp.where(q > 0, q, 1.0)
    return jnp.where(q > 0, DIPOLE_STRENGTH * (3.0 * wz - q) / safe, 0.0) / float(length) ** 3


F32 = jnp.float32
BF16 = jnp.bfloat16
VMEM = pl.BlockSpec(memory_space=pltpu.VMEM)
SMEM = pl.BlockSpec(memory_space=pltpu.SMEM)
HBM = pl.BlockSpec(memory_space=pltpu.HBM)
LIMIT = pltpu.CompilerParams(vmem_limit_bytes=20 * 1024 * 1024)


def halves(table):
    high = table.astype(BF16)
    return np.stack([high, (table - high.astype(np.float32)).astype(BF16)])


HF2 = halves(HF)
BY_SLAB = np.arange(NF).reshape(8, 48).T.reshape(-1)
HF_OUT2 = halves(HF[:, BY_SLAB])
HF_BACK2 = halves(HF[BY_SLAB, :])
PLANE = np.arange(NC).reshape(16, 12).T.reshape(-1)
LIFT_X2 = halves(LIFT[:, np.arange(NC).reshape(64, 3).T.reshape(-1)])
HC2 = halves(HC)
HC_WIDE2 = halves(np.pad(HC, ((0, 64), (0, 64))))
EVOLVE2 = halves(EVOLVE)
EVOLVE_Y2 = halves(np.pad(EVOLVE, ((0, 0), (0, 64))))
EVOLVE_X2 = halves(np.concatenate([EVOLVE[PLANE, :]] * 2, axis=1))
LIFT_Z2 = halves(LIFT[BY_SLAB, :])
LIFT_Y2 = np.stack(
    [
        halves(np.pad(LIFT.reshape(8, 2, 24, NC)[:, core].reshape(NC, NC).T, ((0, 0), (0, 64))))
        for core in range(2)
    ]
)
TURNED = (((1,), (1,)), ((), ()))
PLAIN = (((1,), (0,)), ((), ()))


def split(x):
    high = x.astype(BF16)
    return high, (x - high.astype(F32)).astype(BF16)


def dot3(a, b, dims=PLAIN):
    (ah, al), (bh, bl) = a, b

    def dot(p, q):
        return lax.dot_general(p, q, dims, preferred_element_type=F32)

    return dot(ah, bh) + (dot(al, bh) + dot(ah, bl))


def dot(a, b):
    return jnp.dot(a, b, preferred_element_type=F32)


def left3(x):
    high, low = split(x)
    return jnp.concatenate([high, low, high], axis=1)


def right3(x):
    high, low = split(x)
    return jnp.concatenate([high, high, low], axis=0)


def fetch_left(table, wide, sems):
    size = table.shape[2]
    return [
        pltpu.make_async_copy(table.at[part], wide.at[:, pl.ds(i * size, size)], sems.at[i])
        for i, part in enumerate((0, 1, 0))
    ]


def fetch_right(table, tall, sems):
    size = table.shape[1]
    return [
        pltpu.make_async_copy(table.at[part], tall.at[pl.ds(i * size, size), :], sems.at[i])
        for i, part in enumerate((0, 0, 1))
    ]


def begin(copies):
    for copy in copies:
        copy.start()


def finish(copies):
    for copy in copies:
        copy.wait()


def pair(ref):
    return ref[0], ref[1]


def tiles_of(row):
    return [row[:, 128 * t : 128 * t + 128] for t in range(row.shape[1] // 128)]


def shift_runs(row, lanes):
    lanes %= NF
    return pltpu.roll(row, lanes, 1) if lanes else row


def skew(rows, lead=0):
    return [tiles_of(shift_runs(row, 24 * a - lead)) for a, row in enumerate(rows)]


def diagonals(skewed, count):
    lane = lax.broadcasted_iota(jnp.int32, skewed[0][0].shape, 1)
    result = []
    for b in range(count):
        tiles = []
        for t in range(3):
            tile = None
            for p in range(128 * t // 24, (128 * t + 127) // 24 + 1):
                a = (p - b) % 16
                if a < len(skewed):
                    piece = skewed[a][t]
                    tile = piece if tile is None else jnp.where(lane < 24 * p - 128 * t, tile, piece)
            tiles.append(skewed[0][t] if tile is None else tile)
        result.append(jnp.concatenate(tiles, axis=1))
    return result


def in_hbm(x):
    return pltpu.with_memory_space_constraint(x, pltpu.HBM)


def coarse_pencil_kernel(wave_hbm, matrix_hbm, out_ref, wave_ref, matrix_ref, sems):
    copies = [
        pltpu.make_async_copy(wave_hbm, wave_ref, sems.at[0]),
        pltpu.make_async_copy(matrix_hbm, matrix_ref, sems.at[1]),
    ]
    begin(copies)
    finish(copies)
    high, low = split(wave_ref[...])
    pieces = []
    for k in range(3):
        lead = 32 * k

        def padded(x):
            parts = [jnp.zeros((lead, NC), BF16)] * (k > 0) + [x]
            return jnp.concatenate(parts + [jnp.zeros((96 - lead, NC), BF16)], axis=0)

        rows = slice(64 * k, 64 * k + 64)
        matrix = (matrix_ref[0, rows, :], matrix_ref[1, rows, :])
        pieces.append(tiles_of(dot3(matrix, (padded(high), padded(low)), TURNED)))
    (a0, a1, a2), (b0, b1, b2), (c0, c1, c2) = pieces
    for t, tile in enumerate([a0, a1, a2 + b0, b1, b2 + c0, c1, c2]):
        for p in range(8):
            for core in range(2):
                out_ref[pl.ds(p * 112 + core * 56 + t, 8, stride=7), :] = tile[8 * p : 8 * p + 8, :]


def coarse_pencil(wave):
    return pl.pallas_call(
        coarse_pencil_kernel,
        out_shape=jax.ShapeDtypeStruct((896, 128), F32),
        compiler_params=LIMIT,
        in_specs=[HBM] * 2,
        out_specs=VMEM,
        scratch_shapes=[
            pltpu.VMEM((288, NC), F32),
            pltpu.VMEM((2, NC, NC), BF16),
            pltpu.SemaphoreType.DMA((2,)),
        ],
    )(in_hbm(wave), in_hbm(jnp.asarray(EVOLVE2)))


def coarse_z_kernel(got_ref, ey_ref, ex_ref, matrix_ref, out_ref, plane_ref):
    lane = lax.broadcasted_iota(jnp.int32, (64, 128), 1)
    for k in range(3):
        for g in range(2):
            rows = []
            for c in range(8):
                tiles = [got_ref[pl.ds(g * 448 + c * 7 + 2 * k + t, 8, stride=56), :] for t in range(3)]
                rows.append(jnp.concatenate(tiles, axis=1))
            for i, row in enumerate(diagonals(skew(rows, 32 * k), 12)):
                row = shift_runs(row, -24 * i)
                plane_ref[16 * i + 8 * g : 16 * i + 8 * g + 8, :] = row[:, :256]
        half = dot3(pair(ey_ref), split(plane_ref[...]), TURNED)
        evolved = dot3(split(half), pair(ex_ref))
        density = evolved[:, :256] * evolved[:, :256]
        turned = dot3(pair(matrix_ref), split(density))
        for j in range(3):
            f = tiles_of(turned[64 * j : 64 * j + 64, :])
            e = tiles_of(evolved[64 * j : 64 * j + 64, :])
            for t, tile in enumerate([f[0], jnp.where(lane < 64, f[1], e[1]), e[2]]):
                out_ref[pl.ds(k * 9 + j * 3 + t, 64, stride=27), :] = tile


def coarse_z(got):
    return pl.pallas_call(
        coarse_z_kernel,
        out_shape=jax.ShapeDtypeStruct((1728, 128), F32),
        compiler_params=LIMIT,
        in_specs=[VMEM] * 4,
        out_specs=VMEM,
        scratch_shapes=[pltpu.VMEM((NC, 256), F32)],
    )(got, jnp.asarray(EVOLVE_Y2), jnp.asarray(EVOLVE_X2), jnp.asarray(HC2))


def rows_of_plane(got_ref, base):
    rows = []
    for j in range(3):
        tiles = [got_ref[pl.ds(base + 9 * j + t, 64, stride=27), :] for t in range(3)]
        rows.append(jnp.concatenate(tiles, axis=1))
    return jnp.concatenate(rows, axis=0)


def coarse_y_kernel(place_ref, got_ref, matrix_ref, wide_ref, out_ref):
    lane = lax.broadcasted_iota(jnp.int32, (NC, 128), 1)
    wx = squares(lax.broadcasted_iota(jnp.int32, (NC, 256), 0), NC, 2.0)
    wz = squares(lax.broadcasted_iota(jnp.int32, (NC, 256), 1), NC, 2.0)
    for k in range(3):
        both = rows_of_plane(got_ref, 3 * k)
        both = jnp.concatenate([both, jnp.zeros((64, 384), F32)], axis=0).T
        mid = dot3(pair(matrix_ref), split(both[:NC, :]))
        mid = dot3(split(mid), pair(wide_ref))
        wy = squares(jnp.full((1, 1), 64 * k + place_ref[3], jnp.int32), NC, 2.0)
        mid = mid * dipolar(wx, wy, wz, NC)
        mid = dot3(split(mid), pair(wide_ref))
        q = tiles_of(dot3(pair(matrix_ref), split(mid)))
        e = [pltpu.roll(tile, 64, 1) for tile in tiles_of(both[NC:, :])]
        pieces = [q[0], jnp.where(lane < 64, q[1], e[0]), jnp.where(lane < 64, e[0], e[1])]
        for t, tile in enumerate(pieces):
            out_ref[pl.ds(3 * k + t, NC, stride=9), :] = tile


def coarse_y(place, got):
    return pl.pallas_call(
        coarse_y_kernel,
        out_shape=jax.ShapeDtypeStruct((1728, 128), F32),
        compiler_params=LIMIT,
        in_specs=[SMEM] + [VMEM] * 3,
        out_specs=VMEM,
    )(place, got, jnp.asarray(HC2), jnp.asarray(HC_WIDE2))


def coarse_x_kernel(place_ref, got_ref, potential_ref, matrix_ref, lz_ref, ly_ref, out_ref, lifted_ref):
    lane = lax.broadcasted_iota(jnp.int32, (NC, 128), 1)
    core = place_ref[0]
    slots = []
    for c in range(8):
        slots.append(2 * lax.rem(place_ref[1] - c // 2 + 4, 4) + (place_ref[2] ^ (c % 2)))
    lift_y = (ly_ref[core, 0], ly_ref[core, 1])
    part = jnp.zeros((1, 1), F32)
    blank = jnp.zeros((8, 128), F32)
    for k in range(3):
        rows = []
        for j in range(3):
            tiles = [got_ref[pl.ds(9 * k + 3 * j + t, 64, stride=27), :] for t in range(3)]
            rows.append(jnp.concatenate(tiles, axis=1))
        both = jnp.concatenate(rows, axis=0)
        field = dot3(pair(matrix_ref), split(both[:, :256]))
        e1, e2 = [pltpu.roll(tile, 64, 1) for tile in tiles_of(both)[1:]]
        evolved = [jnp.where(lane < 64, e1, e2), e2[:, :64]]
        pieces = []
        for t, e in enumerate(evolved):
            lanes = slice(128 * t, 128 * t + e.shape[1])
            v = jnp.concatenate([potential_ref[c, 24 * k : 24 * k + 24, lanes] for c in slots], axis=0)
            d = jnp.exp(-TIME_STEP * (v + CONTACT * e * e + field[:, lanes])) * e
            part = part + jnp.sum(d * d, keepdims=True)
            pieces.append(d)
        damped = split(jnp.concatenate(pieces, axis=1))
        lifted = dot3(pair(lz_ref), damped, TURNED)
        lifted_ref[...] = dot3(split(lifted), lift_y)
        for g in range(3):
            rows = []
            for i in range(16):
                row = lifted_ref[128 * g + 8 * i : 128 * g + 8 * i + 8, :]
                rows.append(jnp.concatenate([row, blank], axis=1))
            for p, row in enumerate(diagonals(skew(rows), 8)):
                row = jnp.where(core == 0, shift_runs(row, 24 * p), shift_runs(row, 24 * p + 24))
                for t, tile in enumerate(tiles_of(row)):
                    out_ref[pl.ds(p * 224 + k * 9 + g * 3 + t, 8, stride=28), :] = tile
    out_ref[pl.ds(27, 64, stride=28), :] = jnp.broadcast_to(part, (64, 128))


def coarse_x(place, got, potential):
    return pl.pallas_call(
        coarse_x_kernel,
        out_shape=jax.ShapeDtypeStruct((1792, 128), F32),
        compiler_params=LIMIT,
        in_specs=[SMEM] + [VMEM] * 5,
        out_specs=VMEM,
        scratch_shapes=[pltpu.VMEM((NF, 256), F32)],
    )(place, got, potential, jnp.asarray(HC2), jnp.asarray(LIFT_Z2), jnp.asarray(LIFT_Y2))


def fine_in_kernel(
    got_ref, lift_ref, matrix_hbm, evolved_hbm, out_ref, evolved_ref, matrix_ref, sems, saved
):
    copies = fetch_left(matrix_hbm, matrix_ref, sems)
    begin(copies)
    parts = got_ref[pl.ds(27, 64, stride=28), :]
    total = jnp.sum(parts, axis=0, keepdims=True)
    scale = lax.rsqrt(total / float(NC) ** 3 + EPSILON)
    scale = jnp.concatenate([scale] * 3, axis=1)
    finish(copies)

    def save(n):
        columns = pl.ds(pl.multiple_of(n * 384, 128), 384)
        source, target = evolved_ref.at[:, columns], evolved_hbm.at[:, columns]
        return pltpu.make_async_copy(source, target, saved.at[n])

    def body(n, carry):
        rows = []
        for k in range(3):
            tiles = [got_ref[pl.ds(k * 9 + 3 * n + t, 64, stride=28), :] for t in range(3)]
            rows.append(jnp.concatenate(tiles, axis=1))
        spectrum = split(jnp.concatenate(rows, axis=0))
        evolved = dot3(pair(lift_ref), spectrum) * scale
        evolved_ref[:, pl.ds(pl.multiple_of(n * 384, 128), 384)] = evolved
        turned = dot(matrix_ref[...], right3(evolved * evolved))
        for k in range(3):
            for t in range(3):
                piece = turned[128 * k : 128 * k + 128, 128 * t : 128 * t + 128]
                out_ref[pl.ds(k * 9 + 3 * n + t, 128, stride=27), :] = piece
        save(n).start()
        return carry

    lax.fori_loop(0, 3, body, 0)
    for n in range(3):
        save(n).wait()


def fine_in(got):
    return pl.pallas_call(
        fine_in_kernel,
        out_shape=[
            pltpu.HBM((NF, 1152), F32),
            jax.ShapeDtypeStruct((3456, 128), F32),
        ],
        compiler_params=LIMIT,
        in_specs=[VMEM, VMEM, HBM],
        out_specs=[HBM, VMEM],
        scratch_shapes=[
            pltpu.VMEM((NF, 1152), F32),
            pltpu.VMEM((NF, 1152), BF16),
            pltpu.SemaphoreType.DMA((3,)),
            pltpu.SemaphoreType.DMA((3,)),
        ],
    )(got, jnp.asarray(LIFT_X2), jnp.asarray(HF2))


def fine_slab_kernel(
    place_ref, got_ref, out_hbm, back_hbm, matrix_hbm, out_ref, plane_ref, back_ref, out_m, back_m, matrix, sems
):
    out_copies = fetch_left(out_hbm, out_m, sems.at[0])
    back_copies = fetch_left(back_hbm, back_m, sems.at[1])
    copies = fetch_right(matrix_hbm, matrix, sems.at[2])
    begin(out_copies + copies + back_copies)
    wz = squares(lax.broadcasted_iota(jnp.int32, (NF, NF), 0), NF, 1.0)
    wy = squares(lax.broadcasted_iota(jnp.int32, (NF, NF), 1), NF, 1.0)


    def unpack(k):
        for g in range(3):
            base = k * 9 + g * 3
            skewed = [
                [got_ref[pl.ds(r * 216 + base + t, 8, stride=27), :] for t in range(3)]
                for r in range(16)
            ]
            for i, row in enumerate(diagonals(skewed, 16)):
                start = 128 * g + 8 * i
                plane_ref[start : start + 8, :] = shift_runs(row, -24 * i)

    def pack(k):
        for g in range(3):
            base = k * 9 + g * 3
            rows = [back_ref[128 * g + 8 * i : 128 * g + 8 * i + 8, :] for i in range(16)]
            for r, row in enumerate(diagonals(skew(rows), 16)):
                for t, tile in enumerate(tiles_of(row)):
                    out_ref[pl.ds(r * 216 + base + t, 8, stride=27), :] = tile

    def body(k, carry):
        mid = dot(out_m[...], right3(plane_ref[...]))
        pack(jnp.maximum(k - 1, 0))
        unpack(jnp.minimum(k + 1, 2))
        mid = dot(left3(mid), matrix[...])
        kx = 128 * k + place_ref[4]
        wx = squares(jnp.full((1, 1), kx, jnp.int32), NF, 1.0)
        mid = mid * dipolar(wx, wy, wz, NF)
        mid = dot(left3(mid), matrix[...])
        back_ref[...] = dot(back_m[...], right3(mid))
        return carry

    back_ref[...] = jnp.zeros_like(back_ref)
    unpack(0)
    finish(out_copies + copies + back_copies)
    lax.fori_loop(0, 3, body, 0)
    pack(2)


def fine_slab(place, got):
    return pl.pallas_call(
        fine_slab_kernel,
        out_shape=jax.ShapeDtypeStruct((3456, 128), F32),
        compiler_params=LIMIT,
        in_specs=[SMEM, VMEM] + [HBM] * 3,
        out_specs=VMEM,
        scratch_shapes=[
            pltpu.VMEM((NF, NF), F32),
            pltpu.VMEM((NF, NF), F32),
            pltpu.VMEM((NF, 1152), BF16),
            pltpu.VMEM((NF, 1152), BF16),
            pltpu.VMEM((1152, NF), BF16),
            pltpu.SemaphoreType.DMA((3, 3)),
        ],
    )(place, got, jnp.asarray(HF_OUT2), jnp.asarray(HF_BACK2), jnp.asarray(HF2))


def fine_out_kernel(place_ref, got_ref, evolved_ref, potential_ref, matrix_ref, damped_ref, part_ref):
    part_ref[...] = jnp.zeros_like(part_ref)
    row = place_ref[5]

    def block(n, p):
        return pl.ds(pl.multiple_of(384 * n + 24 * lax.rem(p + 16 - row, 16), 8), 24)

    def body(n, carry):
        rows = []
        for k in range(3):
            tiles = [got_ref[pl.ds(k * 9 + 3 * n + t, 128, stride=27), :] for t in range(3)]
            rows.append(jnp.concatenate(tiles, axis=1))
        field = dot3(pair(matrix_ref), split(jnp.concatenate(rows, axis=0)))
        columns = pl.ds(pl.multiple_of(n * 384, 128), 384)
        evolved = evolved_ref[:, columns]
        potential = jnp.concatenate([potential_ref[block(n, p), :] for p in range(16)], axis=0).T
        exponent = -TIME_STEP * (potential + CONTACT * evolved * evolved + field)
        damped = jnp.exp(exponent) * evolved
        part_ref[...] += jnp.sum(damped * damped)
        turned = damped.T
        for p in range(16):
            damped_ref[block(n, p), :] = turned[24 * p : 24 * p + 24, :]
        return carry

    lax.fori_loop(0, 3, body, 0)


def fine_out(place, got, evolved, potential):
    return pl.pallas_call(
        fine_out_kernel,
        out_shape=[
            jax.ShapeDtypeStruct((1152, NF), F32),
            jax.ShapeDtypeStruct((128, 128), F32),
        ],
        compiler_params=LIMIT,
        in_specs=[SMEM] + [VMEM] * 4,
        out_specs=[VMEM] * 2,
    )(place, got, evolved, potential, jnp.asarray(HF2))


def scale_kernel(parts_ref, damped_ref, out_hbm, scaled_ref, sems):
    total = jnp.sum(parts_ref[...], axis=0, keepdims=True)
    scale = lax.rsqrt(total / float(NF) ** 3 + EPSILON)
    scale = jnp.concatenate([scale] * 3, axis=1)
    copies = []
    for i in range(4):
        rows = pl.ds(288 * i, 288)
        copies.append(pltpu.make_async_copy(scaled_ref.at[rows], out_hbm.at[rows], sems.at[i]))
        scaled_ref[rows, :] = damped_ref[rows, :] * scale
        if i:
            copies[i - 1].start()
    copies[3].start()
    finish(copies)


def scaled(parts, damped):
    return pl.pallas_call(
        scale_kernel,
        out_shape=jax.ShapeDtypeStruct((1152, NF), F32),
        compiler_params=LIMIT,
        in_specs=[VMEM] * 2,
        out_specs=HBM,
        scratch_shapes=[pltpu.VMEM((1152, NF), F32), pltpu.SemaphoreType.DMA((4,))],
    )(parts, damped)


def exchange(buffer, axes, count):
    flat = buffer.reshape(count, 1, -1)
    return lax.all_to_all(flat, axes, split_axis=0, concat_axis=0, tiled=False)


def swap_planes(potential, near):
    planes = potential.reshape(2, 2, 72, NC)
    mine = lax.dynamic_index_in_dim(planes, near, 1, keepdims=False)
    theirs = lax.dynamic_index_in_dim(planes, 1 - near, 1, keepdims=False)
    return jnp.stack([mine, lax.ppermute(theirs, "cols_1", [(0, 1), (1, 0)])], axis=1)


def spread_planes(planes, across):
    slots = []
    for i in range(4):
        chunk = lax.dynamic_index_in_dim(planes, (across + i) % 2, 0, keepdims=False)
        if i:
            moves = [(c * 4 + (y - i) % 4, c * 4 + y) for c in range(2) for y in (2 * c, 2 * c + 1)]
            chunk = lax.ppermute(chunk, (CORE, "cols_0"), moves)
        slots.append(chunk)
    return jnp.stack(slots)


def share_planes(slots, core, across):
    moves = [(y // 2 * 4 + y, (1 - y // 2) * 4 + y) for y in range(4)]
    other = lax.ppermute(slots, (CORE, "cols_0"), moves)
    return jnp.where(core == across // 2, slots, other).reshape(8, 72, NC)


def per_device(wave_coarse, potential_coarse, potential_fine):
    core = lax.axis_index(CORE)
    chip = lax.axis_index(CHIPS)
    device = lax.axis_index(ALL)
    across, near = lax.axis_index("cols_0"), lax.axis_index("cols_1")
    place = jnp.stack([core, across, near, chip, device, lax.axis_index(ROWS)])

    got = exchange(coarse_pencil(wave_coarse.reshape(288, NC)), ALL, 128).reshape(896, 128)
    got, planes = lax.optimization_barrier((got, swap_planes(potential_coarse, near)))
    got = exchange(coarse_z(got), CHIPS, 64).reshape(1728, 128)
    got, planes = lax.optimization_barrier((got, spread_planes(planes, across)))
    got = exchange(coarse_y(place, got), CHIPS, 64).reshape(1728, 128)
    turned = coarse_x(place, got, share_planes(planes, core, across))
    got = exchange(turned, CHIPS, 64).reshape(1792, 128)

    evolved, spectrum = fine_in(got)
    got = exchange(spectrum, ALL, 128).reshape(3456, 128)
    spectrum = fine_slab(place, got)
    got = exchange(spectrum, ALL, 128).reshape(3456, 128)
    damped, part = fine_out(place, got, evolved, potential_fine.reshape(1152, NF))
    parts = exchange(part, ALL, 128).reshape(128, 128)
    return scaled(parts, damped).reshape(48, 24, NF)


def solution(mesh):
    torus = Mesh(
        mesh.devices.reshape(4, 2, 2, 4, 2), ("rows_0", "rows_1", "rows_2", "cols_0", "cols_1")
    )
    return jax.shard_map(
        per_device,
        mesh=torus,
        in_specs=(P(ROWS, COLS, None), P(ROWS, COLS, None), P(COLS, ROWS, None)),
        out_specs=P(COLS, ROWS, None),
        check_vma=False,
    )
```

```python
import math

import jax
import jax.numpy as jnp
import numpy as np
from jax import lax
from jax.experimental import pallas as pl
from jax.experimental.pallas import tpu as pltpu
from jax.sharding import Mesh
from jax.sharding import PartitionSpec as P

NC = 192
NF = 384
ROWS = ("rows_0", "rows_1", "rows_2")
COLS = ("cols_0", "cols_1")
ALL = ROWS + COLS
CHIPS = ("rows_0", "rows_1", "cols_0", "cols_1")
CORE = "rows_2"

TIME_STEP = 0.5
CONTACT = 0.4
DIPOLE_STRENGTH = 0.3
EPSILON = 1e-06


def cas_table(rows, columns, length):
    phases = 2.0 * math.pi / length * ((np.outer(rows, columns)) % length)
    return np.cos(phases) + np.sin(phases)


def signed(length):
    k = np.arange(length)
    return np.where(k < length // 2, k, k - length)


def tables():
    k = np.arange(NC)
    wave = 2.0 * math.pi / NF * signed(NC)
    decay = np.exp(-0.5 * TIME_STEP * wave**2)
    hc = cas_table(k, k, NC)
    hf = cas_table(np.arange(NF), np.arange(NF), NF)
    evolve = hc @ (decay[:, None] * hc) / NC
    lifted = np.where(k < NC // 2, k, k + NC)
    lift = hf[:, lifted] @ (decay[:, None] * hc) / NC
    return [t.astype(np.float32) for t in (hc, hf, evolve, lift)]


HC, HF, EVOLVE, LIFT = tables()


def squares(index, length, spacing):
    s = jnp.where(index < length // 2, index, index - length).astype(jnp.float32)
    w = 2.0 * math.pi / (length * spacing) * s
    return w * w


def dipolar(wx, wy, wz, length):
    q = wx + wy + wz
    safe = jnp.where(q > 0, q, 1.0)
    return jnp.where(q > 0, DIPOLE_STRENGTH * (3.0 * wz - q) / safe, 0.0) / float(length) ** 3


F32 = jnp.float32
BF16 = jnp.bfloat16
VMEM = pl.BlockSpec(memory_space=pltpu.VMEM)
SMEM = pl.BlockSpec(memory_space=pltpu.SMEM)
HBM = pl.BlockSpec(memory_space=pltpu.HBM)
LIMIT = pltpu.CompilerParams(vmem_limit_bytes=20 * 1024 * 1024)


def halves(table):
    high = table.astype(BF16)
    return np.stack([high, (table - high.astype(np.float32)).astype(BF16)])


HF2 = halves(HF)
BY_SLAB = np.arange(NF).reshape(8, 48).T.reshape(-1)
HF_OUT2 = halves(HF[:, BY_SLAB])
HF_BACK2 = halves(HF[BY_SLAB, :])
PLANE = np.arange(NC).reshape(16, 12).T.reshape(-1)
LIFT_X2 = halves(LIFT[:, np.arange(NC).reshape(64, 3).T.reshape(-1)])
HC2 = halves(HC)
HC_WIDE2 = halves(np.pad(HC, ((0, 64), (0, 64))))
EVOLVE2 = halves(EVOLVE)
EVOLVE_Y2 = halves(np.pad(EVOLVE, ((0, 0), (0, 64))))
EVOLVE_X2 = halves(np.pad(EVOLVE[PLANE, :], ((0, 0), (0, 64))))
LIFT_Z2 = halves(LIFT[BY_SLAB, :])
LIFT_Y2 = np.stack(
    [
        halves(np.pad(LIFT.reshape(8, 2, 24, NC)[:, core].reshape(NC, NC).T, ((0, 0), (0, 64))))
        for core in range(2)
    ]
)
TURNED = (((1,), (1,)), ((), ()))
PLAIN = (((1,), (0,)), ((), ()))


def split(x):
    high = x.astype(BF16)
    return high, (x - high.astype(F32)).astype(BF16)


def dot3(a, b, dims=PLAIN):
    (ah, al), (bh, bl) = a, b

    def dot(p, q):
        return lax.dot_general(p, q, dims, preferred_element_type=F32)

    return dot(ah, bh) + (dot(al, bh) + dot(ah, bl))


def dot(a, b):
    return jnp.dot(a, b, preferred_element_type=F32)


def left3(x):
    high, low = split(x)
    return jnp.concatenate([high, low, high], axis=1)


def right3(x):
    high, low = split(x)
    return jnp.concatenate([high, high, low], axis=0)


def fetch_left(table, wide, sems):
    size = table.shape[2]
    return [
        pltpu.make_async_copy(table.at[part], wide.at[:, pl.ds(i * size, size)], sems.at[i])
        for i, part in enumerate((0, 1, 0))
    ]


def fetch_right(table, tall, sems):
    size = table.shape[1]
    return [
        pltpu.make_async_copy(table.at[part], tall.at[pl.ds(i * size, size), :], sems.at[i])
        for i, part in enumerate((0, 0, 1))
    ]


def begin(copies):
    for copy in copies:
        copy.start()


def finish(copies):
    for copy in copies:
        copy.wait()


def pair(ref):
    return ref[0], ref[1]


def tiles_of(row):
    return [row[:, 128 * t : 128 * t + 128] for t in range(row.shape[1] // 128)]


def shift_runs(row, lanes):
    lanes %= NF
    return pltpu.roll(row, lanes, 1) if lanes else row


def skew(rows, lead=0):
    return [tiles_of(shift_runs(row, 24 * a - lead)) for a, row in enumerate(rows)]


def diagonals(skewed, count):
    lane = lax.broadcasted_iota(jnp.int32, skewed[0][0].shape, 1)
    result = []
    for b in range(count):
        tiles = []
        for t in range(3):
            tile = None
            for p in range(128 * t // 24, (128 * t + 127) // 24 + 1):
                a = (p - b) % 16
                if a < len(skewed):
                    piece = skewed[a][t]
                    tile = piece if tile is None else jnp.where(lane < 24 * p - 128 * t, tile, piece)
            tiles.append(skewed[0][t] if tile is None else tile)
        result.append(jnp.concatenate(tiles, axis=1))
    return result


def in_hbm(x):
    return pltpu.with_memory_space_constraint(x, pltpu.HBM)


def coarse_pencil_kernel(wave_hbm, matrix_hbm, out_ref, wave_ref, matrix_ref, sems):
    copies = [
        pltpu.make_async_copy(wave_hbm, wave_ref, sems.at[0]),
        pltpu.make_async_copy(matrix_hbm, matrix_ref, sems.at[1]),
    ]
    begin(copies)
    finish(copies)
    high, low = split(wave_ref[...])
    pieces = []
    for k in range(3):
        lead = 32 * k

        def padded(x):
            parts = [jnp.zeros((lead, NC), BF16)] * (k > 0) + [x]
            return jnp.concatenate(parts + [jnp.zeros((96 - lead, NC), BF16)], axis=0)

        rows = slice(64 * k, 64 * k + 64)
        matrix = (matrix_ref[0, rows, :], matrix_ref[1, rows, :])
        pieces.append(tiles_of(dot3(matrix, (padded(high), padded(low)), TURNED)))
    (a0, a1, a2), (b0, b1, b2), (c0, c1, c2) = pieces
    for t, tile in enumerate([a0, a1, a2 + b0, b1, b2 + c0, c1, c2]):
        for p in range(8):
            for core in range(2):
                out_ref[pl.ds(p * 112 + core * 56 + t, 8, stride=7), :] = tile[8 * p : 8 * p + 8, :]


def coarse_pencil(wave):
    return pl.pallas_call(
        coarse_pencil_kernel,
        out_shape=jax.ShapeDtypeStruct((896, 128), F32),
        compiler_params=LIMIT,
        in_specs=[HBM] * 2,
        out_specs=VMEM,
        scratch_shapes=[
            pltpu.VMEM((288, NC), F32),
            pltpu.VMEM((2, NC, NC), BF16),
            pltpu.SemaphoreType.DMA((2,)),
        ],
    )(in_hbm(wave), in_hbm(jnp.asarray(EVOLVE2)))


def pack_rows(planes):
    (a0, a1), (b0, b1), (c0, c1) = [tiles_of(plane) for plane in planes]
    low = lax.broadcasted_iota(jnp.int32, a0.shape, 1) < 64
    b0, b1 = pltpu.roll(b0, 64, 1), pltpu.roll(b1, 64, 1)
    return [a0, jnp.where(low, a1, b0), jnp.where(low, b0, b1), c0, c1]


def unpack_rows(tiles):
    a0, mixed, b1, c0, c1 = tiles
    low = lax.broadcasted_iota(jnp.int32, a0.shape, 1) < 64
    b1 = pltpu.roll(b1, 64, 1)
    b0 = jnp.where(low, pltpu.roll(mixed, 64, 1), b1)
    return [jnp.concatenate(p, axis=1) for p in ((a0, mixed), (b0, b1), (c0, c1))]


def coarse_z_kernel(place_ref, got_ref, ey_ref, ex_ref, matrix_ref, out_ref, plane_ref):
    core = place_ref[0]
    for k in range(3):
        for g in range(2):
            rows = []
            for c in range(8):
                tiles = [got_ref[pl.ds(g * 448 + c * 7 + 2 * k + t, 8, stride=56), :] for t in range(3)]
                rows.append(jnp.concatenate(tiles, axis=1))
            for i, row in enumerate(diagonals(skew(rows, 32 * k), 12)):
                row = shift_runs(row, -24 * i)
                plane_ref[16 * i + 8 * g : 16 * i + 8 * g + 8, :] = row[:, :256]
        half = dot3(pair(ey_ref), split(plane_ref[...]), TURNED)
        evolved = dot3(split(half), pair(ex_ref))
        turned = dot3(pair(matrix_ref), split(evolved * evolved))
        mine = jnp.where(core == 0, turned, evolved)
        for i, tile in enumerate(pack_rows([mine[64 * j : 64 * j + 64, :] for j in range(3)])):
            out_ref[pl.ds(k * 5 + i, 64, stride=15), :] = tile


def coarse_z(place, got):
    return pl.pallas_call(
        coarse_z_kernel,
        out_shape=jax.ShapeDtypeStruct((960, 128), F32),
        compiler_params=LIMIT,
        in_specs=[SMEM] + [VMEM] * 4,
        out_specs=VMEM,
        scratch_shapes=[pltpu.VMEM((NC, 256), F32)],
    )(place, got, jnp.asarray(EVOLVE_Y2), jnp.asarray(EVOLVE_X2), jnp.asarray(HC2))


def coarse_y_kernel(place_ref, got_ref, matrix_ref, wide_ref, out_ref):
    core = place_ref[0]
    wx = squares(lax.broadcasted_iota(jnp.int32, (NC, 256), 0), NC, 2.0)
    wz = squares(lax.broadcasted_iota(jnp.int32, (NC, 256), 1), NC, 2.0)
    parts = []
    for j in range(3):
        parts.append(unpack_rows([got_ref[pl.ds(5 * j + i, 64, stride=15), :] for i in range(5)]))
    planes = []
    for k in range(3):
        both = jnp.concatenate([part[k] for part in parts] + [jnp.zeros((64, 256), F32)], axis=0)
        both = both.T[:NC, :]
        mid = dot3(pair(matrix_ref), split(both))
        mid = dot3(split(mid), pair(wide_ref))
        wy = squares(jnp.full((1, 1), 64 * k + place_ref[3], jnp.int32), NC, 2.0)
        mid = mid * dipolar(wx, wy, wz, NC)
        mid = dot3(split(mid), pair(wide_ref))
        mid = dot3(pair(matrix_ref), split(mid))
        planes.append(jnp.where(core == 0, mid, both))
    for i, tile in enumerate(pack_rows(planes)):
        out_ref[pl.ds(i, NC, stride=5), :] = tile


def coarse_y(place, got):
    return pl.pallas_call(
        coarse_y_kernel,
        out_shape=jax.ShapeDtypeStruct((960, 128), F32),
        compiler_params=LIMIT,
        in_specs=[SMEM] + [VMEM] * 3,
        out_specs=VMEM,
    )(place, got, jnp.asarray(HC2), jnp.asarray(HC_WIDE2))


def coarse_x_kernel(place_ref, got_ref, other_ref, potential_ref, matrix_ref, lz_ref, ly_ref, out_ref, lifted_ref):
    core = place_ref[0]
    slots = []
    for c in range(8):
        slots.append(2 * lax.rem(place_ref[1] - c // 2 + 4, 4) + (place_ref[2] ^ (c % 2)))
    lift_y = (ly_ref[core, 0], ly_ref[core, 1])
    part = jnp.zeros((1, 1), F32)
    blank = jnp.zeros((8, 128), F32)
    for k in range(3):
        fields, waves = [], []
        for i in range(5):
            rows = pl.ds(5 * k + i, 64, stride=15)
            mine, other = got_ref[rows, :], other_ref[rows, :]
            fields.append(jnp.where(core == 0, mine, other))
            waves.append(jnp.where(core == 0, other, mine))
        field = dot3(pair(matrix_ref), split(jnp.concatenate(unpack_rows(fields), axis=0)))
        wave = jnp.concatenate(unpack_rows(waves), axis=0)
        evolved = [wave[:, :128], wave[:, 128:NC]]
        pieces = []
        for t, e in enumerate(evolved):
            lanes = slice(128 * t, 128 * t + e.shape[1])
            v = jnp.concatenate([potential_ref[c, 24 * k : 24 * k + 24, lanes] for c in slots], axis=0)
            d = jnp.exp(-TIME_STEP * (v + CONTACT * e * e + field[:, lanes])) * e
            part = part + jnp.sum(d * d, keepdims=True)
            pieces.append(d)
        damped = split(jnp.concatenate(pieces, axis=1))
        lifted = dot3(pair(lz_ref), damped, TURNED)
        lifted_ref[...] = dot3(split(lifted), lift_y)
        for g in range(3):
            rows = []
            for i in range(16):
                row = lifted_ref[128 * g + 8 * i : 128 * g + 8 * i + 8, :]
                rows.append(jnp.concatenate([row, blank], axis=1))
            for p, row in enumerate(diagonals(skew(rows), 8)):
                row = jnp.where(core == 0, shift_runs(row, 24 * p), shift_runs(row, 24 * p + 24))
                for t, tile in enumerate(tiles_of(row)):
                    out_ref[pl.ds(p * 224 + k * 9 + g * 3 + t, 8, stride=28), :] = tile
    out_ref[pl.ds(27, 64, stride=28), :] = jnp.broadcast_to(part, (64, 128))


def coarse_x(place, got, other, potential):
    return pl.pallas_call(
        coarse_x_kernel,
        out_shape=jax.ShapeDtypeStruct((1792, 128), F32),
        compiler_params=LIMIT,
        in_specs=[SMEM] + [VMEM] * 6,
        out_specs=VMEM,
        scratch_shapes=[pltpu.VMEM((NF, 256), F32)],
    )(place, got, other, potential, jnp.asarray(HC2), jnp.asarray(LIFT_Z2), jnp.asarray(LIFT_Y2))


def fine_in_kernel(
    got_ref, lift_ref, matrix_hbm, evolved_hbm, out_ref, evolved_ref, matrix_ref, sems, saved
):
    copies = fetch_left(matrix_hbm, matrix_ref, sems)
    begin(copies)
    parts = got_ref[pl.ds(27, 64, stride=28), :]
    total = jnp.sum(parts, axis=0, keepdims=True)
    scale = lax.rsqrt(total / float(NC) ** 3 + EPSILON)
    scale = jnp.concatenate([scale] * 3, axis=1)
    finish(copies)

    def save(n):
        columns = pl.ds(pl.multiple_of(n * 384, 128), 384)
        source, target = evolved_ref.at[:, columns], evolved_hbm.at[:, columns]
        return pltpu.make_async_copy(source, target, saved.at[n])

    def body(n, carry):
        rows = []
        for k in range(3):
            tiles = [got_ref[pl.ds(k * 9 + 3 * n + t, 64, stride=28), :] for t in range(3)]
            rows.append(jnp.concatenate(tiles, axis=1))
        spectrum = split(jnp.concatenate(rows, axis=0))
        evolved = dot3(pair(lift_ref), spectrum) * scale
        evolved_ref[:, pl.ds(pl.multiple_of(n * 384, 128), 384)] = evolved
        turned = dot(matrix_ref[...], right3(evolved * evolved))
        for k in range(3):
            for t in range(3):
                piece = turned[128 * k : 128 * k + 128, 128 * t : 128 * t + 128]
                out_ref[pl.ds(k * 9 + 3 * n + t, 128, stride=27), :] = piece
        save(n).start()
        return carry

    lax.fori_loop(0, 3, body, 0)
    for n in range(3):
        save(n).wait()


def fine_in(got):
    return pl.pallas_call(
        fine_in_kernel,
        out_shape=[
            pltpu.HBM((NF, 1152), F32),
            jax.ShapeDtypeStruct((3456, 128), F32),
        ],
        compiler_params=LIMIT,
        in_specs=[VMEM, VMEM, HBM],
        out_specs=[HBM, VMEM],
        scratch_shapes=[
            pltpu.VMEM((NF, 1152), F32),
            pltpu.VMEM((NF, 1152), BF16),
            pltpu.SemaphoreType.DMA((3,)),
            pltpu.SemaphoreType.DMA((3,)),
        ],
    )(got, jnp.asarray(LIFT_X2), jnp.asarray(HF2))


def fine_slab_kernel(
    place_ref, got_ref, out_hbm, back_hbm, matrix_hbm, out_ref, plane_ref, back_ref, out_m, back_m, matrix, sems
):
    out_copies = fetch_left(out_hbm, out_m, sems.at[0])
    back_copies = fetch_left(back_hbm, back_m, sems.at[1])
    copies = fetch_right(matrix_hbm, matrix, sems.at[2])
    begin(out_copies + copies + back_copies)
    wz = squares(lax.broadcasted_iota(jnp.int32, (NF, NF), 0), NF, 1.0)
    wy = squares(lax.broadcasted_iota(jnp.int32, (NF, NF), 1), NF, 1.0)


    def unpack(k):
        for g in range(3):
            base = k * 9 + g * 3
            skewed = [
                [got_ref[pl.ds(r * 216 + base + t, 8, stride=27), :] for t in range(3)]
                for r in range(16)
            ]
            for i, row in enumerate(diagonals(skewed, 16)):
                start = 128 * g + 8 * i
                plane_ref[start : start + 8, :] = shift_runs(row, -24 * i)

    def pack(k):
        for g in range(3):
            base = k * 9 + g * 3
            rows = [back_ref[128 * g + 8 * i : 128 * g + 8 * i + 8, :] for i in range(16)]
            for r, row in enumerate(diagonals(skew(rows), 16)):
                for t, tile in enumerate(tiles_of(row)):
                    out_ref[pl.ds(r * 216 + base + t, 8, stride=27), :] = tile

    def body(k, carry):
        mid = dot(out_m[...], right3(plane_ref[...]))
        pack(jnp.maximum(k - 1, 0))
        unpack(jnp.minimum(k + 1, 2))
        mid = dot(left3(mid), matrix[...])
        kx = 128 * k + place_ref[4]
        wx = squares(jnp.full((1, 1), kx, jnp.int32), NF, 1.0)
        mid = mid * dipolar(wx, wy, wz, NF)
        mid = dot(left3(mid), matrix[...])
        back_ref[...] = dot(back_m[...], right3(mid))
        return carry

    back_ref[...] = jnp.zeros_like(back_ref)
    unpack(0)
    finish(out_copies + copies + back_copies)
    lax.fori_loop(0, 3, body, 0)
    pack(2)


def fine_slab(place, got):
    return pl.pallas_call(
        fine_slab_kernel,
        out_shape=jax.ShapeDtypeStruct((3456, 128), F32),
        compiler_params=LIMIT,
        in_specs=[SMEM, VMEM] + [HBM] * 3,
        out_specs=VMEM,
        scratch_shapes=[
            pltpu.VMEM((NF, NF), F32),
            pltpu.VMEM((NF, NF), F32),
            pltpu.VMEM((NF, 1152), BF16),
            pltpu.VMEM((NF, 1152), BF16),
            pltpu.VMEM((1152, NF), BF16),
            pltpu.SemaphoreType.DMA((3, 3)),
        ],
    )(place, got, jnp.asarray(HF_OUT2), jnp.asarray(HF_BACK2), jnp.asarray(HF2))


def fine_out_kernel(place_ref, got_ref, evolved_ref, potential_ref, matrix_ref, damped_ref, part_ref):
    part_ref[...] = jnp.zeros_like(part_ref)
    row = place_ref[5]

    def block(n, p):
        return pl.ds(pl.multiple_of(384 * n + 24 * lax.rem(p + 16 - row, 16), 8), 24)

    def body(n, carry):
        rows = []
        for k in range(3):
            tiles = [got_ref[pl.ds(k * 9 + 3 * n + t, 128, stride=27), :] for t in range(3)]
            rows.append(jnp.concatenate(tiles, axis=1))
        field = dot3(pair(matrix_ref), split(jnp.concatenate(rows, axis=0)))
        columns = pl.ds(n * 384, 384)
        evolved = evolved_ref[:, columns]
        potential = jnp.concatenate([potential_ref[block(n, p), :] for p in range(16)], axis=0).T
        exponent = -TIME_STEP * (potential + CONTACT * evolved * evolved + field)
        damped = jnp.exp(exponent) * evolved
        part_ref[...] += jnp.sum(damped * damped)
        turned = damped.T
        for p in range(16):
            damped_ref[block(n, p), :] = turned[24 * p : 24 * p + 24, :]
        return carry

    for n in range(3):
        body(n, 0)


def fine_out(place, got, evolved, potential):
    return pl.pallas_call(
        fine_out_kernel,
        out_shape=[
            jax.ShapeDtypeStruct((1152, NF), F32),
            jax.ShapeDtypeStruct((128, 128), F32),
        ],
        compiler_params=LIMIT,
        in_specs=[SMEM] + [VMEM] * 4,
        out_specs=[VMEM] * 2,
    )(place, got, evolved, potential, jnp.asarray(HF2))


def scale_kernel(parts_ref, damped_ref, out_hbm, scaled_ref, sems):
    total = jnp.sum(parts_ref[...], axis=0, keepdims=True)
    scale = lax.rsqrt(total / float(NF) ** 3 + EPSILON)
    scale = jnp.concatenate([scale] * 3, axis=1)
    copies = []
    for i in range(4):
        rows = pl.ds(288 * i, 288)
        copies.append(pltpu.make_async_copy(scaled_ref.at[rows], out_hbm.at[rows], sems.at[i]))
        scaled_ref[rows, :] = damped_ref[rows, :] * scale
        if i:
            copies[i - 1].start()
    copies[3].start()
    finish(copies)


def scaled(parts, damped):
    return pl.pallas_call(
        scale_kernel,
        out_shape=jax.ShapeDtypeStruct((1152, NF), F32),
        compiler_params=LIMIT,
        in_specs=[VMEM] * 2,
        out_specs=HBM,
        scratch_shapes=[pltpu.VMEM((1152, NF), F32), pltpu.SemaphoreType.DMA((4,))],
    )(parts, damped)


def exchange(buffer, axes, count):
    flat = buffer.reshape(count, 1, -1)
    return lax.all_to_all(flat, axes, split_axis=0, concat_axis=0, tiled=False)


def swap_planes(potential, near):
    planes = potential.reshape(2, 2, 72, NC)
    mine = lax.dynamic_index_in_dim(planes, near, 1, keepdims=False)
    theirs = lax.dynamic_index_in_dim(planes, 1 - near, 1, keepdims=False)
    return jnp.stack([mine, lax.ppermute(theirs, "cols_1", [(0, 1), (1, 0)])], axis=1)


def spread_planes(planes, across):
    slots = []
    for i in range(4):
        chunk = lax.dynamic_index_in_dim(planes, (across + i) % 2, 0, keepdims=False)
        if i:
            moves = [(c * 4 + (y - i) % 4, c * 4 + y) for c in range(2) for y in (2 * c, 2 * c + 1)]
            chunk = lax.ppermute(chunk, (CORE, "cols_0"), moves)
        slots.append(chunk)
    return jnp.stack(slots)


def share_planes(slots, core, across):
    moves = [(y // 2 * 4 + y, (1 - y // 2) * 4 + y) for y in range(4)]
    other = lax.ppermute(slots, (CORE, "cols_0"), moves)
    return jnp.where(core == across // 2, slots, other).reshape(8, 72, NC)


def per_device(wave_coarse, potential_coarse, potential_fine):
    core = lax.axis_index(CORE)
    chip = lax.axis_index(CHIPS)
    device = lax.axis_index(ALL)
    across, near = lax.axis_index("cols_0"), lax.axis_index("cols_1")
    place = jnp.stack([core, across, near, chip, device, lax.axis_index(ROWS)])

    got = exchange(coarse_pencil(wave_coarse.reshape(288, NC)), ALL, 128).reshape(896, 128)
    got, planes = lax.optimization_barrier((got, swap_planes(potential_coarse, near)))
    got = exchange(coarse_z(place, got), CHIPS, 64).reshape(960, 128)
    got, planes = lax.optimization_barrier((got, spread_planes(planes, across)))
    got = exchange(coarse_y(place, got), CHIPS, 64).reshape(960, 128)
    other = lax.ppermute(got, CORE, [(0, 1), (1, 0)])
    turned = coarse_x(place, got, other, share_planes(planes, core, across))
    got = exchange(turned, CHIPS, 64).reshape(1792, 128)

    evolved, spectrum = fine_in(got)
    got = exchange(spectrum, ALL, 128).reshape(3456, 128)
    spectrum = fine_slab(place, got)
    got = exchange(spectrum, ALL, 128).reshape(3456, 128)
    damped, part = fine_out(place, got, evolved, potential_fine.reshape(1152, NF))
    parts = exchange(part, ALL, 128).reshape(128, 128)
    return scaled(parts, damped).reshape(48, 24, NF)


def solution(mesh):
    torus = Mesh(
        mesh.devices.reshape(4, 2, 2, 4, 2), ("rows_0", "rows_1", "rows_2", "cols_0", "cols_1")
    )
    return jax.shard_map(
        per_device,
        mesh=torus,
        in_specs=(P(ROWS, COLS, None), P(ROWS, COLS, None), P(COLS, ROWS, None)),
        out_specs=P(COLS, ROWS, None),
        check_vma=False,
    )
```

```python
import math

import jax
import jax.numpy as jnp
import numpy as np
from jax import lax
from jax.experimental import pallas as pl
from jax.experimental.pallas import tpu as pltpu
from jax.sharding import Mesh
from jax.sharding import PartitionSpec as P

NC = 192
NF = 384
ROWS = ("rows_0", "rows_1", "rows_2")
COLS = ("cols_0", "cols_1")
ALL = ROWS + COLS
CHIPS = ("rows_0", "rows_1", "cols_0", "cols_1")
CORE = "rows_2"

TIME_STEP = 0.5
CONTACT = 0.4
DIPOLE_STRENGTH = 0.3
EPSILON = 1e-06


def cas_table(rows, columns, length):
    phases = 2.0 * math.pi / length * ((np.outer(rows, columns)) % length)
    return np.cos(phases) + np.sin(phases)


def signed(length):
    k = np.arange(length)
    return np.where(k < length // 2, k, k - length)


def tables():
    k = np.arange(NC)
    wave = 2.0 * math.pi / NF * signed(NC)
    decay = np.exp(-0.5 * TIME_STEP * wave**2)
    hc = cas_table(k, k, NC)
    hf = cas_table(np.arange(NF), np.arange(NF), NF)
    evolve = hc @ (decay[:, None] * hc) / NC
    lifted = np.where(k < NC // 2, k, k + NC)
    lift = hf[:, lifted] @ (decay[:, None] * hc) / NC
    return [t.astype(np.float32) for t in (hc, hf, evolve, lift)]


HC, HF, EVOLVE, LIFT = tables()


def squares(index, length, spacing):
    s = jnp.where(index < length // 2, index, index - length).astype(jnp.float32)
    w = 2.0 * math.pi / (length * spacing) * s
    return w * w


def dipolar(wx, wy, wz, length):
    q = wx + wy + wz
    safe = jnp.where(q > 0, q, 1.0)
    return jnp.where(q > 0, DIPOLE_STRENGTH * (3.0 * wz - q) / safe, 0.0) / float(length) ** 3


F32 = jnp.float32
BF16 = jnp.bfloat16
VMEM = pl.BlockSpec(memory_space=pltpu.VMEM)
SMEM = pl.BlockSpec(memory_space=pltpu.SMEM)
HBM = pl.BlockSpec(memory_space=pltpu.HBM)
LIMIT = pltpu.CompilerParams(vmem_limit_bytes=20 * 1024 * 1024)


def halves(table):
    high = table.astype(BF16)
    return np.stack([high, (table - high.astype(np.float32)).astype(BF16)])


HF2 = halves(HF)
BY_SLAB = np.arange(NF).reshape(8, 48).T.reshape(-1)
HF_OUT2 = halves(HF[:, BY_SLAB])
HF_BACK2 = halves(HF[BY_SLAB, :])
PLANE = np.arange(NC).reshape(16, 12).T.reshape(-1)
LIFT_X2 = halves(LIFT[:, np.arange(NC).reshape(64, 3).T.reshape(-1)])
HC2 = halves(HC)
HC_WIDE2 = halves(np.pad(HC, ((0, 64), (0, 64))))
EVOLVE2 = halves(EVOLVE)
EVOLVE_Y2 = halves(np.pad(EVOLVE, ((0, 0), (0, 64))))
EVOLVE_X2 = halves(np.pad(EVOLVE[PLANE, :], ((0, 0), (0, 64))))
LIFT_Z2 = halves(LIFT[BY_SLAB, :])
LIFT_Y2 = np.stack(
    [
        halves(np.pad(LIFT.reshape(8, 2, 24, NC)[:, core].reshape(NC, NC).T, ((0, 0), (0, 64))))
        for core in range(2)
    ]
)
TURNED = (((1,), (1,)), ((), ()))
PLAIN = (((1,), (0,)), ((), ()))


def split(x):
    high = x.astype(BF16)
    return high, (x - high.astype(F32)).astype(BF16)


def dot3(a, b, dims=PLAIN):
    (ah, al), (bh, bl) = a, b

    def dot(p, q):
        return lax.dot_general(p, q, dims, preferred_element_type=F32)

    return dot(ah, bh) + (dot(al, bh) + dot(ah, bl))


def dot(a, b):
    return jnp.dot(a, b, preferred_element_type=F32)


def left3(x):
    high, low = split(x)
    return jnp.concatenate([high, low, high], axis=1)


def right3(x):
    high, low = split(x)
    return jnp.concatenate([high, high, low], axis=0)


def fetch_left(table, wide, sems):
    size = table.shape[2]
    return [
        pltpu.make_async_copy(table.at[part], wide.at[:, pl.ds(i * size, size)], sems.at[i])
        for i, part in enumerate((0, 1, 0))
    ]


def fetch_right(table, tall, sems):
    size = table.shape[1]
    return [
        pltpu.make_async_copy(table.at[part], tall.at[pl.ds(i * size, size), :], sems.at[i])
        for i, part in enumerate((0, 0, 1))
    ]


def begin(copies):
    for copy in copies:
        copy.start()


def finish(copies):
    for copy in copies:
        copy.wait()


def pair(ref):
    return ref[0], ref[1]


def tiles_of(row):
    return [row[:, 128 * t : 128 * t + 128] for t in range(row.shape[1] // 128)]


def shift_runs(row, lanes):
    lanes %= NF
    return pltpu.roll(row, lanes, 1) if lanes else row


def skew(rows, lead=0):
    return [tiles_of(shift_runs(row, 24 * a - lead)) for a, row in enumerate(rows)]


def diagonals(skewed, count):
    lane = lax.broadcasted_iota(jnp.int32, skewed[0][0].shape, 1)
    result = []
    for b in range(count):
        tiles = []
        for t in range(3):
            tile = None
            for p in range(128 * t // 24, (128 * t + 127) // 24 + 1):
                a = (p - b) % 16
                if a < len(skewed):
                    piece = skewed[a][t]
                    tile = piece if tile is None else jnp.where(lane < 24 * p - 128 * t, tile, piece)
            tiles.append(skewed[0][t] if tile is None else tile)
        result.append(jnp.concatenate(tiles, axis=1))
    return result


def in_hbm(x):
    return pltpu.with_memory_space_constraint(x, pltpu.HBM)


def coarse_pencil_kernel(wave_hbm, matrix_hbm, out_ref, wave_ref, matrix_ref, sems):
    copies = [
        pltpu.make_async_copy(wave_hbm, wave_ref, sems.at[0]),
        pltpu.make_async_copy(matrix_hbm, matrix_ref, sems.at[1]),
    ]
    begin(copies)
    finish(copies)
    high, low = split(wave_ref[...])
    pieces = []
    for k in range(3):
        lead = 32 * k

        def padded(x):
            parts = [jnp.zeros((lead, NC), BF16)] * (k > 0) + [x]
            return jnp.concatenate(parts + [jnp.zeros((96 - lead, NC), BF16)], axis=0)

        rows = slice(64 * k, 64 * k + 64)
        matrix = (matrix_ref[0, rows, :], matrix_ref[1, rows, :])
        pieces.append(tiles_of(dot3(matrix, (padded(high), padded(low)), TURNED)))
    (a0, a1, a2), (b0, b1, b2), (c0, c1, c2) = pieces
    for t, tile in enumerate([a0, a1, a2 + b0, b1, b2 + c0, c1, c2]):
        for p in range(8):
            for core in range(2):
                out_ref[pl.ds(p * 112 + core * 56 + t, 8, stride=7), :] = tile[8 * p : 8 * p + 8, :]


def coarse_pencil(wave):
    return pl.pallas_call(
        coarse_pencil_kernel,
        out_shape=jax.ShapeDtypeStruct((896, 128), F32),
        compiler_params=LIMIT,
        in_specs=[HBM] * 2,
        out_specs=VMEM,
        scratch_shapes=[
            pltpu.VMEM((288, NC), F32),
            pltpu.VMEM((2, NC, NC), BF16),
            pltpu.SemaphoreType.DMA((2,)),
        ],
    )(in_hbm(wave), in_hbm(jnp.asarray(EVOLVE2)))


def pack_rows(planes):
    (a0, a1), (b0, b1), (c0, c1) = [tiles_of(plane) for plane in planes]
    low = lax.broadcasted_iota(jnp.int32, a0.shape, 1) < 64
    b0, b1 = pltpu.roll(b0, 64, 1), pltpu.roll(b1, 64, 1)
    return [a0, jnp.where(low, a1, b0), jnp.where(low, b0, b1), c0, c1]


def unpack_rows(tiles):
    a0, mixed, b1, c0, c1 = tiles
    low = lax.broadcasted_iota(jnp.int32, a0.shape, 1) < 64
    b1 = pltpu.roll(b1, 64, 1)
    b0 = jnp.where(low, pltpu.roll(mixed, 64, 1), b1)
    return [jnp.concatenate(p, axis=1) for p in ((a0, mixed), (b0, b1), (c0, c1))]


def coarse_z_kernel(place_ref, got_ref, ey_ref, ex_ref, matrix_ref, out_ref, plane_ref):
    core = place_ref[0]
    for k in range(3):
        for g in range(2):
            rows = []
            for c in range(8):
                tiles = [got_ref[pl.ds(g * 448 + c * 7 + 2 * k + t, 8, stride=56), :] for t in range(3)]
                rows.append(jnp.concatenate(tiles, axis=1))
            for i, row in enumerate(diagonals(skew(rows, 32 * k), 12)):
                row = shift_runs(row, -24 * i)
                plane_ref[16 * i + 8 * g : 16 * i + 8 * g + 8, :] = row[:, :256]
        half = dot3(pair(ey_ref), split(plane_ref[...]), TURNED)
        evolved = dot3(split(half), pair(ex_ref))
        turned = dot3(pair(matrix_ref), split(evolved * evolved))
        mine = jnp.where(core == 0, turned, evolved)
        for i, tile in enumerate(pack_rows([mine[64 * j : 64 * j + 64, :] for j in range(3)])):
            out_ref[pl.ds(k * 5 + i, 64, stride=15), :] = tile


def coarse_z(place, got):
    return pl.pallas_call(
        coarse_z_kernel,
        out_shape=jax.ShapeDtypeStruct((960, 128), F32),
        compiler_params=LIMIT,
        in_specs=[SMEM] + [VMEM] * 4,
        out_specs=VMEM,
        scratch_shapes=[pltpu.VMEM((NC, 256), F32)],
    )(place, got, jnp.asarray(EVOLVE_Y2), jnp.asarray(EVOLVE_X2), jnp.asarray(HC2))


def coarse_y_kernel(place_ref, got_ref, matrix_ref, wide_ref, out_ref):
    core = place_ref[0]
    wx = squares(lax.broadcasted_iota(jnp.int32, (NC, 256), 0), NC, 2.0)
    wz = squares(lax.broadcasted_iota(jnp.int32, (NC, 256), 1), NC, 2.0)
    parts = []
    for j in range(3):
        parts.append(unpack_rows([got_ref[pl.ds(5 * j + i, 64, stride=15), :] for i in range(5)]))
    planes = []
    for k in range(3):
        both = jnp.concatenate([part[k] for part in parts] + [jnp.zeros((64, 256), F32)], axis=0)
        both = both.T[:NC, :]
        mid = dot3(pair(matrix_ref), split(both))
        mid = dot3(split(mid), pair(wide_ref))
        wy = squares(jnp.full((1, 1), 64 * k + place_ref[3], jnp.int32), NC, 2.0)
        mid = mid * dipolar(wx, wy, wz, NC)
        mid = dot3(split(mid), pair(wide_ref))
        mid = dot3(pair(matrix_ref), split(mid))
        planes.append(jnp.where(core == 0, mid, both))
    for i, tile in enumerate(pack_rows(planes)):
        out_ref[pl.ds(i, NC, stride=5), :] = tile


def coarse_y(place, got):
    return pl.pallas_call(
        coarse_y_kernel,
        out_shape=jax.ShapeDtypeStruct((960, 128), F32),
        compiler_params=LIMIT,
        in_specs=[SMEM] + [VMEM] * 3,
        out_specs=VMEM,
    )(place, got, jnp.asarray(HC2), jnp.asarray(HC_WIDE2))


def coarse_x_kernel(place_ref, got_ref, other_ref, potential_ref, matrix_ref, lz_ref, ly_ref, out_ref, lifted_ref):
    core = place_ref[0]
    slots = []
    for c in range(8):
        slots.append(2 * lax.rem(place_ref[1] - c // 2 + 4, 4) + (place_ref[2] ^ (c % 2)))
    lift_y = (ly_ref[core, 0], ly_ref[core, 1])
    part = jnp.zeros((1, 1), F32)
    blank = jnp.zeros((8, 128), F32)
    for k in range(3):
        fields, waves = [], []
        for i in range(5):
            rows = pl.ds(5 * k + i, 64, stride=15)
            mine, other = got_ref[rows, :], other_ref[rows, :]
            fields.append(jnp.where(core == 0, mine, other))
            waves.append(jnp.where(core == 0, other, mine))
        field = dot3(pair(matrix_ref), split(jnp.concatenate(unpack_rows(fields), axis=0)))
        wave = jnp.concatenate(unpack_rows(waves), axis=0)
        evolved = [wave[:, :128], wave[:, 128:NC]]
        pieces = []
        for t, e in enumerate(evolved):
            lanes = slice(128 * t, 128 * t + e.shape[1])
            v = jnp.concatenate([potential_ref[c, 24 * k : 24 * k + 24, lanes] for c in slots], axis=0)
            d = jnp.exp(-TIME_STEP * (v + CONTACT * e * e + field[:, lanes])) * e
            part = part + jnp.sum(d * d, keepdims=True)
            pieces.append(d)
        damped = split(jnp.concatenate(pieces, axis=1))
        lifted = dot3(pair(lz_ref), damped, TURNED)
        lifted_ref[...] = dot3(split(lifted), lift_y)
        for g in range(3):
            rows = []
            for i in range(16):
                row = lifted_ref[128 * g + 8 * i : 128 * g + 8 * i + 8, :]
                rows.append(jnp.concatenate([row, blank], axis=1))
            for p, row in enumerate(diagonals(skew(rows), 8)):
                row = jnp.where(core == 0, shift_runs(row, 24 * p), shift_runs(row, 24 * p + 24))
                for t, tile in enumerate(tiles_of(row)):
                    out_ref[pl.ds(p * 224 + k * 9 + g * 3 + t, 8, stride=28), :] = tile
    out_ref[pl.ds(27, 64, stride=28), :] = jnp.broadcast_to(part, (64, 128))


def coarse_x(place, got, other, potential):
    return pl.pallas_call(
        coarse_x_kernel,
        out_shape=jax.ShapeDtypeStruct((1792, 128), F32),
        compiler_params=LIMIT,
        in_specs=[SMEM] + [VMEM] * 6,
        out_specs=VMEM,
        scratch_shapes=[pltpu.VMEM((NF, 256), F32)],
    )(place, got, other, potential, jnp.asarray(HC2), jnp.asarray(LIFT_Z2), jnp.asarray(LIFT_Y2))


def fine_in_kernel(
    got_ref, lift_ref, matrix_hbm, evolved_hbm, out_ref, evolved_ref, matrix_ref, sems, saved
):
    copies = fetch_left(matrix_hbm, matrix_ref, sems)
    begin(copies)
    parts = got_ref[pl.ds(27, 64, stride=28), :]
    total = jnp.sum(parts, axis=0, keepdims=True)
    scale = lax.rsqrt(total / float(NC) ** 3 + EPSILON)
    scale = jnp.concatenate([scale] * 3, axis=1)
    finish(copies)

    def save(n):
        columns = pl.ds(pl.multiple_of(n * 384, 128), 384)
        source, target = evolved_ref.at[:, columns], evolved_hbm.at[:, columns]
        return pltpu.make_async_copy(source, target, saved.at[n])

    def body(n, carry):
        rows = []
        for k in range(3):
            tiles = [got_ref[pl.ds(k * 9 + 3 * n + t, 64, stride=28), :] for t in range(3)]
            rows.append(jnp.concatenate(tiles, axis=1))
        spectrum = split(jnp.concatenate(rows, axis=0))
        evolved = dot3(pair(lift_ref), spectrum) * scale
        evolved_ref[:, pl.ds(pl.multiple_of(n * 384, 128), 384)] = evolved
        turned = dot(matrix_ref[...], right3(evolved * evolved))
        for k in range(3):
            for t in range(3):
                piece = turned[128 * k : 128 * k + 128, 128 * t : 128 * t + 128]
                out_ref[pl.ds(k * 9 + 3 * n + t, 128, stride=27), :] = piece
        save(n).start()
        return carry

    lax.fori_loop(0, 3, body, 0)
    for n in range(3):
        save(n).wait()


def fine_in(got):
    return pl.pallas_call(
        fine_in_kernel,
        out_shape=[
            pltpu.HBM((NF, 1152), F32),
            jax.ShapeDtypeStruct((3456, 128), F32),
        ],
        compiler_params=LIMIT,
        in_specs=[VMEM, VMEM, HBM],
        out_specs=[HBM, VMEM],
        scratch_shapes=[
            pltpu.VMEM((NF, 1152), F32),
            pltpu.VMEM((NF, 1152), BF16),
            pltpu.SemaphoreType.DMA((3,)),
            pltpu.SemaphoreType.DMA((3,)),
        ],
    )(got, jnp.asarray(LIFT_X2), jnp.asarray(HF2))


def fine_slab_kernel(
    place_ref, got_ref, out_hbm, back_hbm, matrix_hbm, out_ref, plane_ref, back_ref, out_m, back_m, matrix, sems
):
    out_copies = fetch_left(out_hbm, out_m, sems.at[0])
    back_copies = fetch_left(back_hbm, back_m, sems.at[1])
    copies = fetch_right(matrix_hbm, matrix, sems.at[2])
    begin(out_copies + copies + back_copies)
    wz = squares(lax.broadcasted_iota(jnp.int32, (NF, NF), 0), NF, 1.0)
    wy = squares(lax.broadcasted_iota(jnp.int32, (NF, NF), 1), NF, 1.0)


    def unpack(k):
        for g in range(3):
            base = k * 9 + g * 3
            skewed = [
                [got_ref[pl.ds(r * 216 + base + t, 8, stride=27), :] for t in range(3)]
                for r in range(16)
            ]
            for i, row in enumerate(diagonals(skewed, 16)):
                start = 128 * g + 8 * i
                plane_ref[start : start + 8, :] = shift_runs(row, -24 * i)

    def pack(k):
        for g in range(3):
            base = k * 9 + g * 3
            rows = [back_ref[128 * g + 8 * i : 128 * g + 8 * i + 8, :] for i in range(16)]
            for r, row in enumerate(diagonals(skew(rows), 16)):
                for t, tile in enumerate(tiles_of(row)):
                    out_ref[pl.ds(r * 216 + base + t, 8, stride=27), :] = tile

    def body(k, carry):
        mid = dot(out_m[...], right3(plane_ref[...]))
        pack(jnp.maximum(k - 1, 0))
        unpack(jnp.minimum(k + 1, 2))
        mid = dot(left3(mid), matrix[...])
        kx = 128 * k + place_ref[4]
        wx = squares(jnp.full((1, 1), kx, jnp.int32), NF, 1.0)
        mid = mid * dipolar(wx, wy, wz, NF)
        mid = dot(left3(mid), matrix[...])
        back_ref[...] = dot(back_m[...], right3(mid))
        return carry

    back_ref[...] = jnp.zeros_like(back_ref)
    unpack(0)
    finish(out_copies + copies + back_copies)
    lax.fori_loop(0, 3, body, 0)
    pack(2)


def fine_slab(place, got):
    return pl.pallas_call(
        fine_slab_kernel,
        out_shape=jax.ShapeDtypeStruct((3456, 128), F32),
        compiler_params=LIMIT,
        in_specs=[SMEM, VMEM] + [HBM] * 3,
        out_specs=VMEM,
        scratch_shapes=[
            pltpu.VMEM((NF, NF), F32),
            pltpu.VMEM((NF, NF), F32),
            pltpu.VMEM((NF, 1152), BF16),
            pltpu.VMEM((NF, 1152), BF16),
            pltpu.VMEM((1152, NF), BF16),
            pltpu.SemaphoreType.DMA((3, 3)),
        ],
    )(place, got, jnp.asarray(HF_OUT2), jnp.asarray(HF_BACK2), jnp.asarray(HF2))


def fine_out_kernel(place_ref, got_ref, evolved_ref, potential_ref, matrix_ref, damped_ref, part_ref):
    part_ref[...] = jnp.zeros_like(part_ref)
    row = place_ref[5]

    def block(n, p):
        return pl.ds(pl.multiple_of(384 * n + 24 * lax.rem(p + 16 - row, 16), 8), 24)

    def body(n, carry):
        rows = []
        for k in range(3):
            tiles = [got_ref[pl.ds(k * 9 + 3 * n + t, 128, stride=27), :] for t in range(3)]
            rows.append(jnp.concatenate(tiles, axis=1))
        field = dot3(pair(matrix_ref), split(jnp.concatenate(rows, axis=0)))
        columns = pl.ds(n * 384, 384)
        evolved = evolved_ref[:, columns]
        potential = jnp.concatenate([potential_ref[block(n, p), :] for p in range(16)], axis=0).T
        exponent = -TIME_STEP * (potential + CONTACT * evolved * evolved + field)
        damped = jnp.exp(exponent) * evolved
        part_ref[...] += jnp.sum(damped * damped)
        turned = damped.T
        for p in range(16):
            damped_ref[block(n, p), :] = turned[24 * p : 24 * p + 24, :]
        return carry

    for n in range(3):
        body(n, 0)


def fine_out(place, got, evolved, potential):
    return pl.pallas_call(
        fine_out_kernel,
        out_shape=[
            jax.ShapeDtypeStruct((1152, NF), F32),
            jax.ShapeDtypeStruct((128, 128), F32),
        ],
        compiler_params=LIMIT,
        in_specs=[SMEM] + [VMEM] * 4,
        out_specs=[VMEM] * 2,
    )(place, got, evolved, potential, jnp.asarray(HF2))


def scale_kernel(parts_ref, damped_ref, out_hbm, scaled_ref, sems):
    total = jnp.sum(parts_ref[...], axis=0, keepdims=True)
    scale = lax.rsqrt(total / float(NF) ** 3 + EPSILON)
    scale = jnp.concatenate([scale] * 3, axis=1)
    copies = []
    for i in range(4):
        rows = pl.ds(288 * i, 288)
        copies.append(pltpu.make_async_copy(scaled_ref.at[rows], out_hbm.at[rows], sems.at[i]))
        scaled_ref[rows, :] = damped_ref[rows, :] * scale
        if i:
            copies[i - 1].start()
    copies[3].start()
    finish(copies)


def scaled(parts, damped):
    return pl.pallas_call(
        scale_kernel,
        out_shape=jax.ShapeDtypeStruct((1152, NF), F32),
        compiler_params=LIMIT,
        in_specs=[VMEM] * 2,
        out_specs=HBM,
        scratch_shapes=[pltpu.VMEM((1152, NF), F32), pltpu.SemaphoreType.DMA((4,))],
    )(parts, damped)


def exchange(buffer, axes, count):
    flat = buffer.reshape(count, 1, -1)
    return lax.all_to_all(flat, axes, split_axis=0, concat_axis=0, tiled=False)


def swap_planes(potential, near):
    other = lax.ppermute(potential, "cols_1", [(0, 1), (1, 0)])
    planes = [
        lax.dynamic_index_in_dim(held.reshape(2, 2, 72, NC), near, 1, keepdims=False)
        for held in (potential, other)
    ]
    return jnp.stack(planes, axis=1)


def spread_planes(planes, across):
    slots = []
    for i in range(4):
        chunk = lax.dynamic_index_in_dim(planes, (across + i) % 2, 0, keepdims=False)
        if i:
            moves = [(c * 4 + (y - i) % 4, c * 4 + y) for c in range(2) for y in (2 * c, 2 * c + 1)]
            chunk = lax.ppermute(chunk, (CORE, "cols_0"), moves)
        slots.append(chunk)
    return jnp.stack(slots)


def share_planes(slots, core, across):
    moves = [(y // 2 * 4 + y, (1 - y // 2) * 4 + y) for y in range(4)]
    other = lax.ppermute(slots, (CORE, "cols_0"), moves)
    return jnp.where(core == across // 2, slots, other).reshape(8, 72, NC)


def per_device(wave_coarse, potential_coarse, potential_fine):
    core = lax.axis_index(CORE)
    chip = lax.axis_index(CHIPS)
    device = lax.axis_index(ALL)
    across, near = lax.axis_index("cols_0"), lax.axis_index("cols_1")
    place = jnp.stack([core, across, near, chip, device, lax.axis_index(ROWS)])

    got = exchange(coarse_pencil(wave_coarse.reshape(288, NC)), ALL, 128).reshape(896, 128)
    got, planes = lax.optimization_barrier((got, swap_planes(potential_coarse, near)))
    got = exchange(coarse_z(place, got), CHIPS, 64).reshape(960, 128)
    got, planes = lax.optimization_barrier((got, spread_planes(planes, across)))
    got = exchange(coarse_y(place, got), CHIPS, 64).reshape(960, 128)
    other = lax.ppermute(got, CORE, [(0, 1), (1, 0)])
    turned = coarse_x(place, got, other, share_planes(planes, core, across))
    got = exchange(turned, CHIPS, 64).reshape(1792, 128)

    evolved, spectrum = fine_in(got)
    got = exchange(spectrum, ALL, 128).reshape(3456, 128)
    spectrum = fine_slab(place, got)
    got = exchange(spectrum, ALL, 128).reshape(3456, 128)
    damped, part = fine_out(place, got, evolved, potential_fine.reshape(1152, NF))
    parts = exchange(part, ALL, 128).reshape(128, 128)
    return scaled(parts, damped).reshape(48, 24, NF)


def solution(mesh):
    torus = Mesh(
        mesh.devices.reshape(4, 2, 2, 4, 2), ("rows_0", "rows_1", "rows_2", "cols_0", "cols_1")
    )
    return jax.shard_map(
        per_device,
        mesh=torus,
        in_specs=(P(ROWS, COLS, None), P(ROWS, COLS, None), P(COLS, ROWS, None)),
        out_specs=P(COLS, ROWS, None),
        check_vma=False,
    )
```

```python
import math

import jax
import jax.numpy as jnp
import numpy as np
from jax import lax
from jax.experimental import pallas as pl
from jax.experimental.pallas import tpu as pltpu
from jax.sharding import Mesh
from jax.sharding import PartitionSpec as P

NC = 192
NF = 384
ROWS = ("rows_0", "rows_1", "rows_2")
COLS = ("cols_0", "cols_1")
ALL = ROWS + COLS
CHIPS = ("rows_0", "rows_1", "cols_0", "cols_1")
CORE = "rows_2"

TIME_STEP = 0.5
CONTACT = 0.4
DIPOLE_STRENGTH = 0.3
EPSILON = 1e-06


def cas_table(rows, columns, length):
    phases = 2.0 * math.pi / length * ((np.outer(rows, columns)) % length)
    return np.cos(phases) + np.sin(phases)


def signed(length):
    k = np.arange(length)
    return np.where(k < length // 2, k, k - length)


def tables():
    k = np.arange(NC)
    wave = 2.0 * math.pi / NF * signed(NC)
    decay = np.exp(-0.5 * TIME_STEP * wave**2)
    hc = cas_table(k, k, NC)
    hf = cas_table(np.arange(NF), np.arange(NF), NF)
    evolve = hc @ (decay[:, None] * hc) / NC
    lifted = np.where(k < NC // 2, k, k + NC)
    lift = hf[:, lifted] @ (decay[:, None] * hc) / NC
    return [t.astype(np.float32) for t in (hc, hf, evolve, lift)]


HC, HF, EVOLVE, LIFT = tables()


def squares(index, length, spacing):
    s = jnp.where(index < length // 2, index, index - length).astype(jnp.float32)
    w = 2.0 * math.pi / (length * spacing) * s
    return w * w


def dipolar(wx, wy, wz, length):
    q = wx + wy + wz
    safe = jnp.where(q > 0, q, 1.0)
    return jnp.where(q > 0, DIPOLE_STRENGTH * (3.0 * wz - q) / safe, 0.0) / float(length) ** 3


F32 = jnp.float32
BF16 = jnp.bfloat16
VMEM = pl.BlockSpec(memory_space=pltpu.VMEM)
SMEM = pl.BlockSpec(memory_space=pltpu.SMEM)
HBM = pl.BlockSpec(memory_space=pltpu.HBM)
LIMIT = pltpu.CompilerParams(vmem_limit_bytes=20 * 1024 * 1024)


def halves(table):
    high = table.astype(BF16)
    return np.stack([high, (table - high.astype(np.float32)).astype(BF16)])


HF2 = halves(HF)
BY_SLAB = np.arange(NF).reshape(8, 48).T.reshape(-1)
HF_OUT2 = halves(HF[:, BY_SLAB])
HF_BACK2 = halves(HF[BY_SLAB, :])
PLANE = np.arange(NC).reshape(16, 12).T.reshape(-1)
LIFT_X2 = halves(LIFT[:, np.arange(NC).reshape(64, 3).T.reshape(-1)])
HC2 = halves(HC)
HC_WIDE2 = halves(np.pad(HC, ((0, 64), (0, 64))))
EVOLVE2 = halves(EVOLVE)
EVOLVE_Y2 = halves(np.pad(EVOLVE, ((0, 0), (0, 64))))
EVOLVE_X2 = halves(np.pad(EVOLVE[PLANE, :], ((0, 0), (0, 64))))
LIFT_Z2 = halves(LIFT[BY_SLAB, :])
LIFT_Y2 = np.stack(
    [
        halves(np.pad(LIFT.reshape(8, 2, 24, NC)[:, core].reshape(NC, NC).T, ((0, 0), (0, 64))))
        for core in range(2)
    ]
)
TURNED = (((1,), (1,)), ((), ()))
PLAIN = (((1,), (0,)), ((), ()))


def split(x):
    high = x.astype(BF16)
    return high, (x - high.astype(F32)).astype(BF16)


def dot3(a, b, dims=PLAIN):
    (ah, al), (bh, bl) = a, b

    def dot(p, q):
        return lax.dot_general(p, q, dims, preferred_element_type=F32)

    return dot(ah, bh) + (dot(al, bh) + dot(ah, bl))


def dot(a, b):
    return jnp.dot(a, b, preferred_element_type=F32)


def left3(x):
    high, low = split(x)
    return jnp.concatenate([high, low, high], axis=1)


def right3(x):
    high, low = split(x)
    return jnp.concatenate([high, high, low], axis=0)


def fetch_left(table, wide, sems):
    size = table.shape[2]
    return [
        pltpu.make_async_copy(table.at[part], wide.at[:, pl.ds(i * size, size)], sems.at[i])
        for i, part in enumerate((0, 1, 0))
    ]


def fetch_right(table, tall, sems):
    size = table.shape[1]
    return [
        pltpu.make_async_copy(table.at[part], tall.at[pl.ds(i * size, size), :], sems.at[i])
        for i, part in enumerate((0, 0, 1))
    ]


def begin(copies):
    for copy in copies:
        copy.start()


def finish(copies):
    for copy in copies:
        copy.wait()


def pair(ref):
    return ref[0], ref[1]


def tiles_of(row):
    return [row[:, 128 * t : 128 * t + 128] for t in range(row.shape[1] // 128)]


def shift_runs(row, lanes):
    lanes %= NF
    return pltpu.roll(row, lanes, 1) if lanes else row


def skew(rows, lead=0):
    return [tiles_of(shift_runs(row, 24 * a - lead)) for a, row in enumerate(rows)]


def diagonals(skewed, count):
    lane = lax.broadcasted_iota(jnp.int32, skewed[0][0].shape, 1)
    result = []
    for b in range(count):
        tiles = []
        for t in range(3):
            tile = None
            for p in range(128 * t // 24, (128 * t + 127) // 24 + 1):
                a = (p - b) % 16
                if a < len(skewed):
                    piece = skewed[a][t]
                    tile = piece if tile is None else jnp.where(lane < 24 * p - 128 * t, tile, piece)
            tiles.append(skewed[0][t] if tile is None else tile)
        result.append(jnp.concatenate(tiles, axis=1))
    return result


def in_hbm(x):
    return pltpu.with_memory_space_constraint(x, pltpu.HBM)


def coarse_pencil_kernel(wave_hbm, matrix_hbm, out_ref, wave_ref, matrix_ref, sems):
    copies = [
        pltpu.make_async_copy(wave_hbm, wave_ref, sems.at[0]),
        pltpu.make_async_copy(matrix_hbm, matrix_ref, sems.at[1]),
    ]
    begin(copies)
    finish(copies)
    high, low = split(wave_ref[...])
    pieces = []
    for k in range(3):
        lead = 32 * k

        def padded(x):
            parts = [jnp.zeros((lead, NC), BF16)] * (k > 0) + [x]
            return jnp.concatenate(parts + [jnp.zeros((96 - lead, NC), BF16)], axis=0)

        rows = slice(64 * k, 64 * k + 64)
        matrix = (matrix_ref[0, rows, :], matrix_ref[1, rows, :])
        pieces.append(tiles_of(dot3(matrix, (padded(high), padded(low)), TURNED)))
    (a0, a1, a2), (b0, b1, b2), (c0, c1, c2) = pieces
    for t, tile in enumerate([a0, a1, a2 + b0, b1, b2 + c0, c1, c2]):
        for p in range(8):
            for core in range(2):
                out_ref[pl.ds(p * 112 + core * 56 + t, 8, stride=7), :] = tile[8 * p : 8 * p + 8, :]


def coarse_pencil(wave):
    return pl.pallas_call(
        coarse_pencil_kernel,
        out_shape=jax.ShapeDtypeStruct((896, 128), F32),
        compiler_params=LIMIT,
        in_specs=[HBM] * 2,
        out_specs=VMEM,
        scratch_shapes=[
            pltpu.VMEM((288, NC), F32),
            pltpu.VMEM((2, NC, NC), BF16),
            pltpu.SemaphoreType.DMA((2,)),
        ],
    )(in_hbm(wave), in_hbm(jnp.asarray(EVOLVE2)))


def pack_rows(planes):
    (a0, a1), (b0, b1), (c0, c1) = [tiles_of(plane) for plane in planes]
    low = lax.broadcasted_iota(jnp.int32, a0.shape, 1) < 64
    b0, b1 = pltpu.roll(b0, 64, 1), pltpu.roll(b1, 64, 1)
    return [a0, jnp.where(low, a1, b0), jnp.where(low, b0, b1), c0, c1]


def unpack_rows(tiles):
    a0, mixed, b1, c0, c1 = tiles
    low = lax.broadcasted_iota(jnp.int32, a0.shape, 1) < 64
    b1 = pltpu.roll(b1, 64, 1)
    b0 = jnp.where(low, pltpu.roll(mixed, 64, 1), b1)
    return [jnp.concatenate(p, axis=1) for p in ((a0, mixed), (b0, b1), (c0, c1))]


def coarse_z_kernel(place_ref, got_ref, ey_ref, ex_ref, matrix_ref, out_ref, plane_ref):
    core = place_ref[0]
    for k in range(3):
        for g in range(2):
            rows = []
            for c in range(8):
                tiles = [got_ref[pl.ds(g * 448 + c * 7 + 2 * k + t, 8, stride=56), :] for t in range(3)]
                rows.append(jnp.concatenate(tiles, axis=1))
            for i, row in enumerate(diagonals(skew(rows, 32 * k), 12)):
                row = shift_runs(row, -24 * i)
                plane_ref[16 * i + 8 * g : 16 * i + 8 * g + 8, :] = row[:, :256]
        half = dot3(pair(ey_ref), split(plane_ref[...]), TURNED)
        evolved = dot3(split(half), pair(ex_ref))
        turned = dot3(pair(matrix_ref), split(evolved * evolved))
        mine = jnp.where(core == 0, turned, evolved)
        for i, tile in enumerate(pack_rows([mine[64 * j : 64 * j + 64, :] for j in range(3)])):
            out_ref[pl.ds(k * 5 + i, 64, stride=15), :] = tile


def coarse_z(place, got):
    return pl.pallas_call(
        coarse_z_kernel,
        out_shape=jax.ShapeDtypeStruct((960, 128), F32),
        compiler_params=LIMIT,
        in_specs=[SMEM] + [VMEM] * 4,
        out_specs=VMEM,
        scratch_shapes=[pltpu.VMEM((NC, 256), F32)],
    )(place, got, jnp.asarray(EVOLVE_Y2), jnp.asarray(EVOLVE_X2), jnp.asarray(HC2))


def coarse_y_kernel(place_ref, got_ref, matrix_ref, wide_ref, out_ref):
    core = place_ref[0]
    wx = squares(lax.broadcasted_iota(jnp.int32, (NC, 256), 0), NC, 2.0)
    wz = squares(lax.broadcasted_iota(jnp.int32, (NC, 256), 1), NC, 2.0)
    parts = []
    for j in range(3):
        parts.append(unpack_rows([got_ref[pl.ds(5 * j + i, 64, stride=15), :] for i in range(5)]))
    planes = []
    for k in range(3):
        both = jnp.concatenate([part[k] for part in parts] + [jnp.zeros((64, 256), F32)], axis=0)
        both = both.T[:NC, :]
        mid = dot3(pair(matrix_ref), split(both))
        mid = dot3(split(mid), pair(wide_ref))
        wy = squares(jnp.full((1, 1), 64 * k + place_ref[3], jnp.int32), NC, 2.0)
        mid = mid * dipolar(wx, wy, wz, NC)
        mid = dot3(split(mid), pair(wide_ref))
        mid = dot3(pair(matrix_ref), split(mid))
        planes.append(jnp.where(core == 0, mid, both))
    for i, tile in enumerate(pack_rows(planes)):
        out_ref[pl.ds(i, NC, stride=5), :] = tile


def coarse_y(place, got):
    return pl.pallas_call(
        coarse_y_kernel,
        out_shape=jax.ShapeDtypeStruct((960, 128), F32),
        compiler_params=LIMIT,
        in_specs=[SMEM] + [VMEM] * 3,
        out_specs=VMEM,
    )(place, got, jnp.asarray(HC2), jnp.asarray(HC_WIDE2))


def coarse_x_kernel(place_ref, got_ref, other_ref, potential_ref, matrix_ref, lz_ref, ly_ref, out_ref, lifted_ref):
    core = place_ref[0]
    slots = []
    for c in range(8):
        slots.append(2 * lax.rem(place_ref[1] - c // 2 + 4, 4) + (place_ref[2] ^ (c % 2)))
    lift_y = (ly_ref[core, 0], ly_ref[core, 1])
    part = jnp.zeros((1, 1), F32)
    blank = jnp.zeros((8, 128), F32)
    for k in range(3):
        fields, waves = [], []
        for i in range(5):
            rows = pl.ds(5 * k + i, 64, stride=15)
            mine, other = got_ref[rows, :], other_ref[rows, :]
            fields.append(jnp.where(core == 0, mine, other))
            waves.append(jnp.where(core == 0, other, mine))
        field = dot3(pair(matrix_ref), split(jnp.concatenate(unpack_rows(fields), axis=0)))
        wave = jnp.concatenate(unpack_rows(waves), axis=0)
        evolved = [wave[:, :128], wave[:, 128:NC]]
        pieces = []
        for t, e in enumerate(evolved):
            lanes = slice(128 * t, 128 * t + e.shape[1])
            v = jnp.concatenate([potential_ref[c, 24 * k : 24 * k + 24, lanes] for c in slots], axis=0)
            d = jnp.exp(-TIME_STEP * (v + CONTACT * e * e + field[:, lanes])) * e
            part = part + jnp.sum(d * d, keepdims=True)
            pieces.append(d)
        damped = split(jnp.concatenate(pieces, axis=1))
        lifted = dot3(pair(lz_ref), damped, TURNED)
        lifted_ref[...] = dot3(split(lifted), lift_y)
        for g in range(3):
            rows = []
            for i in range(16):
                row = lifted_ref[128 * g + 8 * i : 128 * g + 8 * i + 8, :]
                rows.append(jnp.concatenate([row, blank], axis=1))
            for p, row in enumerate(diagonals(skew(rows), 8)):
                row = jnp.where(core == 0, shift_runs(row, 24 * p), shift_runs(row, 24 * p + 24))
                for t, tile in enumerate(tiles_of(row)):
                    out_ref[pl.ds(p * 224 + k * 9 + g * 3 + t, 8, stride=28), :] = tile
    out_ref[pl.ds(27, 64, stride=28), :] = jnp.broadcast_to(part, (64, 128))


def coarse_x(place, got, other, potential):
    return pl.pallas_call(
        coarse_x_kernel,
        out_shape=jax.ShapeDtypeStruct((1792, 128), F32),
        compiler_params=LIMIT,
        in_specs=[SMEM] + [VMEM] * 6,
        out_specs=VMEM,
        scratch_shapes=[pltpu.VMEM((NF, 256), F32)],
    )(place, got, other, potential, jnp.asarray(HC2), jnp.asarray(LIFT_Z2), jnp.asarray(LIFT_Y2))


def fine_in_kernel(
    got_ref, lift_ref, matrix_hbm, evolved_hbm, out_ref, evolved_ref, matrix_ref, sems, saved
):
    copies = fetch_left(matrix_hbm, matrix_ref, sems)
    begin(copies)
    parts = got_ref[pl.ds(27, 64, stride=28), :]
    total = jnp.sum(parts, axis=0, keepdims=True)
    scale = lax.rsqrt(total / float(NC) ** 3 + EPSILON)
    scale = jnp.concatenate([scale] * 3, axis=1)
    finish(copies)

    def save(n):
        columns = pl.ds(pl.multiple_of(n * 384, 128), 384)
        source, target = evolved_ref.at[:, columns], evolved_hbm.at[:, columns]
        return pltpu.make_async_copy(source, target, saved.at[n])

    def body(n, carry):
        rows = []
        for k in range(3):
            tiles = [got_ref[pl.ds(k * 9 + 3 * n + t, 64, stride=28), :] for t in range(3)]
            rows.append(jnp.concatenate(tiles, axis=1))
        spectrum = split(jnp.concatenate(rows, axis=0))
        evolved = dot3(pair(lift_ref), spectrum) * scale
        evolved_ref[:, pl.ds(pl.multiple_of(n * 384, 128), 384)] = evolved
        turned = dot(matrix_ref[...], right3(evolved * evolved))
        for k in range(3):
            for t in range(3):
                piece = turned[128 * k : 128 * k + 128, 128 * t : 128 * t + 128]
                out_ref[pl.ds(k * 9 + 3 * n + t, 128, stride=27), :] = piece
        save(n).start()
        return carry

    lax.fori_loop(0, 3, body, 0)
    for n in range(3):
        save(n).wait()


def fine_in(got):
    return pl.pallas_call(
        fine_in_kernel,
        out_shape=[
            pltpu.HBM((NF, 1152), F32),
            jax.ShapeDtypeStruct((3456, 128), F32),
        ],
        compiler_params=LIMIT,
        in_specs=[VMEM, VMEM, HBM],
        out_specs=[HBM, VMEM],
        scratch_shapes=[
            pltpu.VMEM((NF, 1152), F32),
            pltpu.VMEM((NF, 1152), BF16),
            pltpu.SemaphoreType.DMA((3,)),
            pltpu.SemaphoreType.DMA((3,)),
        ],
    )(got, jnp.asarray(LIFT_X2), jnp.asarray(HF2))


def fine_slab_kernel(
    place_ref, got_ref, out_hbm, back_hbm, matrix_hbm, out_ref, plane_ref, back_ref, out_m, back_m, matrix, sems
):
    out_copies = fetch_left(out_hbm, out_m, sems.at[0])
    back_copies = fetch_left(back_hbm, back_m, sems.at[1])
    copies = fetch_right(matrix_hbm, matrix, sems.at[2])
    begin(out_copies + copies + back_copies)
    wz = squares(lax.broadcasted_iota(jnp.int32, (NF, NF), 0), NF, 1.0)
    wy = squares(lax.broadcasted_iota(jnp.int32, (NF, NF), 1), NF, 1.0)


    def unpack(k):
        for g in range(3):
            base = k * 9 + g * 3
            skewed = [
                [got_ref[pl.ds(r * 216 + base + t, 8, stride=27), :] for t in range(3)]
                for r in range(16)
            ]
            for i, row in enumerate(diagonals(skewed, 16)):
                start = 128 * g + 8 * i
                plane_ref[start : start + 8, :] = shift_runs(row, -24 * i)

    def pack(k):
        for g in range(3):
            base = k * 9 + g * 3
            rows = [back_ref[128 * g + 8 * i : 128 * g + 8 * i + 8, :] for i in range(16)]
            for r, row in enumerate(diagonals(skew(rows), 16)):
                for t, tile in enumerate(tiles_of(row)):
                    out_ref[pl.ds(r * 216 + base + t, 8, stride=27), :] = tile

    def body(k, carry):
        mid = dot(out_m[...], right3(plane_ref[...]))
        pack(jnp.maximum(k - 1, 0))
        unpack(jnp.minimum(k + 1, 2))
        mid = dot(left3(mid), matrix[...])
        kx = 128 * k + place_ref[4]
        wx = squares(jnp.full((1, 1), kx, jnp.int32), NF, 1.0)
        mid = mid * dipolar(wx, wy, wz, NF)
        mid = dot(left3(mid), matrix[...])
        back_ref[...] = dot(back_m[...], right3(mid))
        return carry

    back_ref[...] = jnp.zeros_like(back_ref)
    unpack(0)
    finish(out_copies + copies + back_copies)
    lax.fori_loop(0, 3, body, 0)
    pack(2)


def fine_slab(place, got):
    return pl.pallas_call(
        fine_slab_kernel,
        out_shape=jax.ShapeDtypeStruct((3456, 128), F32),
        compiler_params=LIMIT,
        in_specs=[SMEM, VMEM] + [HBM] * 3,
        out_specs=VMEM,
        scratch_shapes=[
            pltpu.VMEM((NF, NF), F32),
            pltpu.VMEM((NF, NF), F32),
            pltpu.VMEM((NF, 1152), BF16),
            pltpu.VMEM((NF, 1152), BF16),
            pltpu.VMEM((1152, NF), BF16),
            pltpu.SemaphoreType.DMA((3, 3)),
        ],
    )(place, got, jnp.asarray(HF_OUT2), jnp.asarray(HF_BACK2), jnp.asarray(HF2))


def fine_out_kernel(place_ref, got_ref, evolved_ref, potential_ref, matrix_ref, damped_ref, part_ref):
    part_ref[...] = jnp.zeros_like(part_ref)
    row = place_ref[5]

    def block(n, p):
        return pl.ds(pl.multiple_of(384 * n + 24 * lax.rem(p + 16 - row, 16), 8), 24)

    def body(n, carry):
        rows = []
        for k in range(3):
            tiles = [got_ref[pl.ds(k * 9 + 3 * n + t, 128, stride=27), :] for t in range(3)]
            rows.append(jnp.concatenate(tiles, axis=1))
        field = dot3(pair(matrix_ref), split(jnp.concatenate(rows, axis=0)))
        columns = pl.ds(n * 384, 384)
        evolved = evolved_ref[:, columns]
        potential = jnp.concatenate([potential_ref[block(n, p), :] for p in range(16)], axis=0).T
        exponent = -TIME_STEP * (potential + CONTACT * evolved * evolved + field)
        damped = jnp.exp(exponent) * evolved
        part_ref[...] += jnp.sum(damped * damped)
        turned = damped.T
        for p in range(16):
            damped_ref[block(n, p), :] = turned[24 * p : 24 * p + 24, :]
        return carry

    for n in range(3):
        body(n, 0)


def fine_out(place, got, evolved, potential):
    return pl.pallas_call(
        fine_out_kernel,
        out_shape=[
            jax.ShapeDtypeStruct((1152, NF), F32),
            jax.ShapeDtypeStruct((128, 128), F32),
        ],
        compiler_params=LIMIT,
        in_specs=[SMEM] + [VMEM] * 4,
        out_specs=[VMEM] * 2,
    )(place, got, evolved, potential, jnp.asarray(HF2))


def scale_kernel(parts_ref, damped_ref, out_hbm, scaled_ref, sems):
    total = jnp.sum(parts_ref[...], axis=0, keepdims=True)
    scale = lax.rsqrt(total / float(NF) ** 3 + EPSILON)
    scale = jnp.concatenate([scale] * 3, axis=1)
    copies = []
    for i in range(4):
        rows = pl.ds(288 * i, 288)
        copies.append(pltpu.make_async_copy(scaled_ref.at[rows], out_hbm.at[rows], sems.at[i]))
        scaled_ref[rows, :] = damped_ref[rows, :] * scale
        if i:
            copies[i - 1].start()
    copies[3].start()
    finish(copies)


def scaled(parts, damped):
    return pl.pallas_call(
        scale_kernel,
        out_shape=jax.ShapeDtypeStruct((1152, NF), F32),
        compiler_params=LIMIT,
        in_specs=[VMEM] * 2,
        out_specs=HBM,
        scratch_shapes=[pltpu.VMEM((1152, NF), F32), pltpu.SemaphoreType.DMA((4,))],
    )(parts, damped)


def exchange(buffer, axes, count):
    flat = buffer.reshape(count, 1, -1)
    return lax.all_to_all(flat, axes, split_axis=0, concat_axis=0, tiled=False)


def swap_planes(potential, near):
    other = lax.ppermute(potential, "cols_1", [(0, 1), (1, 0)])
    planes = [
        lax.dynamic_index_in_dim(held.reshape(2, 2, 72, NC), near, 1, keepdims=False)
        for held in (potential, other)
    ]
    return jnp.stack(planes, axis=1)


def spread_planes(planes, across):
    slots = []
    for i in range(4):
        chunk = lax.dynamic_index_in_dim(planes, (across + i) % 2, 0, keepdims=False)
        if i:
            moves = [(c * 4 + (y - i) % 4, c * 4 + y) for c in range(2) for y in (2 * c, 2 * c + 1)]
            chunk = lax.ppermute(chunk, (CORE, "cols_0"), moves)
        slots.append(chunk)
    return jnp.stack(slots)


def share_planes(slots, core, across):
    moves = [(y // 2 * 4 + y, (1 - y // 2) * 4 + y) for y in range(4)]
    other = lax.ppermute(slots, (CORE, "cols_0"), moves)
    return jnp.where(core == across // 2, slots, other).reshape(8, 72, NC)


def per_device(wave_coarse, potential_coarse, potential_fine):
    core = lax.axis_index(CORE)
    chip = lax.axis_index(CHIPS)
    device = lax.axis_index(ALL)
    across, near = lax.axis_index("cols_0"), lax.axis_index("cols_1")
    place = jnp.stack([core, across, near, chip, device, lax.axis_index(ROWS)])

    got = exchange(coarse_pencil(wave_coarse.reshape(288, NC)), ALL, 128).reshape(896, 128)
    planes = spread_planes(swap_planes(potential_coarse, near), across)
    got, planes = lax.optimization_barrier((got, planes))
    turned, planes = lax.optimization_barrier((coarse_z(place, got), planes))
    got = exchange(turned, CHIPS, 64).reshape(960, 128)
    got, planes = lax.optimization_barrier((got, share_planes(planes, core, across)))
    got = exchange(coarse_y(place, got), CHIPS, 64).reshape(960, 128)
    other = lax.ppermute(got, CORE, [(0, 1), (1, 0)])
    turned = coarse_x(place, got, other, planes)
    got = exchange(turned, CHIPS, 64).reshape(1792, 128)

    evolved, spectrum = fine_in(got)
    got = exchange(spectrum, ALL, 128).reshape(3456, 128)
    spectrum = fine_slab(place, got)
    got = exchange(spectrum, ALL, 128).reshape(3456, 128)
    damped, part = fine_out(place, got, evolved, potential_fine.reshape(1152, NF))
    parts = exchange(part, ALL, 128).reshape(128, 128)
    return scaled(parts, damped).reshape(48, 24, NF)


def solution(mesh):
    torus = Mesh(
        mesh.devices.reshape(4, 2, 2, 4, 2), ("rows_0", "rows_1", "rows_2", "cols_0", "cols_1")
    )
    return jax.shard_map(
        per_device,
        mesh=torus,
        in_specs=(P(ROWS, COLS, None), P(ROWS, COLS, None), P(COLS, ROWS, None)),
        out_specs=P(COLS, ROWS, None),
        check_vma=False,
    )
```

```python
import math

import jax
import jax.numpy as jnp
import numpy as np
from jax import lax
from jax.experimental import pallas as pl
from jax.experimental.pallas import tpu as pltpu
from jax.sharding import Mesh
from jax.sharding import PartitionSpec as P

NC = 192
NF = 384
ROWS = ("rows_0", "rows_1", "rows_2")
COLS = ("cols_0", "cols_1")
ALL = ROWS + COLS
CHIPS = ("rows_0", "rows_1", "cols_0", "cols_1")
CORE = "rows_2"

TIME_STEP = 0.5
CONTACT = 0.4
DIPOLE_STRENGTH = 0.3
EPSILON = 1e-06


def cas_table(rows, columns, length):
    phases = 2.0 * math.pi / length * ((np.outer(rows, columns)) % length)
    return np.cos(phases) + np.sin(phases)


def signed(length):
    k = np.arange(length)
    return np.where(k < length // 2, k, k - length)


def tables():
    k = np.arange(NC)
    wave = 2.0 * math.pi / NF * signed(NC)
    decay = np.exp(-0.5 * TIME_STEP * wave**2)
    hc = cas_table(k, k, NC)
    hf = cas_table(np.arange(NF), np.arange(NF), NF)
    evolve = hc @ (decay[:, None] * hc) / NC
    lifted = np.where(k < NC // 2, k, k + NC)
    lift = hf[:, lifted] @ (decay[:, None] * hc) / NC
    return [t.astype(np.float32) for t in (hc, hf, evolve, lift)]


HC, HF, EVOLVE, LIFT = tables()


def squares(index, length, spacing):
    s = jnp.where(index < length // 2, index, index - length).astype(jnp.float32)
    w = 2.0 * math.pi / (length * spacing) * s
    return w * w


def dipolar(wx, wy, wz, length):
    q = wx + wy + wz
    safe = jnp.where(q > 0, q, 1.0)
    return jnp.where(q > 0, DIPOLE_STRENGTH * (3.0 * wz - q) / safe, 0.0) / float(length) ** 3


F32 = jnp.float32
BF16 = jnp.bfloat16
VMEM = pl.BlockSpec(memory_space=pltpu.VMEM)
SMEM = pl.BlockSpec(memory_space=pltpu.SMEM)
HBM = pl.BlockSpec(memory_space=pltpu.HBM)
LIMIT = pltpu.CompilerParams(vmem_limit_bytes=20 * 1024 * 1024)


def halves(table):
    high = table.astype(BF16)
    return np.stack([high, (table - high.astype(np.float32)).astype(BF16)])


HF2 = halves(HF)
BY_SLAB = np.arange(NF).reshape(8, 48).T.reshape(-1)
HF_OUT2 = halves(HF[:, BY_SLAB])
HF_BACK2 = halves(HF[BY_SLAB, :])
PLANE = np.arange(NC).reshape(16, 12).T.reshape(-1)
LIFT_X2 = halves(LIFT[:, np.arange(NC).reshape(64, 3).T.reshape(-1)])
HC2 = halves(HC)
HC_WIDE2 = halves(np.pad(HC, ((0, 64), (0, 64))))
EVOLVE2 = halves(EVOLVE)
EVOLVE_Y2 = halves(np.pad(EVOLVE, ((0, 0), (0, 64))))
EVOLVE_X2 = halves(np.pad(EVOLVE[PLANE, :], ((0, 0), (0, 64))))
LIFT_Z2 = halves(LIFT[BY_SLAB, :])
LIFT_Y2 = np.stack(
    [
        halves(np.pad(LIFT.reshape(8, 2, 24, NC)[:, core].reshape(NC, NC).T, ((0, 0), (0, 64))))
        for core in range(2)
    ]
)
TURNED = (((1,), (1,)), ((), ()))
PLAIN = (((1,), (0,)), ((), ()))


def split(x):
    high = x.astype(BF16)
    return high, (x - high.astype(F32)).astype(BF16)


def dot3(a, b, dims=PLAIN):
    (ah, al), (bh, bl) = a, b

    def dot(p, q):
        return lax.dot_general(p, q, dims, preferred_element_type=F32)

    return dot(ah, bh) + (dot(al, bh) + dot(ah, bl))


def dot(a, b):
    return jnp.dot(a, b, preferred_element_type=F32)


def left3(x):
    high, low = split(x)
    return jnp.concatenate([high, low, high], axis=1)


def right3(x):
    high, low = split(x)
    return jnp.concatenate([high, high, low], axis=0)


def fetch_left(table, wide, sems):
    size = table.shape[2]
    return [
        pltpu.make_async_copy(table.at[part], wide.at[:, pl.ds(i * size, size)], sems.at[i])
        for i, part in enumerate((0, 1, 0))
    ]


def fetch_right(table, tall, sems):
    size = table.shape[1]
    return [
        pltpu.make_async_copy(table.at[part], tall.at[pl.ds(i * size, size), :], sems.at[i])
        for i, part in enumerate((0, 0, 1))
    ]


def begin(copies):
    for copy in copies:
        copy.start()


def finish(copies):
    for copy in copies:
        copy.wait()


def pair(ref):
    return ref[0], ref[1]


def tiles_of(row):
    return [row[:, 128 * t : 128 * t + 128] for t in range(row.shape[1] // 128)]


def shift_runs(row, lanes):
    lanes %= NF
    return pltpu.roll(row, lanes, 1) if lanes else row


def skew(rows, lead=0):
    return [tiles_of(shift_runs(row, 24 * a - lead)) for a, row in enumerate(rows)]


def diagonals(skewed, count):
    lane = lax.broadcasted_iota(jnp.int32, skewed[0][0].shape, 1)
    result = []
    for b in range(count):
        tiles = []
        for t in range(3):
            tile = None
            for p in range(128 * t // 24, (128 * t + 127) // 24 + 1):
                a = (p - b) % 16
                if a < len(skewed):
                    piece = skewed[a][t]
                    tile = piece if tile is None else jnp.where(lane < 24 * p - 128 * t, tile, piece)
            tiles.append(skewed[0][t] if tile is None else tile)
        result.append(jnp.concatenate(tiles, axis=1))
    return result


def in_hbm(x):
    return pltpu.with_memory_space_constraint(x, pltpu.HBM)


def coarse_pencil_kernel(wave_hbm, matrix_hbm, out_ref, wave_ref, matrix_ref, sems):
    copies = [
        pltpu.make_async_copy(wave_hbm, wave_ref, sems.at[0]),
        pltpu.make_async_copy(matrix_hbm, matrix_ref, sems.at[1]),
    ]
    begin(copies)
    finish(copies)
    high, low = split(wave_ref[...])
    pieces = []
    for k in range(3):
        lead = 32 * k

        def padded(x):
            parts = [jnp.zeros((lead, NC), BF16)] * (k > 0) + [x]
            return jnp.concatenate(parts + [jnp.zeros((96 - lead, NC), BF16)], axis=0)

        rows = slice(64 * k, 64 * k + 64)
        matrix = (matrix_ref[0, rows, :], matrix_ref[1, rows, :])
        pieces.append(tiles_of(dot3(matrix, (padded(high), padded(low)), TURNED)))
    (a0, a1, a2), (b0, b1, b2), (c0, c1, c2) = pieces
    for t, tile in enumerate([a0, a1, a2 + b0, b1, b2 + c0, c1, c2]):
        for p in range(8):
            for core in range(2):
                out_ref[pl.ds(p * 112 + core * 56 + t, 8, stride=7), :] = tile[8 * p : 8 * p + 8, :]


def coarse_pencil(wave):
    return pl.pallas_call(
        coarse_pencil_kernel,
        out_shape=jax.ShapeDtypeStruct((896, 128), F32),
        compiler_params=LIMIT,
        in_specs=[HBM] * 2,
        out_specs=VMEM,
        scratch_shapes=[
            pltpu.VMEM((288, NC), F32),
            pltpu.VMEM((2, NC, NC), BF16),
            pltpu.SemaphoreType.DMA((2,)),
        ],
    )(in_hbm(wave), in_hbm(jnp.asarray(EVOLVE2)))


def pack_rows(planes):
    (a0, a1), (b0, b1), (c0, c1) = [tiles_of(plane) for plane in planes]
    low = lax.broadcasted_iota(jnp.int32, a0.shape, 1) < 64
    b0, b1 = pltpu.roll(b0, 64, 1), pltpu.roll(b1, 64, 1)
    return [a0, jnp.where(low, a1, b0), jnp.where(low, b0, b1), c0, c1]


def unpack_rows(tiles):
    a0, mixed, b1, c0, c1 = tiles
    low = lax.broadcasted_iota(jnp.int32, a0.shape, 1) < 64
    b1 = pltpu.roll(b1, 64, 1)
    b0 = jnp.where(low, pltpu.roll(mixed, 64, 1), b1)
    return [jnp.concatenate(p, axis=1) for p in ((a0, mixed), (b0, b1), (c0, c1))]


def coarse_z_kernel(place_ref, got_ref, ey_ref, ex_ref, matrix_ref, out_ref, plane_ref):
    core = place_ref[0]
    for k in range(3):
        for g in range(2):
            rows = []
            for c in range(8):
                tiles = [got_ref[pl.ds(g * 448 + c * 7 + 2 * k + t, 8, stride=56), :] for t in range(3)]
                rows.append(jnp.concatenate(tiles, axis=1))
            for i, row in enumerate(diagonals(skew(rows, 32 * k), 12)):
                row = shift_runs(row, -24 * i)
                plane_ref[16 * i + 8 * g : 16 * i + 8 * g + 8, :] = row[:, :256]
        half = dot3(pair(ey_ref), split(plane_ref[...]), TURNED)
        evolved = dot3(split(half), pair(ex_ref))
        turned = dot3(pair(matrix_ref), split(evolved * evolved))
        mine = jnp.where(core == 0, turned, evolved)
        for i, tile in enumerate(pack_rows([mine[64 * j : 64 * j + 64, :] for j in range(3)])):
            out_ref[pl.ds(k * 5 + i, 64, stride=15), :] = tile


def coarse_z(place, got):
    return pl.pallas_call(
        coarse_z_kernel,
        out_shape=jax.ShapeDtypeStruct((960, 128), F32),
        compiler_params=LIMIT,
        in_specs=[SMEM] + [VMEM] * 4,
        out_specs=VMEM,
        scratch_shapes=[pltpu.VMEM((NC, 256), F32)],
    )(place, got, jnp.asarray(EVOLVE_Y2), jnp.asarray(EVOLVE_X2), jnp.asarray(HC2))


def coarse_y_kernel(place_ref, got_ref, matrix_ref, wide_ref, out_ref):
    core = place_ref[0]
    wx = squares(lax.broadcasted_iota(jnp.int32, (NC, 256), 0), NC, 2.0)
    wz = squares(lax.broadcasted_iota(jnp.int32, (NC, 256), 1), NC, 2.0)
    parts = []
    for j in range(3):
        parts.append(unpack_rows([got_ref[pl.ds(5 * j + i, 64, stride=15), :] for i in range(5)]))
    planes = []
    for k in range(3):
        both = jnp.concatenate([part[k] for part in parts] + [jnp.zeros((64, 256), F32)], axis=0)
        both = both.T[:NC, :]
        mid = dot3(pair(matrix_ref), split(both))
        mid = dot3(split(mid), pair(wide_ref))
        wy = squares(jnp.full((1, 1), 64 * k + place_ref[3], jnp.int32), NC, 2.0)
        mid = mid * dipolar(wx, wy, wz, NC)
        mid = dot3(split(mid), pair(wide_ref))
        mid = dot3(pair(matrix_ref), split(mid))
        planes.append(jnp.where(core == 0, mid, both))
    for i, tile in enumerate(pack_rows(planes)):
        out_ref[pl.ds(i, NC, stride=5), :] = tile


def coarse_y(place, got):
    return pl.pallas_call(
        coarse_y_kernel,
        out_shape=jax.ShapeDtypeStruct((960, 128), F32),
        compiler_params=LIMIT,
        in_specs=[SMEM] + [VMEM] * 3,
        out_specs=VMEM,
    )(place, got, jnp.asarray(HC2), jnp.asarray(HC_WIDE2))


def coarse_x_kernel(place_ref, got_ref, other_ref, potential_ref, matrix_ref, lz_ref, ly_ref, out_ref, lifted_ref):
    core = place_ref[0]
    slots = []
    for c in range(8):
        slots.append(2 * lax.rem(place_ref[1] - c // 2 + 4, 4) + (place_ref[2] ^ (c % 2)))
    lift_y = (ly_ref[core, 0], ly_ref[core, 1])
    part = jnp.zeros((1, 1), F32)
    blank = jnp.zeros((8, 128), F32)
    for k in range(3):
        fields, waves = [], []
        for i in range(5):
            rows = pl.ds(5 * k + i, 64, stride=15)
            mine, other = got_ref[rows, :], other_ref[rows, :]
            fields.append(jnp.where(core == 0, mine, other))
            waves.append(jnp.where(core == 0, other, mine))
        field = dot3(pair(matrix_ref), split(jnp.concatenate(unpack_rows(fields), axis=0)))
        wave = jnp.concatenate(unpack_rows(waves), axis=0)
        evolved = [wave[:, :128], wave[:, 128:NC]]
        pieces = []
        for t, e in enumerate(evolved):
            lanes = slice(128 * t, 128 * t + e.shape[1])
            v = jnp.concatenate([potential_ref[c, 24 * k : 24 * k + 24, lanes] for c in slots], axis=0)
            d = jnp.exp(-TIME_STEP * (v + CONTACT * e * e + field[:, lanes])) * e
            part = part + jnp.sum(d * d, keepdims=True)
            pieces.append(d)
        damped = split(jnp.concatenate(pieces, axis=1))
        lifted = dot3(pair(lz_ref), damped, TURNED)
        lifted_ref[...] = dot3(split(lifted), lift_y)
        for g in range(3):
            rows = []
            for i in range(16):
                row = lifted_ref[128 * g + 8 * i : 128 * g + 8 * i + 8, :]
                rows.append(jnp.concatenate([row, blank], axis=1))
            for p, row in enumerate(diagonals(skew(rows), 8)):
                row = jnp.where(core == 0, shift_runs(row, 24 * p), shift_runs(row, 24 * p + 24))
                for t, tile in enumerate(tiles_of(row)):
                    out_ref[pl.ds(p * 224 + k * 9 + g * 3 + t, 8, stride=28), :] = tile
    out_ref[pl.ds(27, 64, stride=28), :] = jnp.broadcast_to(part, (64, 128))


def coarse_x(place, got, other, potential):
    return pl.pallas_call(
        coarse_x_kernel,
        out_shape=jax.ShapeDtypeStruct((1792, 128), F32),
        compiler_params=LIMIT,
        in_specs=[SMEM] + [VMEM] * 6,
        out_specs=VMEM,
        scratch_shapes=[pltpu.VMEM((NF, 256), F32)],
    )(place, got, other, potential, jnp.asarray(HC2), jnp.asarray(LIFT_Z2), jnp.asarray(LIFT_Y2))


def fine_in_kernel(
    got_ref, lift_ref, matrix_hbm, evolved_hbm, out_ref, evolved_ref, matrix_ref, sems, saved
):
    copies = fetch_left(matrix_hbm, matrix_ref, sems)
    begin(copies)
    parts = got_ref[pl.ds(27, 64, stride=28), :]
    total = jnp.sum(parts, axis=0, keepdims=True)
    scale = lax.rsqrt(total / float(NC) ** 3 + EPSILON)
    scale = jnp.concatenate([scale] * 3, axis=1)
    finish(copies)

    def save(n):
        columns = pl.ds(pl.multiple_of(n * 384, 128), 384)
        source, target = evolved_ref.at[:, columns], evolved_hbm.at[:, columns]
        return pltpu.make_async_copy(source, target, saved.at[n])

    def body(n, carry):
        rows = []
        for k in range(3):
            tiles = [got_ref[pl.ds(k * 9 + 3 * n + t, 64, stride=28), :] for t in range(3)]
            rows.append(jnp.concatenate(tiles, axis=1))
        spectrum = split(jnp.concatenate(rows, axis=0))
        evolved = dot3(pair(lift_ref), spectrum) * scale
        evolved_ref[:, pl.ds(pl.multiple_of(n * 384, 128), 384)] = evolved
        turned = dot(matrix_ref[...], right3(evolved * evolved))
        for k in range(3):
            for t in range(3):
                piece = turned[128 * k : 128 * k + 128, 128 * t : 128 * t + 128]
                out_ref[pl.ds(k * 9 + 3 * n + t, 128, stride=27), :] = piece
        save(n).start()
        return carry

    lax.fori_loop(0, 3, body, 0)
    for n in range(3):
        save(n).wait()


def fine_in(got):
    return pl.pallas_call(
        fine_in_kernel,
        out_shape=[
            pltpu.HBM((NF, 1152), F32),
            jax.ShapeDtypeStruct((3456, 128), F32),
        ],
        compiler_params=LIMIT,
        in_specs=[VMEM, VMEM, HBM],
        out_specs=[HBM, VMEM],
        scratch_shapes=[
            pltpu.VMEM((NF, 1152), F32),
            pltpu.VMEM((NF, 1152), BF16),
            pltpu.SemaphoreType.DMA((3,)),
            pltpu.SemaphoreType.DMA((3,)),
        ],
    )(got, jnp.asarray(LIFT_X2), jnp.asarray(HF2))


def fine_slab_kernel(
    place_ref, got_ref, out_hbm, back_hbm, matrix_hbm, out_ref, plane_ref, back_ref, out_m, back_m, matrix, sems
):
    out_copies = fetch_left(out_hbm, out_m, sems.at[0])
    back_copies = fetch_left(back_hbm, back_m, sems.at[1])
    copies = fetch_right(matrix_hbm, matrix, sems.at[2])
    begin(out_copies + copies + back_copies)
    wz = squares(lax.broadcasted_iota(jnp.int32, (NF, NF), 0), NF, 1.0)
    wy = squares(lax.broadcasted_iota(jnp.int32, (NF, NF), 1), NF, 1.0)


    def unpack(k):
        for g in range(3):
            base = k * 9 + g * 3
            skewed = [
                [got_ref[pl.ds(r * 216 + base + t, 8, stride=27), :] for t in range(3)]
                for r in range(16)
            ]
            for i, row in enumerate(diagonals(skewed, 16)):
                start = 128 * g + 8 * i
                plane_ref[start : start + 8, :] = shift_runs(row, -24 * i)

    def pack(k):
        for g in range(3):
            base = k * 9 + g * 3
            rows = [back_ref[128 * g + 8 * i : 128 * g + 8 * i + 8, :] for i in range(16)]
            for r, row in enumerate(diagonals(skew(rows), 16)):
                for t, tile in enumerate(tiles_of(row)):
                    out_ref[pl.ds(r * 216 + base + t, 8, stride=27), :] = tile

    def body(k, carry):
        mid = dot(out_m[...], right3(plane_ref[...]))
        pack(jnp.maximum(k - 1, 0))
        unpack(jnp.minimum(k + 1, 2))
        mid = dot(left3(mid), matrix[...])
        kx = 128 * k + place_ref[4]
        wx = squares(jnp.full((1, 1), kx, jnp.int32), NF, 1.0)
        mid = mid * dipolar(wx, wy, wz, NF)
        mid = dot(left3(mid), matrix[...])
        back_ref[...] = dot(back_m[...], right3(mid))
        return carry

    back_ref[...] = jnp.zeros_like(back_ref)
    unpack(0)
    finish(out_copies + copies + back_copies)
    lax.fori_loop(0, 3, body, 0)
    pack(2)


def fine_slab(place, got):
    return pl.pallas_call(
        fine_slab_kernel,
        out_shape=jax.ShapeDtypeStruct((3456, 128), F32),
        compiler_params=LIMIT,
        in_specs=[SMEM, VMEM] + [HBM] * 3,
        out_specs=VMEM,
        scratch_shapes=[
            pltpu.VMEM((NF, NF), F32),
            pltpu.VMEM((NF, NF), F32),
            pltpu.VMEM((NF, 1152), BF16),
            pltpu.VMEM((NF, 1152), BF16),
            pltpu.VMEM((1152, NF), BF16),
            pltpu.SemaphoreType.DMA((3, 3)),
        ],
    )(place, got, jnp.asarray(HF_OUT2), jnp.asarray(HF_BACK2), jnp.asarray(HF2))


def fine_out_kernel(place_ref, got_ref, evolved_ref, potential_ref, matrix_ref, damped_ref, part_ref):
    part_ref[...] = jnp.zeros_like(part_ref)
    row = place_ref[5]

    def block(n, p):
        return pl.ds(pl.multiple_of(384 * n + 24 * lax.rem(p + 16 - row, 16), 8), 24)

    def body(n, carry):
        rows = []
        for k in range(3):
            tiles = [got_ref[pl.ds(k * 9 + 3 * n + t, 128, stride=27), :] for t in range(3)]
            rows.append(jnp.concatenate(tiles, axis=1))
        field = dot3(pair(matrix_ref), split(jnp.concatenate(rows, axis=0)))
        columns = pl.ds(n * 384, 384)
        evolved = evolved_ref[:, columns]
        potential = jnp.concatenate([potential_ref[block(n, p), :] for p in range(16)], axis=0).T
        exponent = -TIME_STEP * (potential + CONTACT * evolved * evolved + field)
        damped = jnp.exp(exponent) * evolved
        part_ref[...] += jnp.sum(damped * damped)
        turned = damped.T
        for p in range(16):
            damped_ref[block(n, p), :] = turned[24 * p : 24 * p + 24, :]
        return carry

    for n in range(3):
        body(n, 0)


def fine_out(place, got, evolved, potential):
    return pl.pallas_call(
        fine_out_kernel,
        out_shape=[
            jax.ShapeDtypeStruct((1152, NF), F32),
            jax.ShapeDtypeStruct((128, 128), F32),
        ],
        compiler_params=LIMIT,
        in_specs=[SMEM] + [VMEM] * 4,
        out_specs=[VMEM] * 2,
    )(place, got, evolved, potential, jnp.asarray(HF2))


def scale_kernel(parts_ref, damped_ref, out_hbm, scaled_ref, sems):
    total = jnp.sum(parts_ref[...], axis=0, keepdims=True)
    scale = lax.rsqrt(total / float(NF) ** 3 + EPSILON)
    scale = jnp.concatenate([scale] * 3, axis=1)
    copies = []
    for i in range(4):
        rows = pl.ds(288 * i, 288)
        copies.append(pltpu.make_async_copy(scaled_ref.at[rows], out_hbm.at[rows], sems.at[i]))
        scaled_ref[rows, :] = damped_ref[rows, :] * scale
        if i:
            copies[i - 1].start()
    copies[3].start()
    finish(copies)


def scaled(parts, damped):
    return pl.pallas_call(
        scale_kernel,
        out_shape=jax.ShapeDtypeStruct((1152, NF), F32),
        compiler_params=LIMIT,
        in_specs=[VMEM] * 2,
        out_specs=HBM,
        scratch_shapes=[pltpu.VMEM((1152, NF), F32), pltpu.SemaphoreType.DMA((4,))],
    )(parts, damped)


def exchange(buffer, axes, count):
    flat = buffer.reshape(count, 1, -1)
    return lax.all_to_all(flat, axes, split_axis=0, concat_axis=0, tiled=False)


def swap_planes(potential, near):
    other = lax.ppermute(potential, "cols_1", [(0, 1), (1, 0)])
    planes = [
        lax.dynamic_index_in_dim(held.reshape(2, 2, 72, NC), near, 1, keepdims=False)
        for held in (potential, other)
    ]
    return jnp.stack(planes, axis=1)


def spread_planes(planes, across):
    slots = []
    for i in range(4):
        chunk = lax.dynamic_index_in_dim(planes, (across + i) % 2, 0, keepdims=False)
        if i:
            moves = [(c * 4 + (y - i) % 4, c * 4 + y) for c in range(2) for y in (2 * c, 2 * c + 1)]
            chunk = lax.ppermute(chunk, (CORE, "cols_0"), moves)
        slots.append(chunk)
    return jnp.stack(slots)


def share_planes(slots, core, across):
    moves = [(y // 2 * 4 + y, (1 - y // 2) * 4 + y) for y in range(4)]
    other = lax.ppermute(slots, (CORE, "cols_0"), moves)
    return jnp.where(core == across // 2, slots, other).reshape(8, 72, NC)


def per_device(wave_coarse, potential_coarse, potential_fine):
    core = lax.axis_index(CORE)
    chip = lax.axis_index(CHIPS)
    device = lax.axis_index(ALL)
    across, near = lax.axis_index("cols_0"), lax.axis_index("cols_1")
    place = jnp.stack([core, across, near, chip, device, lax.axis_index(ROWS)])

    got = exchange(coarse_pencil(wave_coarse.reshape(288, NC)), ALL, 128).reshape(896, 128)
    got, planes = lax.optimization_barrier((got, swap_planes(potential_coarse, near)))
    got = exchange(coarse_z(place, got), CHIPS, 64).reshape(960, 128)
    planes = spread_planes(planes, across)
    got = exchange(coarse_y(place, got), CHIPS, 64).reshape(960, 128)
    other = lax.ppermute(got, CORE, [(0, 1), (1, 0)])
    turned = coarse_x(place, got, other, share_planes(planes, core, across))
    got = exchange(turned, CHIPS, 64).reshape(1792, 128)

    evolved, spectrum = fine_in(got)
    got = exchange(spectrum, ALL, 128).reshape(3456, 128)
    spectrum = fine_slab(place, got)
    got = exchange(spectrum, ALL, 128).reshape(3456, 128)
    damped, part = fine_out(place, got, evolved, potential_fine.reshape(1152, NF))
    parts = exchange(part, ALL, 128).reshape(128, 128)
    return scaled(parts, damped).reshape(48, 24, NF)


def solution(mesh):
    torus = Mesh(
        mesh.devices.reshape(4, 2, 2, 4, 2), ("rows_0", "rows_1", "rows_2", "cols_0", "cols_1")
    )
    return jax.shard_map(
        per_device,
        mesh=torus,
        in_specs=(P(ROWS, COLS, None), P(ROWS, COLS, None), P(COLS, ROWS, None)),
        out_specs=P(COLS, ROWS, None),
        check_vma=False,
    )
```
